256 devices in a mesh: grp: 8 (over x, y_hi), blk: 32 (over z, y_lo, core).
Axes of the slice: x: 4, y: 4 (y_hi: 2, y_lo: 2; y = y_hi * 2 + y_lo), z: 8, core: 2. Of those that a mesh axis runs over, the one named last changes fastest.
Arguments:
- counts: int32 [65536, 1024], P(('grp', 'blk')), may hold values from 0 to 5
- tile_live: int32 [512, 8], P(('grp', 'blk')), may hold values from 0 to 1
- doc_lengths: int32 [65536], P(('grp', 'blk')), may hold values from 256 to 4095
- doc_mix: bfloat16 [65536, 4096], P(('grp', 'blk')), may hold values from 0.019897461 to 50
- word_topic: float32 [4096, 4096], P('blk'), may hold values from 0.01 to 8
- topic_total: float32 [4096], replicated, may hold values from 20000 to 400000
Outputs:
- doc_share: bfloat16 [65536, 4096], P(('grp', 'blk'))
- word_topic_new: float32 [4096, 4096], P('blk')
- topic_mean: float32 [4096], replicated
The draws below stay inside these ranges and needn't reach their ends.
All inputs are finite; a program needn't handle non-finite values.
Results may differ from the reference program's by a relative error of at most 0.0004.
The reference program's roundings to bfloat16 on the way (of `word_low`, `doc_low` and `ratio`) count: a program that leaves them out, or rounds other values in their place, can miss the bound.
Values may be sent and summed in bfloat16 or wider, within the bound.
A program may use at most 128 MiB of HBM per device.

```python
import math
import jax
import jax.numpy as jnp
from jax import lax

K = 4096
VOCAB = 262144
WB = 128
DOC_DEV = 256
SPAN = 8
W = 4096
DOCS = 65536
N_BLK = 32


def draw_counts(key, part):
    row_count = DOCS
    col_count = SPAN * WB
    key_pick = jax.random.fold_in(key, 11)
    key_value = jax.random.fold_in(key, 23)
    shard_count = DOCS // DOC_DEV
    shard_place = jnp.arange(row_count, dtype=jnp.int32) // DOC_DEV
    threshold = 2 + 4 * shard_place // max(shard_count - 1, 1)
    pick = jax.random.randint(key_pick, (row_count, col_count), 0, 64)
    value = jax.random.randint(key_value, (row_count, col_count), 1, 6)
    return jnp.where(pick < threshold[:, None], value, 0).astype(jnp.int32)


def draw_tile_live(key, part):
    row_count = DOCS // WB
    key_level = jax.random.fold_in(key, 31)
    key_pick = jax.random.fold_in(key, 37)
    level = jax.random.randint(key_level, (row_count, 1), 1, 5)
    pick = jax.random.randint(key_pick, (row_count, SPAN), 0, 4)
    return (pick < level).astype(jnp.int32)


def set_ends(result, own_key, low, high):
    shape = result.shape
    spot = [jax.random.randint(jax.random.fold_in(own_key, axis), (), 0, shape[axis]) for axis in range(len(shape))]
    result = result.at[tuple(spot)].set(low)
    longest = shape.index(max(shape))
    spot[longest] = (spot[longest] + 1) % shape[longest]
    return result.at[tuple(spot)].set(high)


def levels(rng, shape, cuts, smallest, high):
    factor_of = 1.0
    for axis_at, parts in cuts:
        draws = jax.random.uniform(jax.random.fold_in(jax.random.fold_in(rng, 6), axis_at), (parts,), jnp.float32, smallest / len(cuts), high / len(cuts))
        factor_of = factor_of * jnp.repeat(jnp.exp(draws), shape[axis_at] // parts).reshape((-1,) + (1,) * (len(shape) - 1 - axis_at))
    return factor_of


def setup_inputs(seed: int = 0) -> dict:
    streams_of = jax.random.split(jax.random.key(seed), 7)
    return {
        "counts": draw_counts(jax.random.fold_in(streams_of[6], 71), 0),
        "tile_live": draw_tile_live(jax.random.fold_in(streams_of[6], 71), 0),
        "doc_lengths": set_ends(jax.random.randint(streams_of[2], (DOCS,), 256, 4096), jax.random.fold_in(streams_of[2], 1), 256, 4095).astype(jnp.int32),
        "doc_mix": jnp.clip(jnp.exp(math.log(50.0) - 7.829186 * jax.random.uniform(streams_of[3], (DOCS, K), jnp.float32) ** levels(streams_of[3], (DOCS, K), ((0, 256),), -0.2, 0.2)), 0.019897461, 50.0).astype(jnp.bfloat16),
        "word_topic": jnp.clip(jnp.exp(math.log(8.0) - 6.684612 * jax.random.uniform(streams_of[4], (W, K), jnp.float32) ** levels(streams_of[4], (W, K), ((0, 32),), -0.2, 0.2)), 0.01, 8.0),
        "topic_total": jnp.clip(jnp.exp(jax.random.uniform(streams_of[5], (K,), jnp.float32, math.log(20000.0), math.log(400000.0))), 20000.0, 400000.0),
    }


alpha_prior = 0.1
beta_prior = 0.01


def reference(counts, tile_live, doc_lengths, doc_mix, word_topic, topic_total):
    word_weight = (word_topic + beta_prior) / (topic_total + beta_prior * VOCAB)[None, :]
    word_low = word_weight.astype(jnp.bfloat16)
    shards = DOCS // DOC_DEV
    tiles_shard = DOC_DEV // WB
    counts_shard = counts.reshape(shards, DOC_DEV, SPAN * WB)
    live_shard = tile_live.reshape(shards, tiles_shard, SPAN)
    lengths_shard = doc_lengths.reshape(shards, DOC_DEV)
    mix_shard = doc_mix.reshape(shards, DOC_DEV, K)
    positions = jnp.arange(shards, dtype=jnp.int32)

    def one_shard(state_pair, inputs):
        word_sum, topic_sum = state_pair
        shard_counts, shard_live, shard_lengths, shard_mix, position = inputs
        mix_wide = shard_mix.astype(jnp.float32)
        doc_theta = mix_wide / jnp.sum(mix_wide, axis=1, keepdims=True)
        doc_weight = shard_lengths.astype(jnp.float32)[:, None] * doc_theta + alpha_prior
        doc_low = doc_weight.astype(jnp.bfloat16)
        live_full = jnp.repeat(jnp.repeat(shard_live, WB, axis=0), WB, axis=1)
        live_counts = shard_counts.astype(jnp.float32) * live_full.astype(jnp.float32)
        window_len = jnp.sum(live_counts, axis=1)
        doc_proj = jnp.zeros((DOC_DEV, K), jnp.float32)
        loop_place = position % N_BLK
        for offset in range(SPAN):
            block_index = ((loop_place + offset) % N_BLK).astype(jnp.int32)
            row_start = (block_index * WB).astype(jnp.int32)
            visitor = lax.dynamic_slice_in_dim(word_low, row_start, WB, 0)
            block_counts = live_counts[:, offset * WB:(offset + 1) * WB]
            normalizer = jnp.dot(doc_low, visitor.T, preferred_element_type=jnp.float32)
            ratio = (block_counts / normalizer).astype(jnp.bfloat16)
            doc_proj = doc_proj + jnp.dot(ratio, visitor, preferred_element_type=jnp.float32)
            word_inc = jnp.dot(ratio.T, doc_low, preferred_element_type=jnp.float32)
            current = lax.dynamic_slice_in_dim(word_sum, row_start, WB, 0)
            word_sum = lax.dynamic_update_slice_in_dim(word_sum, current + word_inc, row_start, 0)
        doc_new = doc_weight * doc_proj
        topic_sum = topic_sum + jnp.sum(doc_new, axis=0)
        doc_share = (K * (doc_new + alpha_prior) / (window_len[:, None] + K * alpha_prior)).astype(jnp.bfloat16)
        return (word_sum, topic_sum), doc_share

    initial = (jnp.zeros((W, K), jnp.float32), jnp.zeros((K,), jnp.float32))
    final_pair, shares = lax.scan(one_shard, initial, (counts_shard, live_shard, lengths_shard, mix_shard, positions))
    word_sum, topic_sum = final_pair
    return shares.reshape(DOCS, K), word_weight * word_sum, topic_sum / W
```

```python
import jax
import jax.numpy as jnp
from jax import lax
from jax.experimental import pallas as pl
from jax.experimental.pallas import tpu as pltpu
from jax.sharding import PartitionSpec as P

VOCAB = 262144

alpha_prior = 0.1
beta_prior = 0.01

MESH = pl.DeviceIdType.MESH
F32 = jnp.float32
BF16 = jnp.bfloat16

DOCS = 256
WB = 128
K = 4096
SPAN = 8
SLOTS = 11
CH = 4
ROWS = WB // CH
KD = K // 8
KH = KD // 2


def place(x, h, z, a, c):
    return {"grp": x * 2 + h, "blk": (z * 2 + a) * 2 + c}


def kernel(
    counts,
    live,
    lengths,
    mix,
    topic,
    total,
    share,
    summed,
    mean,
    words,
    doc_low,
    scale,
    docs,
    ratio,
    ratio_t,
    part,
    near,
    far,
    acc,
    hop1,
    hop2,
    gathered,
    wlen,
    column,
    col_z,
    col_x,
    col_p,
    send_w,
    recv_w,
    send_d,
    recv_d,
    send_r,
    send_rf,
    recv_r,
    send_n,
    recv_n,
    send_f,
    recv_f,
    send_z,
    recv_z,
    send_g,
    recv_g,
    send_t,
    recv_tz,
    recv_tx,
    recv_tp,
):
    grp = lax.axis_index("grp")
    blk = lax.axis_index("blk")
    x = lax.div(grp, 2)
    h = lax.rem(grp, 2)
    z = lax.div(blk, 4)
    i = lax.rem(blk, 4)
    a = lax.div(i, 2)
    c = lax.rem(i, 2)
    i2 = 2 * (1 - a) + c

    def xo(dx):
        return lax.rem(x + dx, 4)

    def zo(dz):
        return lax.rem(z + dz + 8, 8)

    def ho(dh):
        return lax.rem(h + dh, 2)

    def ao(da):
        return lax.rem(a + da, 2)

    def co(dc):
        return lax.rem(c + dc, 2)

    def remote(src, dst, send, recv, x_=x, h_=h, z_=z, a_=a, c_=c):
        return pltpu.make_async_remote_copy(
            src_ref=src,
            dst_ref=dst,
            send_sem=send,
            recv_sem=recv,
            device_id=place(x_, h_, z_, a_, c_),
            device_id_type=MESH,
        )

    barrier = pltpu.get_barrier_semaphore()
    greeted = 0

    def greet(**where):
        at = dict(x=x, h=h, z=z, a=a, c=c)
        at.update(where)
        pl.semaphore_signal(barrier, inc=1, device_id=place(**at), device_id_type=MESH)

    for dz in range(1, 8):
        greet(z=zo(dz))
        greeted += 1
    for dh in range(2):
        for da in range(2):
            for dc in range(2):
                if dh + da + dc:
                    greet(h=ho(dh), a=ao(da), c=co(dc))
                    greeted += 1
    for dx in range(1, 4):
        for dh in range(2):
            for dc in range(2):
                greet(x=xo(dx), h=ho(dh), c=co(dc))
                greeted += 1

    def chunk(slot, r):
        return words.at[pl.ds(pl.multiple_of(slot * WB + r * ROWS, ROWS), ROWS), :]

    def to_z(j, r):
        slot = 4 * j + i
        return remote(chunk(slot, r), chunk(slot + 4, r), send_w.at[j, r, 0], recv_w.at[slot + 4, r], z_=zo(-1))

    def to_partner(j, r):
        slot = 4 * j + i
        return remote(chunk(slot, r), chunk(slot, r), send_w.at[j, r, 1], recv_w.at[slot, r], c_=1 - c)

    def to_y(j, r):
        slot = 4 * j + i
        side = jnp.where(r < CH // 2, h, 1 - h)
        return remote(
            chunk(slot, r), chunk(slot, r), send_w.at[j, r, 2], recv_w.at[slot, r], h_=side, a_=1 - a
        )

    def relay(j, r):
        slot = 4 * j + i2
        return remote(chunk(slot, r), chunk(slot, r), send_w.at[j, r, 3], recv_w.at[slot, r], c_=1 - c)

    def arrived(slot, r):
        return pltpu.make_async_copy(chunk(slot, r), chunk(slot, r), recv_w.at[slot, r])

    def column_copies(j, r, act):
        if j == 0:
            act(to_z(j, r))
        elif j == 1:
            @pl.when(i <= 2)
            def _():
                act(to_z(j, r))
        if j == 1:
            act(to_partner(j, r))
            act(to_y(j, r))
        else:
            @pl.when(c == (1 if j == 0 else 0))
            def _():
                act(to_partner(j, r))

            @pl.when(a == (1 if j == 0 else 0))
            def _():
                act(to_y(j, r))

    start = lambda copy: copy.start()
    drain = lambda copy: copy.wait_send()

    inverse = 1.0 / (total[...] + beta_prior * VOCAB)

    @pl.loop(0, CH)
    def _(r):
        rows = pl.ds(pl.multiple_of(r * ROWS, ROWS), ROWS)
        own = pl.ds(pl.multiple_of(i * WB + r * ROWS, ROWS), ROWS)
        words[own, :] = ((topic[rows, :] + beta_prior) * inverse).astype(BF16)

        @pl.when(r == 0)
        def _():
            pl.semaphore_wait(barrier, greeted)

        @pl.when(r > 0)
        def _():
            column_copies(0, r - 1, start)

    own_docs = lax.rem(blk, 2) + 2 * x

    @pl.loop(0, DOCS // 32)
    def _(n):
        rows = pl.ds(pl.multiple_of(n * 32, 32), 32)
        wide = mix[rows, :].astype(F32)
        factor = lengths[rows, :].astype(F32) / jnp.sum(wide, axis=1, keepdims=True)
        scale[rows, :] = factor
        doc_low[rows, :] = (wide * factor + alpha_prior).astype(BF16)

        @pl.when(n == 0)
        def _():
            column_copies(0, CH - 1, start)

    def doc_rows(q):
        return pl.ds(pl.multiple_of(q * DOCS, DOCS), DOCS)

    def topics(q):
        return pl.ds(pl.multiple_of(q * KD, KD), KD)

    def doc_copy(dx, dc):
        to = 2 * xo(dx) + co(dc)
        return remote(
            doc_low.at[:, topics(to)],
            docs.at[doc_rows(own_docs), :],
            send_d.at[dx, dc],
            recv_d.at[own_docs],
            x_=xo(dx),
            c_=co(dc),
        )

    others = [(dx, dc) for dx in range(4) for dc in range(2) if dx + dc]
    docs[doc_rows(own_docs), :] = doc_low[:, topics(own_docs)]
    for dx, dc in others:
        doc_copy(dx, dc).start()

    wlen[...] = jnp.zeros_like(wlen)
    for q in range(4):
        ratio_t[SPAN, :, 2 * q * DOCS : (2 * q + 1) * DOCS] = jnp.zeros((WB, DOCS), BF16)
        ratio_t[0, :, (2 * q + 1) * DOCS : (2 * q + 2) * DOCS] = jnp.zeros((WB, DOCS), BF16)

    def ratio_at(q, k):
        return ratio_t.at[k + lax.rem(q, 2), :, doc_rows(q)]

    def ratio_out(k, dx):
        return remote(
            ratio_at(own_docs, k), ratio_at(own_docs, k), send_r.at[k, dx], recv_r.at[own_docs, k], x_=xo(dx)
        )

    def ratio_over(k):
        return remote(
            ratio_at(own_docs, k), ratio_at(own_docs, k), send_r.at[k, 0], recv_r.at[own_docs, k], c_=1 - c
        )

    def ratio_relay(k, dx):
        q = 2 * xo(dx) + c
        return remote(ratio_at(q, k), ratio_at(q, k), send_rf.at[k, dx - 1], recv_r.at[q, k], c_=1 - c)

    def ratio_arrived(q, k):
        return pltpu.make_async_copy(ratio_at(q, k), ratio_at(q, k), recv_r.at[q, k])

    def meet(slot):
        k = slot - i
        block = words[pl.ds(pl.multiple_of(slot * WB, WB), WB), :]
        normalizer = lax.dot_general(
            doc_low[...], block, (((1,), (1,)), ((), ())), preferred_element_type=F32
        )
        at = pl.ds(pl.multiple_of(k * WB, WB), WB)
        half = DOCS // 2
        top = live[0, k].astype(F32)
        low = live[1, k].astype(F32)
        mask = jnp.where(lax.broadcasted_iota(jnp.int32, (DOCS, WB), 0) < half, top, low)
        kept = counts[:, at].astype(F32) * mask
        wide = kept / normalizer
        ratio_t[k + c, :, doc_rows(own_docs)] = wide.T.astype(BF16)
        ratio[:, at] = wide.astype(BF16)
        wlen[...] += kept
        for dx in range(1, 4):
            ratio_out(k, dx).start()
        ratio_over(k).start()

    def relay_ratio(k):
        for dx in range(1, 4):
            ratio_arrived(2 * xo(dx) + c, k).wait()
            ratio_relay(k, dx).start()

    meet(i)

    @pl.loop(1, SLOTS + 3)
    def _(t):
        @pl.when(t <= 4)
        def _():
            r = t - 1
            arrived(4 + i, r).wait()
            column_copies(1, r, start)

        @pl.when(jnp.logical_and(t == 2, a == 0))
        def _():
            for r in range(CH):
                arrived(i2, r).wait()
                relay(0, r).start()

        @pl.when(jnp.logical_and(t >= 2, t <= 5))
        def _():
            r = t - 2
            arrived(4 + i2, r).wait()
            relay(1, r).start()

        @pl.when(jnp.logical_and(jnp.logical_and(t >= 5, t <= 8), i <= 2))
        def _():
            r = t - 5
            arrived(8 + i, r).wait()
            column_copies(2, r, start)

        @pl.when(jnp.logical_and(jnp.logical_and(t >= 6, t <= 9), a == 1))
        def _():
            r = t - 6
            arrived(8 + i2, r).wait()
            relay(2, r).start()

        back = t - 3 - i

        @pl.when(jnp.logical_and(back >= 0, back < SPAN))
        def _():
            relay_ratio(back)

        slot = t - 1
        column_of = lax.rem(slot, 4)

        @pl.when(jnp.logical_and(slot > i, slot < i + SPAN))
        def _():
            @pl.when(jnp.logical_and(column_of != i, column_of != i2))
            def _():
                for r in range(CH):
                    arrived(slot, r).wait()

            meet(slot)

    for dx, dc in others:
        q = 2 * xo(dx) + co(dc)
        pltpu.make_async_copy(docs.at[doc_rows(q), :], docs.at[doc_rows(q), :], recv_d.at[q]).wait()

    @pl.loop(0, SPAN)
    def _(k):
        for dx in range(4):
            ratio_arrived(2 * xo(dx) + (1 - c), k).wait()

    def products(n):
        made = jnp.dot(ratio_t[n], docs[...], preferred_element_type=F32)
        part[n, 0] = made[:, :KH]
        part[n, 1] = made[:, KH:]

    def near_copy(m, side):
        n = m + 2 + 2 * lax.div(m, 2)
        return remote(
            part.at[n, side], near.at[h, m], send_n.at[m, side], recv_n.at[h, m], h_=side, a_=1 - a
        )

    def far_copy(m):
        n = m + 2 * lax.div(m, 2)
        return remote(part.at[n, 1 - h], far.at[m], send_f.at[m], recv_f.at[m], h_=1 - h)

    @pl.loop(0, 4)
    def _(m):
        products(m + 2 + 2 * lax.div(m, 2))
        for side in range(2):
            near_copy(m, side).start()

    @pl.loop(0, 5)
    def _(m):
        products(m + 2 * lax.div(m, 2))
        far_copy(m).start()

    length = jnp.sum(wlen[...], axis=1, keepdims=True)
    under = 1.0 / (length + K * alpha_prior)

    @pl.loop(0, K // 512)
    def _(n):
        at = pl.ds(pl.multiple_of(n * 512, 512), 512)
        proj = jnp.dot(
            ratio[...],
            words[pl.ds(pl.multiple_of(i * WB, WB), SPAN * WB), at],
            preferred_element_type=F32,
        )
        weight = mix[:, at].astype(F32) * scale[...] + alpha_prior
        new = weight * proj
        column[:, at] = jnp.sum(new, axis=0, keepdims=True)
        share[:, at] = (K * (new + alpha_prior) * under).astype(BF16)

    def topic_z(dz):
        return remote(column, col_z.at[z], send_t.at[0, dz], recv_tz.at[z], z_=zo(dz))

    col_z[z] = column[...]
    for dz in range(1, 8):
        topic_z(dz).start()

    def wait_far(m):
        pltpu.make_async_copy(far.at[m], far.at[m], recv_f.at[m]).wait()

    def wait_near(m):
        for side in range(2):
            pltpu.make_async_copy(near.at[side, m], near.at[side, m], recv_n.at[side, m]).wait()

    def hop_copy(stage, q):
        source, target = ((4, hop1), (2, hop2))[stage]
        return remote(acc.at[source + q], target.at[q], send_z.at[stage, q], recv_z.at[stage, q], z_=zo(1))

    def hop_arrived(stage, q):
        target = (hop1, hop2)[stage]
        return pltpu.make_async_copy(target.at[q], target.at[q], recv_z.at[stage, q])

    wait_far(4)
    acc[4] = part[8, h] + far[4]

    @pl.when(a == 0)
    def _():
        for q in (4, 5):
            wait_near(q - 2)
        acc[4] += near[0, 2] + near[1, 2]
        acc[5] = near[0, 3] + near[1, 3]
        hop_copy(0, 1).start()

    hop_copy(0, 0).start()

    for q in (2, 3):
        wait_far(q)
        acc[q] = part[(4, 5)[q - 2], h] + far[q]
        m = q - 2 + 2 * a
        wait_near(m)
        acc[q] += near[0, m] + near[1, m]
    for q in (0, 1):
        wait_far(q)
        acc[q] = part[q, h] + far[q]

        @pl.when(a == 1)
        def _():
            wait_near(q)
            acc[q] += near[0, q] + near[1, q]

    hop_arrived(0, 0).wait()
    acc[2] += hop1[0]

    @pl.when(a == 0)
    def _():
        hop_arrived(0, 1).wait()
        acc[3] += hop1[1]

    for q in range(2):
        hop_copy(1, q).start()

    for dz in range(1, 8):
        q = zo(dz)
        pltpu.make_async_copy(col_z.at[q], col_z.at[q], recv_tz.at[q]).wait()
    column_z = col_z[0]
    for q in range(1, 8):
        column_z += col_z[q]
    col_x[x] = column_z

    def topic_x(dx):
        return remote(col_x.at[x], col_x.at[x], send_t.at[1, dx], recv_tx.at[x], x_=xo(dx))

    for dx in range(1, 4):
        topic_x(dx).start()

    for q in range(2):
        hop_arrived(1, q).wait()
        acc[q] += hop2[q]

    def piece(q, h_):
        return pl.ds(pl.multiple_of(q * KD + h_ * KH, KH), KH)

    def gather_copy(dx, dh, dc):
        return remote(
            acc.at[co(dc)],
            gathered.at[:, piece(own_docs, h)],
            send_g.at[dx, dh, dc],
            recv_g.at[own_docs, h],
            x_=xo(dx),
            h_=ho(dh),
            c_=co(dc),
        )

    fan = [(dx, dh, dc) for dx in (2, 1, 3, 0) for dh in range(2) for dc in range(2) if dx + dh + dc]
    for where in fan:
        gather_copy(*where).start()
    gathered[:, piece(own_docs, h)] = acc[c]

    for dx in range(1, 4):
        q = xo(dx)
        pltpu.make_async_copy(col_x.at[q], col_x.at[q], recv_tx.at[q]).wait()
    column_x = col_x[0]
    for q in range(1, 4):
        column_x += col_x[q]
    me = h * 4 + i
    col_p[me] = column_x

    def topic_p(dh, da, dc):
        return remote(
            col_p.at[me],
            col_p.at[me],
            send_t.at[2, 4 * dh + 2 * da + dc],
            recv_tp.at[me],
            h_=ho(dh),
            a_=ao(da),
            c_=co(dc),
        )

    plane = [(dh, da, dc) for dh in range(2) for da in range(2) for dc in range(2) if dh + da + dc]
    for where in plane:
        topic_p(*where).start()

    for dh, da, dc in plane:
        q = 4 * ho(dh) + 2 * ao(da) + co(dc)
        pltpu.make_async_copy(col_p.at[q], col_p.at[q], recv_tp.at[q]).wait()
    column_p = col_p[0]
    for q in range(1, 8):
        column_p += col_p[q]
    mean[...] = column_p * (1.0 / (WB * 32))

    for dx, dh, dc in fan:
        q = 2 * xo(dx) + co(dc)
        at = gathered.at[:, piece(q, ho(dh))]
        pltpu.make_async_copy(at, at, recv_g.at[q, ho(dh)]).wait()
    summed[...] = gathered[...]

    @pl.loop(0, CH)
    def _(r):
        column_copies(0, r, drain)
        column_copies(1, r, drain)

        @pl.when(i <= 2)
        def _():
            column_copies(2, r, drain)

        @pl.when(a == 0)
        def _():
            drain(relay(0, r))

        drain(relay(1, r))

        @pl.when(a == 1)
        def _():
            drain(relay(2, r))

    for dx, dc in others:
        drain(doc_copy(dx, dc))

    @pl.loop(0, SPAN)
    def _(k):
        for dx in range(1, 4):
            drain(ratio_out(k, dx))
            drain(ratio_relay(k, dx))
        drain(ratio_over(k))

    @pl.loop(0, 4)
    def _(m):
        for side in range(2):
            drain(near_copy(m, side))

    @pl.loop(0, 5)
    def _(m):
        drain(far_copy(m))

    drain(hop_copy(0, 0))

    @pl.when(a == 0)
    def _():
        drain(hop_copy(0, 1))

    for q in range(2):
        drain(hop_copy(1, q))
    for where in fan:
        drain(gather_copy(*where))
    for dz in range(1, 8):
        drain(topic_z(dz))
    for dx in range(1, 4):
        drain(topic_x(dx))
    for where in plane:
        drain(topic_p(*where))


def exchange(counts, tile_live, lengths, doc_mix, word_topic, topic_total):
    vmem = pl.BlockSpec(memory_space=pltpu.VMEM)
    smem = pl.BlockSpec(memory_space=pltpu.SMEM)
    dma = pltpu.SemaphoreType.DMA
    return pl.pallas_call(
        kernel,
        name="window",
        out_shape=(
            jax.ShapeDtypeStruct((DOCS, K), BF16),
            jax.ShapeDtypeStruct((WB, K), F32),
            jax.ShapeDtypeStruct((1, K), F32),
        ),
        in_specs=[vmem, smem, vmem, vmem, vmem, vmem],
        out_specs=(vmem, vmem, vmem),
        scratch_shapes=[
            pltpu.VMEM((SLOTS * WB, K), BF16),
            pltpu.VMEM((DOCS, K), BF16),
            pltpu.VMEM((DOCS, 1), F32),
            pltpu.VMEM((8 * DOCS, KD), BF16),
            pltpu.VMEM((DOCS, SPAN * WB), BF16),
            pltpu.VMEM((SPAN + 1, WB, 8 * DOCS), BF16),
            pltpu.VMEM((SPAN + 1, 2, WB, KH), F32),
            pltpu.VMEM((2, 4, WB, KH), F32),
            pltpu.VMEM((5, WB, KH), F32),
            pltpu.VMEM((6, WB, KH), F32),
            pltpu.VMEM((2, WB, KH), F32),
            pltpu.VMEM((2, WB, KH), F32),
            pltpu.VMEM((WB, K), F32),
            pltpu.VMEM((DOCS, WB), F32),
            pltpu.VMEM((1, K), F32),
            pltpu.VMEM((8, 1, K), F32),
            pltpu.VMEM((4, 1, K), F32),
            pltpu.VMEM((8, 1, K), F32),
            dma((3, CH, 4)),
            dma((SLOTS, CH)),
            dma((4, 2)),
            dma((8,)),
            dma((SPAN, 4)),
            dma((SPAN, 3)),
            dma((8, SPAN)),
            dma((4, 2)),
            dma((2, 4)),
            dma((5,)),
            dma((5,)),
            dma((2, 2)),
            dma((2, 2)),
            dma((4, 2, 2)),
            dma((8, 2)),
            dma((3, 8)),
            dma((8,)),
            dma((4,)),
            dma((8,)),
        ],
        compiler_params=pltpu.CompilerParams(
            collective_id=0, has_side_effects=True, vmem_limit_bytes=60 * 1024 * 1024
        ),
    )(counts, tile_live, lengths, doc_mix, word_topic, topic_total)


def local(counts, tile_live, doc_lengths, doc_mix, word_topic, topic_total):
    doc_share, word_sum, topic_mean = exchange(
        counts, tile_live, doc_lengths[:, None], doc_mix, word_topic, topic_total[None, :]
    )
    word_weight = (word_topic + beta_prior) / (topic_total + beta_prior * VOCAB)[None, :]
    return (doc_share, word_weight * word_sum, topic_mean[0])


def solution(mesh):
    return jax.shard_map(
        local,
        mesh=mesh,
        in_specs=(
            P(("grp", "blk"), None),
            P(("grp", "blk"), None),
            P(("grp", "blk")),
            P(("grp", "blk"), None),
            P("blk", None),
            P(),
        ),
        out_specs=(P(("grp", "blk"), None), P("blk", None), P()),
        check_vma=False,
    )
```

```python
import jax
import jax.numpy as jnp
from jax import lax
from jax.experimental import pallas as pl
from jax.experimental.pallas import tpu as pltpu
from jax.sharding import PartitionSpec as P

VOCAB = 262144

alpha_prior = 0.1
beta_prior = 0.01

MESH = pl.DeviceIdType.MESH
F32 = jnp.float32
BF16 = jnp.bfloat16

DOCS = 256
WB = 128
K = 4096
SPAN = 8
SLOTS = 11
CH = 4
ROWS = WB // CH
KD = K // 8
KH = KD // 2
PARTS = 2


def place(x, h, z, a, c):
    return {"grp": x * 2 + h, "blk": (z * 2 + a) * 2 + c}


def kernel(
    counts_in,
    live,
    lengths,
    mix_in,
    topic_in,
    total,
    share_out,
    topic_out,
    mean,
    counts,
    mix,
    topic,
    share,
    inverse,
    span,
    words,
    doc_low,
    scale,
    docs,
    ratio,
    ratio_t,
    part,
    near,
    far,
    acc,
    hop1,
    hop2,
    gathered,
    wlen,
    column,
    col_z,
    col_x,
    col_p,
    send_w,
    recv_w,
    send_d,
    recv_d,
    send_r,
    send_rf,
    recv_r,
    send_n,
    recv_n,
    send_f,
    recv_f,
    send_z,
    recv_z,
    send_g,
    recv_g,
    send_t,
    recv_tz,
    recv_tx,
    recv_tp,
    load,
    store,
):
    grp = lax.axis_index("grp")
    blk = lax.axis_index("blk")
    x = lax.div(grp, 2)
    h = lax.rem(grp, 2)
    z = lax.div(blk, 4)
    i = lax.rem(blk, 4)
    a = lax.div(i, 2)
    c = lax.rem(i, 2)
    i2 = 2 * (1 - a) + c

    def xo(dx):
        return lax.rem(x + dx, 4)

    def zo(dz):
        return lax.rem(z + dz + 8, 8)

    def ho(dh):
        return lax.rem(h + dh, 2)

    def ao(da):
        return lax.rem(a + da, 2)

    def co(dc):
        return lax.rem(c + dc, 2)

    def remote(src, dst, send, recv, x_=x, h_=h, z_=z, a_=a, c_=c):
        return pltpu.make_async_remote_copy(
            src_ref=src,
            dst_ref=dst,
            send_sem=send,
            recv_sem=recv,
            device_id=place(x_, h_, z_, a_, c_),
            device_id_type=MESH,
        )

    def topic_load(r):
        rows = pl.ds(pl.multiple_of(r * ROWS, ROWS), ROWS)
        return pltpu.make_async_copy(topic_in.at[rows, :], topic.at[rows, :], load.at[r])

    mix_load = pltpu.make_async_copy(mix_in, mix, load.at[CH])
    counts_load = pltpu.make_async_copy(counts_in, counts, load.at[CH + 1])
    for r in range(CH):
        topic_load(r).start()
    mix_load.start()
    counts_load.start()

    barrier = pltpu.get_barrier_semaphore()
    greeted = 0

    def greet(**where):
        at = dict(x=x, h=h, z=z, a=a, c=c)
        at.update(where)
        pl.semaphore_signal(barrier, inc=1, device_id=place(**at), device_id_type=MESH)

    for dz in range(1, 8):
        greet(z=zo(dz))
        greeted += 1
    for dh in range(2):
        for da in range(2):
            for dc in range(2):
                if dh + da + dc:
                    greet(h=ho(dh), a=ao(da), c=co(dc))
                    greeted += 1
    for dx in range(1, 4):
        for dh in range(2):
            for dc in range(2):
                greet(x=xo(dx), h=ho(dh), c=co(dc))
                greeted += 1

    def chunk(slot, r):
        return words.at[pl.ds(pl.multiple_of(slot * WB + r * ROWS, ROWS), ROWS), :]

    def to_z(j, r):
        slot = 4 * j + i
        return remote(chunk(slot, r), chunk(slot + 4, r), send_w.at[j, r, 0], recv_w.at[slot + 4, r], z_=zo(-1))

    def to_partner(j, r):
        slot = 4 * j + i
        return remote(chunk(slot, r), chunk(slot, r), send_w.at[j, r, 1], recv_w.at[slot, r], c_=1 - c)

    def to_y(j, r):
        slot = 4 * j + i
        side = jnp.where(r < CH // 2, h, 1 - h)
        return remote(
            chunk(slot, r), chunk(slot, r), send_w.at[j, r, 2], recv_w.at[slot, r], h_=side, a_=1 - a
        )

    def relay(j, r):
        slot = 4 * j + i2
        return remote(chunk(slot, r), chunk(slot, r), send_w.at[j, r, 3], recv_w.at[slot, r], c_=1 - c)

    def arrived(slot, r):
        return pltpu.make_async_copy(chunk(slot, r), chunk(slot, r), recv_w.at[slot, r])

    def column_copies(j, r, act):
        if j == 0:
            act(to_z(j, r))
        elif j == 1:
            @pl.when(i <= 2)
            def _():
                act(to_z(j, r))
        if j == 1:
            act(to_partner(j, r))
            act(to_y(j, r))
        else:
            @pl.when(c == (1 if j == 0 else 0))
            def _():
                act(to_partner(j, r))

            @pl.when(a == (1 if j == 0 else 0))
            def _():
                act(to_y(j, r))

    start = lambda copy: copy.start()
    drain = lambda copy: copy.wait_send()

    inverse[...] = 1.0 / (total[...] + beta_prior * VOCAB)
    span[...] = jnp.broadcast_to(lengths[...].astype(F32), (8, DOCS)).T[:, :1]

    @pl.loop(0, CH)
    def _(r):
        rows = pl.ds(pl.multiple_of(r * ROWS, ROWS), ROWS)
        own = pl.ds(pl.multiple_of(i * WB + r * ROWS, ROWS), ROWS)
        topic_load(r).wait()
        weight = (topic[rows, :] + beta_prior) * inverse[...]
        topic[rows, :] = weight
        words[own, :] = weight.astype(BF16)

        @pl.when(r == 0)
        def _():
            pl.semaphore_wait(barrier, greeted)

        @pl.when(r > 0)
        def _():
            column_copies(0, r - 1, start)

    own_docs = 2 * x + c
    mix_load.wait()

    @pl.loop(0, DOCS // 32)
    def _(n):
        rows = pl.ds(pl.multiple_of(n * 32, 32), 32)
        wide = mix[rows, :].astype(F32)
        factor = span[rows, :] / jnp.sum(wide, axis=1, keepdims=True)
        scale[rows, :] = factor
        doc_low[rows, :] = (wide * factor + alpha_prior).astype(BF16)

        @pl.when(n == 0)
        def _():
            column_copies(0, CH - 1, start)

    def doc_rows(q):
        return pl.ds(pl.multiple_of(q * DOCS, DOCS), DOCS)

    def topics(q):
        return pl.ds(pl.multiple_of(q * KD, KD), KD)

    def doc_copy(dx, dc):
        to = 2 * xo(dx) + co(dc)
        return remote(
            doc_low.at[:, topics(to)],
            docs.at[doc_rows(own_docs), :],
            send_d.at[dx, dc],
            recv_d.at[own_docs],
            x_=xo(dx),
            c_=co(dc),
        )

    others = [(dx, dc) for dx in range(4) for dc in range(2) if dx + dc]
    docs[doc_rows(own_docs), :] = doc_low[:, topics(own_docs)]
    for dx, dc in others:
        doc_copy(dx, dc).start()

    wlen[...] = jnp.zeros_like(wlen)
    for q in range(4):
        ratio_t[SPAN, :, 2 * q * DOCS : (2 * q + 1) * DOCS] = jnp.zeros((WB, DOCS), BF16)
        ratio_t[0, :, (2 * q + 1) * DOCS : (2 * q + 2) * DOCS] = jnp.zeros((WB, DOCS), BF16)

    def ratio_at(q, k):
        return ratio_t.at[k + lax.rem(q, 2), :, doc_rows(q)]

    def ratio_out(k, dx):
        return remote(
            ratio_at(own_docs, k), ratio_at(own_docs, k), send_r.at[k, dx], recv_r.at[own_docs, k], x_=xo(dx)
        )

    def ratio_over(k):
        return remote(
            ratio_at(own_docs, k), ratio_at(own_docs, k), send_r.at[k, 0], recv_r.at[own_docs, k], c_=1 - c
        )

    def ratio_relay(k, dx):
        q = 2 * xo(dx) + c
        return remote(ratio_at(q, k), ratio_at(q, k), send_rf.at[k, dx - 1], recv_r.at[q, k], c_=1 - c)

    def ratio_arrived(q, k):
        return pltpu.make_async_copy(ratio_at(q, k), ratio_at(q, k), recv_r.at[q, k])

    def meet(slot):
        k = slot - i
        block = words[pl.ds(pl.multiple_of(slot * WB, WB), WB), :]
        normalizer = lax.dot_general(
            doc_low[...], block, (((1,), (1,)), ((), ())), preferred_element_type=F32
        )
        at = pl.ds(pl.multiple_of(k * WB, WB), WB)
        half = DOCS // 2
        top = live[0, k].astype(F32)
        low = live[1, k].astype(F32)
        mask = jnp.where(lax.broadcasted_iota(jnp.int32, (DOCS, WB), 0) < half, top, low)
        kept = counts[:, at].astype(F32) * mask
        wide = kept / normalizer
        ratio_t[k + c, :, doc_rows(own_docs)] = wide.T.astype(BF16)
        ratio[:, at] = wide.astype(BF16)
        wlen[...] += kept
        for dx in range(1, 4):
            ratio_out(k, dx).start()
        ratio_over(k).start()

    def relay_ratio(k):
        for dx in range(1, 4):
            ratio_arrived(2 * xo(dx) + c, k).wait()
            ratio_relay(k, dx).start()

    def near_copy(m, side):
        n = m + 2 + 2 * lax.div(m, 2)
        return remote(
            part.at[n, side], near.at[h, m], send_n.at[m, side], recv_n.at[h, m], h_=side, a_=1 - a
        )

    def far_copy(m):
        n = m + 2 * lax.div(m, 2)
        return remote(part.at[n, 1 - h], far.at[m], send_f.at[m], recv_f.at[m], h_=1 - h)

    def products(n):
        @pl.when(n == 0)
        def _():
            for dx, dc in others:
                q = 2 * xo(dx) + co(dc)
                pltpu.make_async_copy(docs.at[doc_rows(q), :], docs.at[doc_rows(q), :], recv_d.at[q]).wait()

        k = n - (1 - c)

        @pl.when(jnp.logical_and(k >= 0, k < SPAN))
        def _():
            for dx in range(4):
                ratio_arrived(2 * xo(dx) + (1 - c), k).wait()

        made = jnp.dot(ratio_t[n], docs[...], preferred_element_type=F32)
        part[n, 0] = made[:, :KH]
        part[n, 1] = made[:, KH:]
        m = n - 2 * lax.div(n, 4)

        @pl.when(lax.rem(lax.div(n, 2), 2) == 1)
        def _():
            for side in range(2):
                near_copy(m - 2, side).start()

        @pl.when(lax.rem(lax.div(n, 2), 2) == 0)
        def _():
            far_copy(m).start()

    counts_load.wait()
    meet(i)

    @pl.loop(1, SLOTS + 4)
    def _(t):
        @pl.when(t <= 4)
        def _():
            r = t - 1
            arrived(4 + i, r).wait()
            column_copies(1, r, start)

        @pl.when(jnp.logical_and(t == 2, a == 0))
        def _():
            for r in range(CH):
                arrived(i2, r).wait()
                relay(0, r).start()

        @pl.when(jnp.logical_and(t >= 2, t <= 5))
        def _():
            r = t - 2
            arrived(4 + i2, r).wait()
            relay(1, r).start()

        @pl.when(jnp.logical_and(jnp.logical_and(t >= 5, t <= 8), i <= 2))
        def _():
            r = t - 5
            arrived(8 + i, r).wait()
            column_copies(2, r, start)

        @pl.when(jnp.logical_and(jnp.logical_and(t >= 6, t <= 9), a == 1))
        def _():
            r = t - 6
            arrived(8 + i2, r).wait()
            relay(2, r).start()

        back = t - 3 - i

        @pl.when(jnp.logical_and(back >= 0, back < SPAN))
        def _():
            relay_ratio(back)

        ready = t - 4 - 2 * a

        @pl.when(jnp.logical_and(ready >= 0, ready <= SPAN))
        def _():
            products(ready)

        slot = t - 1
        column_of = lax.rem(slot, 4)

        @pl.when(jnp.logical_and(slot > i, slot < i + SPAN))
        def _():
            @pl.when(jnp.logical_and(column_of != i, column_of != i2))
            def _():
                for r in range(CH):
                    arrived(slot, r).wait()

            meet(slot)

    length = jnp.sum(wlen[...], axis=1, keepdims=True)
    under = 1.0 / (length + K * alpha_prior)

    @pl.loop(0, K // 512)
    def _(n):
        at = pl.ds(pl.multiple_of(n * 512, 512), 512)
        proj = jnp.dot(
            ratio[...],
            words[pl.ds(pl.multiple_of(i * WB, WB), SPAN * WB), at],
            preferred_element_type=F32,
        )
        weight = mix[:, at].astype(F32) * scale[...] + alpha_prior
        new = weight * proj
        column[:, at] = jnp.sum(new, axis=0, keepdims=True)
        share[:, at] = (K * (new + alpha_prior) * under).astype(BF16)

    share_store = pltpu.make_async_copy(share, share_out, store.at[2])
    share_store.start()

    def topic_z(dz):
        return remote(column, col_z.at[z], send_t.at[0, dz], recv_tz.at[z], z_=zo(dz))

    col_z[z] = column[...]
    for dz in range(1, 8):
        topic_z(dz).start()

    def wait_far(m):
        pltpu.make_async_copy(far.at[m], far.at[m], recv_f.at[m]).wait()

    def wait_near(m):
        for side in range(2):
            pltpu.make_async_copy(near.at[side, m], near.at[side, m], recv_n.at[side, m]).wait()

    def part_rows(p):
        return slice(p * WB // PARTS, (p + 1) * WB // PARTS)

    def hop_copy(stage, q, p):
        source, target = ((4, hop1), (2, hop2))[stage]
        return remote(
            acc.at[source + q, part_rows(p), :],
            target.at[q, part_rows(p), :],
            send_z.at[stage, q, p],
            recv_z.at[stage, q, p],
            z_=zo(1),
        )

    def hop_arrived(stage, q, p):
        at = (hop1, hop2)[stage].at[q, part_rows(p), :]
        return pltpu.make_async_copy(at, at, recv_z.at[stage, q, p])

    wait_far(4)
    acc[4] = part[8, h] + far[4]

    @pl.when(a == 0)
    def _():
        for q in (4, 5):
            wait_near(q - 2)
        acc[4] += near[0, 2] + near[1, 2]
        acc[5] = near[0, 3] + near[1, 3]
        for p in range(PARTS):
            hop_copy(0, 1, p).start()

    for p in range(PARTS):
        hop_copy(0, 0, p).start()

    for q in (2, 3):
        wait_far(q)
        acc[q] = part[(4, 5)[q - 2], h] + far[q]
        m = q - 2 + 2 * a
        wait_near(m)
        acc[q] += near[0, m] + near[1, m]
    for q in (0, 1):
        wait_far(q)
        acc[q] = part[q, h] + far[q]

        @pl.when(a == 1)
        def _():
            wait_near(q)
            acc[q] += near[0, q] + near[1, q]

    for p in range(PARTS):
        rows = part_rows(p)
        hop_arrived(0, 0, p).wait()
        acc[2, rows] += hop1[0, rows]

        @pl.when(a == 0)
        def _():
            hop_arrived(0, 1, p).wait()
            acc[3, rows] += hop1[1, rows]

        for q in range(2):
            hop_copy(1, q, p).start()

    for dz in range(1, 8):
        q = zo(dz)
        pltpu.make_async_copy(col_z.at[q], col_z.at[q], recv_tz.at[q]).wait()
    column_z = col_z[0]
    for q in range(1, 8):
        column_z += col_z[q]
    col_x[x] = column_z

    def topic_x(dx):
        return remote(col_x.at[x], col_x.at[x], send_t.at[1, dx], recv_tx.at[x], x_=xo(dx))

    for dx in range(1, 4):
        topic_x(dx).start()

    def piece(q, h_):
        return pl.ds(pl.multiple_of(q * KD + h_ * KH, KH), KH)

    def gather_copy(p, dx, dh, dc):
        return remote(
            acc.at[co(dc), part_rows(p), :],
            gathered.at[part_rows(p), piece(own_docs, h)],
            send_g.at[p, dx, dh, dc],
            recv_g.at[p, own_docs, h],
            x_=xo(dx),
            h_=ho(dh),
            c_=co(dc),
        )

    fan = [(dx, dh, dc) for dx in (2, 1, 3, 0) for dh in range(2) for dc in range(2) if dx + dh + dc]
    for p in range(PARTS):
        rows = part_rows(p)
        for q in range(2):
            hop_arrived(1, q, p).wait()
            acc[q, rows] += hop2[q, rows]
        gathered[rows, piece(own_docs, h)] = acc[c, rows]
        for where in fan:
            gather_copy(p, *where).start()

    for dx in range(1, 4):
        q = xo(dx)
        pltpu.make_async_copy(col_x.at[q], col_x.at[q], recv_tx.at[q]).wait()
    column_x = col_x[0]
    for q in range(1, 4):
        column_x += col_x[q]
    me = h * 4 + i
    col_p[me] = column_x

    def topic_p(dh, da, dc):
        return remote(
            col_p.at[me],
            col_p.at[me],
            send_t.at[2, 4 * dh + 2 * da + dc],
            recv_tp.at[me],
            h_=ho(dh),
            a_=ao(da),
            c_=co(dc),
        )

    plane = [(dh, da, dc) for dh in range(2) for da in range(2) for dc in range(2) if dh + da + dc]
    for where in plane:
        topic_p(*where).start()

    for dh, da, dc in plane:
        q = 4 * ho(dh) + 2 * ao(da) + co(dc)
        pltpu.make_async_copy(col_p.at[q], col_p.at[q], recv_tp.at[q]).wait()
    column_p = col_p[0]
    for q in range(1, 8):
        column_p += col_p[q]
    mean[...] = column_p * (1.0 / (WB * 32))

    def topic_store(p):
        return pltpu.make_async_copy(gathered.at[part_rows(p), :], topic_out.at[part_rows(p), :], store.at[p])

    for p in range(PARTS):
        rows = part_rows(p)
        for dx, dh, dc in fan:
            q = 2 * xo(dx) + co(dc)
            at = gathered.at[rows, piece(q, ho(dh))]
            pltpu.make_async_copy(at, at, recv_g.at[p, q, ho(dh)]).wait()
        gathered[rows, :] = gathered[rows, :] * topic[rows, :]
        topic_store(p).start()

    @pl.loop(0, CH)
    def _(r):
        column_copies(0, r, drain)
        column_copies(1, r, drain)

        @pl.when(i <= 2)
        def _():
            column_copies(2, r, drain)

        @pl.when(a == 0)
        def _():
            drain(relay(0, r))

        drain(relay(1, r))

        @pl.when(a == 1)
        def _():
            drain(relay(2, r))

    for dx, dc in others:
        drain(doc_copy(dx, dc))

    @pl.loop(0, SPAN)
    def _(k):
        for dx in range(1, 4):
            drain(ratio_out(k, dx))
            drain(ratio_relay(k, dx))
        drain(ratio_over(k))

    @pl.loop(0, 4)
    def _(m):
        for side in range(2):
            drain(near_copy(m, side))

    @pl.loop(0, 5)
    def _(m):
        drain(far_copy(m))

    for p in range(PARTS):
        drain(hop_copy(0, 0, p))

        @pl.when(a == 0)
        def _():
            drain(hop_copy(0, 1, p))

        for q in range(2):
            drain(hop_copy(1, q, p))
        for where in fan:
            drain(gather_copy(p, *where))
    for dz in range(1, 8):
        drain(topic_z(dz))
    for dx in range(1, 4):
        drain(topic_x(dx))
    for where in plane:
        drain(topic_p(*where))
    share_store.wait()
    for p in range(PARTS):
        topic_store(p).wait()


def exchange(counts, tile_live, lengths, doc_mix, word_topic, topic_total):
    vmem = pl.BlockSpec(memory_space=pltpu.VMEM)
    hbm = pl.BlockSpec(memory_space=pltpu.HBM)
    smem = pl.BlockSpec(memory_space=pltpu.SMEM)
    dma = pltpu.SemaphoreType.DMA
    return pl.pallas_call(
        kernel,
        name="window",
        out_shape=(
            jax.ShapeDtypeStruct((DOCS, K), BF16),
            jax.ShapeDtypeStruct((WB, K), F32),
            jax.ShapeDtypeStruct((1, K), F32),
        ),
        in_specs=[hbm, smem, vmem, hbm, hbm, vmem],
        out_specs=(hbm, hbm, vmem),
        scratch_shapes=[
            pltpu.VMEM((DOCS, SPAN * WB), jnp.int32),
            pltpu.VMEM((DOCS, K), BF16),
            pltpu.VMEM((WB, K), F32),
            pltpu.VMEM((DOCS, K), BF16),
            pltpu.VMEM((1, K), F32),
            pltpu.VMEM((DOCS, 1), F32),
            pltpu.VMEM((SLOTS * WB, K), BF16),
            pltpu.VMEM((DOCS, K), BF16),
            pltpu.VMEM((DOCS, 1), F32),
            pltpu.VMEM((8 * DOCS, KD), BF16),
            pltpu.VMEM((DOCS, SPAN * WB), BF16),
            pltpu.VMEM((SPAN + 1, WB, 8 * DOCS), BF16),
            pltpu.VMEM((SPAN + 1, 2, WB, KH), F32),
            pltpu.VMEM((2, 4, WB, KH), F32),
            pltpu.VMEM((5, WB, KH), F32),
            pltpu.VMEM((6, WB, KH), F32),
            pltpu.VMEM((2, WB, KH), F32),
            pltpu.VMEM((2, WB, KH), F32),
            pltpu.VMEM((WB, K), F32),
            pltpu.VMEM((DOCS, WB), F32),
            pltpu.VMEM((1, K), F32),
            pltpu.VMEM((8, 1, K), F32),
            pltpu.VMEM((4, 1, K), F32),
            pltpu.VMEM((8, 1, K), F32),
            dma((3, CH, 4)),
            dma((SLOTS, CH)),
            dma((4, 2)),
            dma((8,)),
            dma((SPAN, 4)),
            dma((SPAN, 3)),
            dma((8, SPAN)),
            dma((4, 2)),
            dma((2, 4)),
            dma((5,)),
            dma((5,)),
            dma((2, 2, PARTS)),
            dma((2, 2, PARTS)),
            dma((PARTS, 4, 2, 2)),
            dma((PARTS, 8, 2)),
            dma((3, 8)),
            dma((8,)),
            dma((4,)),
            dma((8,)),
            dma((CH + 2,)),
            dma((PARTS + 1,)),
        ],
        compiler_params=pltpu.CompilerParams(
            collective_id=0, has_side_effects=True, vmem_limit_bytes=60 * 1024 * 1024
        ),
    )(counts, tile_live, lengths, doc_mix, word_topic, topic_total)


def local(counts, tile_live, doc_lengths, doc_mix, word_topic, topic_total):
    doc_share, topic_new, topic_mean = exchange(
        counts, tile_live, doc_lengths[None, :], doc_mix, word_topic, topic_total[None, :]
    )
    return (doc_share, topic_new, topic_mean[0])


def solution(mesh):
    return jax.shard_map(
        local,
        mesh=mesh,
        in_specs=(
            P(("grp", "blk"), None),
            P(("grp", "blk"), None),
            P(("grp", "blk")),
            P(("grp", "blk"), None),
            P("blk", None),
            P(),
        ),
        out_specs=(P(("grp", "blk"), None), P("blk", None), P()),
        check_vma=False,
    )
```

```python
import jax
import jax.numpy as jnp
from jax import lax
from jax.experimental import pallas as pl
from jax.experimental.pallas import tpu as pltpu
from jax.sharding import PartitionSpec as P

VOCAB = 262144

alpha_prior = 0.1
beta_prior = 0.01

MESH = pl.DeviceIdType.MESH
F32 = jnp.float32
BF16 = jnp.bfloat16

DOCS = 256
WB = 128
K = 4096
SPAN = 8
SLOTS = 11
CH = 4
ROWS = WB // CH
KD = K // 8
KH = KD // 2
PARTS = 2


def place(x, h, z, a, c):
    return {"grp": x * 2 + h, "blk": (z * 2 + a) * 2 + c}


def kernel(
    counts_in,
    live,
    lengths,
    mix_in,
    topic_in,
    total,
    share_out,
    topic_out,
    mean,
    counts,
    mix,
    topic,
    inverse,
    span,
    words,
    doc_low,
    scale,
    docs,
    ratio,
    ratio_t,
    part,
    near,
    far,
    acc,
    hop1,
    hop2,
    gathered,
    wlen,
    column,
    col_z,
    col_x,
    col_p,
    send_w,
    recv_w,
    send_d,
    recv_d,
    send_r,
    send_rf,
    recv_r,
    send_n,
    recv_n,
    send_f,
    recv_f,
    send_z,
    recv_z,
    send_g,
    recv_g,
    send_t,
    recv_tz,
    recv_tx,
    recv_tp,
    load,
):
    grp = lax.axis_index("grp")
    blk = lax.axis_index("blk")
    x = lax.div(grp, 2)
    h = lax.rem(grp, 2)
    z = lax.div(blk, 4)
    i = lax.rem(blk, 4)
    a = lax.div(i, 2)
    c = lax.rem(i, 2)
    i2 = 2 * (1 - a) + c

    def xo(dx):
        return lax.rem(x + dx, 4)

    def zo(dz):
        return lax.rem(z + dz + 8, 8)

    def ho(dh):
        return lax.rem(h + dh, 2)

    def ao(da):
        return lax.rem(a + da, 2)

    def co(dc):
        return lax.rem(c + dc, 2)

    def remote(src, dst, send, recv, x_=x, h_=h, z_=z, a_=a, c_=c):
        return pltpu.make_async_remote_copy(
            src_ref=src,
            dst_ref=dst,
            send_sem=send,
            recv_sem=recv,
            device_id=place(x_, h_, z_, a_, c_),
            device_id_type=MESH,
        )

    def topic_load(r):
        rows = pl.ds(pl.multiple_of(r * ROWS, ROWS), ROWS)
        return pltpu.make_async_copy(topic_in.at[rows, :], topic.at[rows, :], load.at[r])

    mix_load = pltpu.make_async_copy(mix_in, mix, load.at[CH])
    counts_load = pltpu.make_async_copy(counts_in, counts, load.at[CH + 1])
    for u in range(CH):
        topic_load(lax.rem(u + 2 * h, CH)).start()
    mix_load.start()
    counts_load.start()

    barrier = pltpu.get_barrier_semaphore()
    greeted = 0

    def greet(**where):
        at = dict(x=x, h=h, z=z, a=a, c=c)
        at.update(where)
        pl.semaphore_signal(barrier, inc=1, device_id=place(**at), device_id_type=MESH)

    for dz in range(1, 8):
        greet(z=zo(dz))
        greeted += 1
    for dh in range(2):
        for da in range(2):
            for dc in range(2):
                if dh + da + dc:
                    greet(h=ho(dh), a=ao(da), c=co(dc))
                    greeted += 1
    for dx in range(1, 4):
        for dh in range(2):
            for dc in range(2):
                greet(x=xo(dx), h=ho(dh), c=co(dc))
                greeted += 1

    def chunk(slot, r):
        return words.at[pl.ds(pl.multiple_of(slot * WB + r * ROWS, ROWS), ROWS), :]

    def to_z(j, r):
        slot = 4 * j + i
        return remote(chunk(slot, r), chunk(slot + 4, r), send_w.at[j, r, 0], recv_w.at[slot + 4, r], z_=zo(-1))

    def to_partner(j, r):
        slot = 4 * j + i
        return remote(chunk(slot, r), chunk(slot, r), send_w.at[j, r, 1], recv_w.at[slot, r], c_=1 - c)

    def to_y(j, r):
        slot = 4 * j + i
        return remote(
            chunk(slot, r), chunk(slot, r), send_w.at[j, r, 2], recv_w.at[slot, r], h_=lax.rem(r + h, 2), a_=1 - a
        )

    def to_other_y(r):
        slot = 8 + i
        return remote(
            chunk(slot, r), chunk(slot, r), send_w.at[2, r, 4], recv_w.at[slot, r], h_=lax.rem(r + h + 1, 2), a_=1 - a
        )

    def to_far(r):
        slot = 8 + i
        return remote(
            chunk(slot, r), chunk(slot, r), send_w.at[2, r, 0], recv_w.at[slot, r], h_=1 - h, c_=1 - c
        )

    def relay(j, r):
        slot = 4 * j + i2
        return remote(chunk(slot, r), chunk(slot, r), send_w.at[j, r, 3], recv_w.at[slot, r], c_=1 - c)

    def arrived(slot, r):
        return pltpu.make_async_copy(chunk(slot, r), chunk(slot, r), recv_w.at[slot, r])

    def mine(r):
        return lax.div(r, CH // 2) == h

    def column_copies(j, r, act):
        if j == 0:
            act(to_z(j, r))
        elif j == 1:
            @pl.when(jnp.logical_and(i <= 2, mine(r)))
            def _():
                act(to_z(j, r))
        else:
            @pl.when(c == 0)
            def _():
                act(to_far(r))

            @pl.when(a == 0)
            def _():
                act(to_other_y(r))
        if j == 1:
            act(to_partner(j, r))
            act(to_y(j, r))
        else:
            @pl.when(c == (1 if j == 0 else 0))
            def _():
                act(to_partner(j, r))

            @pl.when(a == (1 if j == 0 else 0))
            def _():
                act(to_y(j, r))

    start = lambda copy: copy.start()
    drain = lambda copy: copy.wait_send()

    inverse[...] = 1.0 / (total[...] + beta_prior * VOCAB)
    span[...] = jnp.broadcast_to(lengths[...].astype(F32), (8, DOCS)).T[:, :1]

    def turn(u):
        return lax.rem(u + 2 * h, CH)

    @pl.loop(0, CH)
    def _(u):
        r = turn(u)
        rows = pl.ds(pl.multiple_of(r * ROWS, ROWS), ROWS)
        own = pl.ds(pl.multiple_of(i * WB + r * ROWS, ROWS), ROWS)
        topic_load(r).wait()
        weight = (topic[rows, :] + beta_prior) * inverse[...]
        topic[rows, :] = weight
        words[own, :] = weight.astype(BF16)

        @pl.when(u == 0)
        def _():
            pl.semaphore_wait(barrier, greeted)

        @pl.when(u > 0)
        def _():
            column_copies(0, turn(u - 1), start)

    own_docs = 2 * x + c
    mix_load.wait()

    @pl.loop(0, DOCS // 32)
    def _(n):
        rows = pl.ds(pl.multiple_of(n * 32, 32), 32)
        wide = mix[rows, :].astype(F32)
        factor = span[rows, :] / jnp.sum(wide, axis=1, keepdims=True)
        scale[rows, :] = factor
        doc_low[rows, :] = (wide * factor + alpha_prior).astype(BF16)

        @pl.when(n == 0)
        def _():
            column_copies(0, turn(CH - 1), start)

    def doc_rows(q):
        return pl.ds(pl.multiple_of(q * DOCS, DOCS), DOCS)

    def topics(q):
        return pl.ds(pl.multiple_of(q * KD, KD), KD)

    def doc_copy(dx, dc):
        to = 2 * xo(dx) + co(dc)
        return remote(
            doc_low.at[:, topics(to)],
            docs.at[doc_rows(own_docs), :],
            send_d.at[dx, dc],
            recv_d.at[own_docs],
            x_=xo(dx),
            c_=co(dc),
        )

    others = [(dx, dc) for dx in range(4) for dc in range(2) if dx + dc]
    docs[doc_rows(own_docs), :] = doc_low[:, topics(own_docs)]
    for dx, dc in others:
        doc_copy(dx, dc).start()

    wlen[...] = jnp.zeros_like(wlen)
    for q in range(4):
        ratio_t[SPAN, :, 2 * q * DOCS : (2 * q + 1) * DOCS] = jnp.zeros((WB, DOCS), BF16)
        ratio_t[0, :, (2 * q + 1) * DOCS : (2 * q + 2) * DOCS] = jnp.zeros((WB, DOCS), BF16)

    def ratio_at(q, k):
        return ratio_t.at[k + lax.rem(q, 2), :, doc_rows(q)]

    def ratio_out(k, dx):
        return remote(
            ratio_at(own_docs, k), ratio_at(own_docs, k), send_r.at[k, dx], recv_r.at[own_docs, k], x_=xo(dx)
        )

    def ratio_over(k):
        return remote(
            ratio_at(own_docs, k), ratio_at(own_docs, k), send_r.at[k, 0], recv_r.at[own_docs, k], c_=1 - c
        )

    def ratio_relay(k, dx):
        q = 2 * xo(dx) + c
        return remote(ratio_at(q, k), ratio_at(q, k), send_rf.at[k, dx - 1], recv_r.at[q, k], c_=1 - c)

    def ratio_arrived(q, k):
        return pltpu.make_async_copy(ratio_at(q, k), ratio_at(q, k), recv_r.at[q, k])

    def meet(slot):
        k = slot - i
        block = words[pl.ds(pl.multiple_of(slot * WB, WB), WB), :]
        normalizer = lax.dot_general(
            doc_low[...], block, (((1,), (1,)), ((), ())), preferred_element_type=F32
        )
        at = pl.ds(pl.multiple_of(k * WB, WB), WB)
        half = DOCS // 2
        top = live[0, k].astype(F32)
        low = live[1, k].astype(F32)
        mask = jnp.where(lax.broadcasted_iota(jnp.int32, (DOCS, WB), 0) < half, top, low)
        kept = counts[:, at].astype(F32) * mask
        wide = kept / normalizer
        ratio_t[k + c, :, doc_rows(own_docs)] = wide.T.astype(BF16)
        ratio[:, at] = wide.astype(BF16)
        wlen[...] += kept
        for dx in range(1, 4):
            ratio_out(k, dx).start()
        ratio_over(k).start()

    def relay_ratio(k):
        for dx in range(1, 4):
            ratio_arrived(2 * xo(dx) + c, k).wait()
            ratio_relay(k, dx).start()

    def near_copy(m, side):
        n = m + 2 + 2 * lax.div(m, 2)
        return remote(
            part.at[n, side], near.at[h, m], send_n.at[m, side], recv_n.at[h, m], h_=side, a_=1 - a
        )

    def far_copy(m):
        n = m + 2 * lax.div(m, 2)
        return remote(part.at[n, 1 - h], far.at[m], send_f.at[m], recv_f.at[m], h_=1 - h)

    def products(n):
        @pl.when(n == 0)
        def _():
            for dx, dc in others:
                q = 2 * xo(dx) + co(dc)
                pltpu.make_async_copy(docs.at[doc_rows(q), :], docs.at[doc_rows(q), :], recv_d.at[q]).wait()

        k = n - (1 - c)

        @pl.when(jnp.logical_and(k >= 0, k < SPAN))
        def _():
            for dx in range(4):
                ratio_arrived(2 * xo(dx) + (1 - c), k).wait()

        made = jnp.dot(ratio_t[n], docs[...], preferred_element_type=F32)
        part[n, 0] = made[:, :KH]
        part[n, 1] = made[:, KH:]
        m = n - 2 * lax.div(n, 4)

        @pl.when(lax.rem(lax.div(n, 2), 2) == 1)
        def _():
            for side in range(2):
                near_copy(m - 2, side).start()

        @pl.when(lax.rem(lax.div(n, 2), 2) == 0)
        def _():
            far_copy(m).start()

    counts_load.wait()
    meet(i)

    @pl.loop(1, SLOTS + 4)
    def _(t):
        @pl.when(t <= 4)
        def _():
            r = turn(t - 1)
            arrived(4 + i, r).wait()
            column_copies(1, r, start)

        @pl.when(jnp.logical_and(t == 2, a == 0))
        def _():
            for u in range(CH):
                r = lax.rem(2 * h + CH - u, CH)
                arrived(i2, r).wait()
                relay(0, r).start()

        @pl.when(jnp.logical_and(t >= 2, t <= 5))
        def _():
            r = lax.rem(2 * h + CH + 2 - t, CH)
            arrived(4 + i2, r).wait()
            relay(1, r).start()

        @pl.when(jnp.logical_and(jnp.logical_and(t >= 5, t <= 6), i <= 2))
        def _():
            r = 2 * h + t - 5
            arrived(8 + i, r).wait()
            column_copies(2, r, start)

        @pl.when(jnp.logical_and(jnp.logical_and(t >= 6, t <= 7), a == 1))
        def _():
            for u in range(2):
                r = t - 6 + 2 * u
                arrived(8 + i2, r).wait()
                relay(2, r).start()

        back = t - 3 - i

        @pl.when(jnp.logical_and(back >= 0, back < SPAN))
        def _():
            relay_ratio(back)

        ready = t - 4 - 2 * a

        @pl.when(jnp.logical_and(ready >= 0, ready <= SPAN))
        def _():
            products(ready)

        slot = t - 1
        column_of = lax.rem(slot, 4)

        @pl.when(jnp.logical_and(slot > i, slot < i + SPAN))
        def _():
            @pl.when(jnp.logical_and(column_of != i, column_of != i2))
            def _():
                for r in range(CH):
                    arrived(slot, r).wait()

            meet(slot)

    length = jnp.sum(wlen[...], axis=1, keepdims=True)
    under = 1.0 / (length + K * alpha_prior)

    @pl.loop(0, K // 512)
    def _(n):
        at = pl.ds(pl.multiple_of(n * 512, 512), 512)
        proj = jnp.dot(
            ratio[...],
            words[pl.ds(pl.multiple_of(i * WB, WB), SPAN * WB), at],
            preferred_element_type=F32,
        )
        weight = mix[:, at].astype(F32) * scale[...] + alpha_prior
        new = weight * proj
        column[:, at] = jnp.sum(new, axis=0, keepdims=True)
        share_out[:, at] = (K * (new + alpha_prior) * under).astype(BF16)

    def topic_z(dz):
        return remote(column, col_z.at[z], send_t.at[0, dz], recv_tz.at[z], z_=zo(dz))

    col_z[z] = column[...]
    for dz in range(1, 8):
        topic_z(dz).start()

    def wait_far(m):
        pltpu.make_async_copy(far.at[m], far.at[m], recv_f.at[m]).wait()

    def wait_near(m):
        for side in range(2):
            pltpu.make_async_copy(near.at[side, m], near.at[side, m], recv_n.at[side, m]).wait()

    def part_rows(p):
        return slice(p * WB // PARTS, (p + 1) * WB // PARTS)

    def hop_copy(stage, q, p):
        source, target = ((4, hop1), (2, hop2))[stage]
        return remote(
            acc.at[source + q, part_rows(p), :],
            target.at[q, part_rows(p), :],
            send_z.at[stage, q, p],
            recv_z.at[stage, q, p],
            z_=zo(1),
        )

    def hop_arrived(stage, q, p):
        at = (hop1, hop2)[stage].at[q, part_rows(p), :]
        return pltpu.make_async_copy(at, at, recv_z.at[stage, q, p])

    wait_far(4)
    acc[4] = part[8, h] + far[4]

    @pl.when(a == 0)
    def _():
        for q in (4, 5):
            wait_near(q - 2)
        acc[4] += near[0, 2] + near[1, 2]
        acc[5] = near[0, 3] + near[1, 3]
        for p in range(PARTS):
            hop_copy(0, 1, p).start()

    for p in range(PARTS):
        hop_copy(0, 0, p).start()

    for q in (2, 3):
        wait_far(q)
        acc[q] = part[(4, 5)[q - 2], h] + far[q]
        m = q - 2 + 2 * a
        wait_near(m)
        acc[q] += near[0, m] + near[1, m]
    for q in (0, 1):
        wait_far(q)
        acc[q] = part[q, h] + far[q]

        @pl.when(a == 1)
        def _():
            wait_near(q)
            acc[q] += near[0, q] + near[1, q]

    for p in range(PARTS):
        rows = part_rows(p)
        hop_arrived(0, 0, p).wait()
        acc[2, rows] += hop1[0, rows]

        @pl.when(a == 0)
        def _():
            hop_arrived(0, 1, p).wait()
            acc[3, rows] += hop1[1, rows]

        for q in range(2):
            hop_copy(1, q, p).start()

    for dz in range(1, 8):
        q = zo(dz)
        pltpu.make_async_copy(col_z.at[q], col_z.at[q], recv_tz.at[q]).wait()
    column_z = col_z[0]
    for q in range(1, 8):
        column_z += col_z[q]
    col_x[x] = column_z

    def topic_x(dx):
        return remote(col_x.at[x], col_x.at[x], send_t.at[1, dx], recv_tx.at[x], x_=xo(dx))

    for dx in range(1, 4):
        topic_x(dx).start()

    def piece(q, h_):
        return pl.ds(pl.multiple_of(q * KD + h_ * KH, KH), KH)

    def gather_copy(p, dx, dh, dc):
        return remote(
            acc.at[co(dc), part_rows(p), :],
            gathered.at[part_rows(p), piece(own_docs, h)],
            send_g.at[p, dx, dh, dc],
            recv_g.at[p, own_docs, h],
            x_=xo(dx),
            h_=ho(dh),
            c_=co(dc),
        )

    fan = [(dx, dh, dc) for dx in (2, 1, 3, 0) for dh in range(2) for dc in range(2) if dx + dh + dc]
    for p in range(PARTS):
        rows = part_rows(p)
        for q in range(2):
            hop_arrived(1, q, p).wait()
            acc[q, rows] += hop2[q, rows]
        gathered[rows, piece(own_docs, h)] = acc[c, rows]
        for where in fan:
            gather_copy(p, *where).start()

    for dx in range(1, 4):
        q = xo(dx)
        pltpu.make_async_copy(col_x.at[q], col_x.at[q], recv_tx.at[q]).wait()
    column_x = col_x[0]
    for q in range(1, 4):
        column_x += col_x[q]
    me = h * 4 + i
    col_p[me] = column_x

    def topic_p(dh, da, dc):
        return remote(
            col_p.at[me],
            col_p.at[me],
            send_t.at[2, 4 * dh + 2 * da + dc],
            recv_tp.at[me],
            h_=ho(dh),
            a_=ao(da),
            c_=co(dc),
        )

    plane = [(dh, da, dc) for dh in range(2) for da in range(2) for dc in range(2) if dh + da + dc]
    for where in plane:
        topic_p(*where).start()

    for dh, da, dc in plane:
        q = 4 * ho(dh) + 2 * ao(da) + co(dc)
        pltpu.make_async_copy(col_p.at[q], col_p.at[q], recv_tp.at[q]).wait()
    column_p = col_p[0]
    for q in range(1, 8):
        column_p += col_p[q]
    mean[...] = column_p * (1.0 / (WB * 32))

    for p in range(PARTS):
        rows = part_rows(p)
        for dx, dh, dc in fan:
            q = 2 * xo(dx) + co(dc)
            at = gathered.at[rows, piece(q, ho(dh))]
            pltpu.make_async_copy(at, at, recv_g.at[p, q, ho(dh)]).wait()
        topic_out[rows, :] = gathered[rows, :] * topic[rows, :]

    @pl.loop(0, CH)
    def _(r):
        column_copies(0, r, drain)
        column_copies(1, r, drain)

        @pl.when(jnp.logical_and(i <= 2, mine(r)))
        def _():
            column_copies(2, r, drain)

        @pl.when(a == 0)
        def _():
            drain(relay(0, r))

        drain(relay(1, r))

        @pl.when(a == 1)
        def _():
            drain(relay(2, r))

    for dx, dc in others:
        drain(doc_copy(dx, dc))

    @pl.loop(0, SPAN)
    def _(k):
        for dx in range(1, 4):
            drain(ratio_out(k, dx))
            drain(ratio_relay(k, dx))
        drain(ratio_over(k))

    @pl.loop(0, 4)
    def _(m):
        for side in range(2):
            drain(near_copy(m, side))

    @pl.loop(0, 5)
    def _(m):
        drain(far_copy(m))

    for p in range(PARTS):
        drain(hop_copy(0, 0, p))

        @pl.when(a == 0)
        def _():
            drain(hop_copy(0, 1, p))

        for q in range(2):
            drain(hop_copy(1, q, p))
        for where in fan:
            drain(gather_copy(p, *where))
    for dz in range(1, 8):
        drain(topic_z(dz))
    for dx in range(1, 4):
        drain(topic_x(dx))
    for where in plane:
        drain(topic_p(*where))


def exchange(counts, tile_live, lengths, doc_mix, word_topic, topic_total):
    vmem = pl.BlockSpec(memory_space=pltpu.VMEM)
    hbm = pl.BlockSpec(memory_space=pltpu.HBM)
    smem = pl.BlockSpec(memory_space=pltpu.SMEM)
    dma = pltpu.SemaphoreType.DMA
    return pl.pallas_call(
        kernel,
        name="window",
        out_shape=(
            pltpu.VMEM((DOCS, K), BF16),
            pltpu.VMEM((WB, K), F32),
            jax.ShapeDtypeStruct((1, K), F32),
        ),
        in_specs=[hbm, smem, vmem, hbm, hbm, vmem],
        out_specs=(vmem, vmem, vmem),
        scratch_shapes=[
            pltpu.VMEM((DOCS, SPAN * WB), jnp.int32),
            pltpu.VMEM((DOCS, K), BF16),
            pltpu.VMEM((WB, K), F32),
            pltpu.VMEM((1, K), F32),
            pltpu.VMEM((DOCS, 1), F32),
            pltpu.VMEM((SLOTS * WB, K), BF16),
            pltpu.VMEM((DOCS, K), BF16),
            pltpu.VMEM((DOCS, 1), F32),
            pltpu.VMEM((8 * DOCS, KD), BF16),
            pltpu.VMEM((DOCS, SPAN * WB), BF16),
            pltpu.VMEM((SPAN + 1, WB, 8 * DOCS), BF16),
            pltpu.VMEM((SPAN + 1, 2, WB, KH), F32),
            pltpu.VMEM((2, 4, WB, KH), F32),
            pltpu.VMEM((5, WB, KH), F32),
            pltpu.VMEM((6, WB, KH), F32),
            pltpu.VMEM((2, WB, KH), F32),
            pltpu.VMEM((2, WB, KH), F32),
            pltpu.VMEM((WB, K), F32),
            pltpu.VMEM((DOCS, WB), F32),
            pltpu.VMEM((1, K), F32),
            pltpu.VMEM((8, 1, K), F32),
            pltpu.VMEM((4, 1, K), F32),
            pltpu.VMEM((8, 1, K), F32),
            dma((3, CH, 5)),
            dma((SLOTS, CH)),
            dma((4, 2)),
            dma((8,)),
            dma((SPAN, 4)),
            dma((SPAN, 3)),
            dma((8, SPAN)),
            dma((4, 2)),
            dma((2, 4)),
            dma((5,)),
            dma((5,)),
            dma((2, 2, PARTS)),
            dma((2, 2, PARTS)),
            dma((PARTS, 4, 2, 2)),
            dma((PARTS, 8, 2)),
            dma((3, 8)),
            dma((8,)),
            dma((4,)),
            dma((8,)),
            dma((CH + 2,)),
        ],
        compiler_params=pltpu.CompilerParams(
            collective_id=0, has_side_effects=True, vmem_limit_bytes=62820000
        ),
    )(counts, tile_live, lengths, doc_mix, word_topic, topic_total)


def local(counts, tile_live, doc_lengths, doc_mix, word_topic, topic_total):
    doc_share, topic_new, topic_mean = exchange(
        counts, tile_live, doc_lengths[None, :], doc_mix, word_topic, topic_total[None, :]
    )
    return (doc_share, topic_new, topic_mean[0])


def solution(mesh):
    return jax.shard_map(
        local,
        mesh=mesh,
        in_specs=(
            P(("grp", "blk"), None),
            P(("grp", "blk"), None),
            P(("grp", "blk")),
            P(("grp", "blk"), None),
            P("blk", None),
            P(),
        ),
        out_specs=(P(("grp", "blk"), None), P("blk", None), P()),
        check_vma=False,
    )
```

```python
import jax
import jax.numpy as jnp
from jax import lax
from jax.experimental import pallas as pl
from jax.experimental.pallas import tpu as pltpu
from jax.sharding import PartitionSpec as P

VOCAB = 262144

alpha_prior = 0.1
beta_prior = 0.01

MESH = pl.DeviceIdType.MESH
F32 = jnp.float32
BF16 = jnp.bfloat16

DOCS = 256
WB = 128
K = 4096
SPAN = 8
SLOTS = 11
CH = 4
ROWS = WB // CH
KD = K // 8
KH = KD // 2
PARTS = 4


def place(x, h, z, a, c):
    return {"grp": x * 2 + h, "blk": (z * 2 + a) * 2 + c}


def kernel(
    counts_in,
    live,
    lengths,
    mix_in,
    topic_in,
    total,
    share_out,
    topic_out,
    mean,
    counts,
    mix,
    topic,
    inverse,
    span,
    words,
    doc_low,
    scale,
    docs,
    ratio,
    ratio_t,
    part,
    near,
    far,
    acc,
    hop1,
    hop2,
    gathered,
    wlen,
    column,
    col_z,
    col_x,
    col_p,
    send_w,
    recv_w,
    send_d,
    recv_d,
    send_r,
    send_rf,
    recv_r,
    send_n,
    recv_n,
    send_f,
    recv_f,
    send_z,
    recv_z,
    send_g,
    send_p,
    recv_g,
    send_t,
    recv_tz,
    recv_tx,
    recv_tp,
    load,
):
    grp = lax.axis_index("grp")
    blk = lax.axis_index("blk")
    x = lax.div(grp, 2)
    h = lax.rem(grp, 2)
    z = lax.div(blk, 4)
    i = lax.rem(blk, 4)
    a = lax.div(i, 2)
    c = lax.rem(i, 2)
    i2 = 2 * (1 - a) + c

    def xo(dx):
        return lax.rem(x + dx, 4)

    def zo(dz):
        return lax.rem(z + dz + 8, 8)

    def ho(dh):
        return lax.rem(h + dh, 2)

    def ao(da):
        return lax.rem(a + da, 2)

    def co(dc):
        return lax.rem(c + dc, 2)

    def remote(src, dst, send, recv, x_=x, h_=h, z_=z, a_=a, c_=c):
        return pltpu.make_async_remote_copy(
            src_ref=src,
            dst_ref=dst,
            send_sem=send,
            recv_sem=recv,
            device_id=place(x_, h_, z_, a_, c_),
            device_id_type=MESH,
        )

    def topic_load(r):
        rows = pl.ds(pl.multiple_of(r * ROWS, ROWS), ROWS)
        return pltpu.make_async_copy(topic_in.at[rows, :], topic.at[rows, :], load.at[r])

    mix_load = pltpu.make_async_copy(mix_in, mix, load.at[CH])
    counts_load = pltpu.make_async_copy(counts_in, counts, load.at[CH + 1])
    for u in range(CH):
        topic_load(lax.rem(u + 2 * h, CH)).start()
    mix_load.start()
    counts_load.start()

    barrier = pltpu.get_barrier_semaphore()
    greeted = 0

    def greet(**where):
        at = dict(x=x, h=h, z=z, a=a, c=c)
        at.update(where)
        pl.semaphore_signal(barrier, inc=1, device_id=place(**at), device_id_type=MESH)

    for dz in range(1, 8):
        greet(z=zo(dz))
        greeted += 1
    for dh in range(2):
        for da in range(2):
            for dc in range(2):
                if dh + da + dc:
                    greet(h=ho(dh), a=ao(da), c=co(dc))
                    greeted += 1
    for dx in range(1, 4):
        for dh in range(2):
            for dc in range(2):
                greet(x=xo(dx), h=ho(dh), c=co(dc))
                greeted += 1

    def chunk(slot, r):
        return words.at[pl.ds(pl.multiple_of(slot * WB + r * ROWS, ROWS), ROWS), :]

    def to_z(j, r):
        slot = 4 * j + i
        return remote(chunk(slot, r), chunk(slot + 4, r), send_w.at[j, r, 0], recv_w.at[slot + 4, r], z_=zo(-1))

    def to_partner(j, r):
        slot = 4 * j + i
        return remote(chunk(slot, r), chunk(slot, r), send_w.at[j, r, 1], recv_w.at[slot, r], c_=1 - c)

    def to_y(j, r):
        slot = 4 * j + i
        return remote(
            chunk(slot, r), chunk(slot, r), send_w.at[j, r, 2], recv_w.at[slot, r], h_=lax.rem(r + h, 2), a_=1 - a
        )

    def to_other_y(r):
        slot = 8 + i
        return remote(
            chunk(slot, r), chunk(slot, r), send_w.at[2, r, 4], recv_w.at[slot, r], h_=lax.rem(r + h + 1, 2), a_=1 - a
        )

    def to_far(r):
        slot = 8 + i
        return remote(
            chunk(slot, r), chunk(slot, r), send_w.at[2, r, 0], recv_w.at[slot, r], h_=1 - h, c_=1 - c
        )

    def relay(j, r):
        slot = 4 * j + i2
        return remote(chunk(slot, r), chunk(slot, r), send_w.at[j, r, 3], recv_w.at[slot, r], c_=1 - c)

    def arrived(slot, r):
        return pltpu.make_async_copy(chunk(slot, r), chunk(slot, r), recv_w.at[slot, r])

    def mine(r):
        return lax.div(r, CH // 2) == h

    def column_copies(j, r, act):
        if j == 0:
            act(to_z(j, r))
        elif j == 1:
            @pl.when(jnp.logical_and(i <= 2, mine(r)))
            def _():
                act(to_z(j, r))
        else:
            @pl.when(c == 0)
            def _():
                act(to_far(r))

            @pl.when(a == 0)
            def _():
                act(to_other_y(r))
        if j == 1:
            act(to_partner(j, r))
            act(to_y(j, r))
        else:
            @pl.when(c == (1 if j == 0 else 0))
            def _():
                act(to_partner(j, r))

            @pl.when(a == (1 if j == 0 else 0))
            def _():
                act(to_y(j, r))

    start = lambda copy: copy.start()
    drain = lambda copy: copy.wait_send()

    inverse[...] = 1.0 / (total[...] + beta_prior * VOCAB)
    span[...] = jnp.broadcast_to(lengths[...].astype(F32), (8, DOCS)).T[:, :1]

    def turn(u):
        return lax.rem(u + 2 * h, CH)

    @pl.loop(0, CH)
    def _(u):
        r = turn(u)
        rows = pl.ds(pl.multiple_of(r * ROWS, ROWS), ROWS)
        own = pl.ds(pl.multiple_of(i * WB + r * ROWS, ROWS), ROWS)
        topic_load(r).wait()
        weight = (topic[rows, :] + beta_prior) * inverse[...]
        topic[rows, :] = weight
        words[own, :] = weight.astype(BF16)

        @pl.when(u == 0)
        def _():
            pl.semaphore_wait(barrier, greeted)

        @pl.when(u > 0)
        def _():
            column_copies(0, turn(u - 1), start)

    own_docs = 2 * x + c
    mix_load.wait()

    @pl.loop(0, DOCS // 32)
    def _(n):
        rows = pl.ds(pl.multiple_of(n * 32, 32), 32)
        wide = mix[rows, :].astype(F32)
        factor = span[rows, :] / jnp.sum(wide, axis=1, keepdims=True)
        scale[rows, :] = factor
        doc_low[rows, :] = (wide * factor + alpha_prior).astype(BF16)

        @pl.when(n == 0)
        def _():
            column_copies(0, turn(CH - 1), start)

    def doc_rows(q):
        return pl.ds(pl.multiple_of(q * DOCS, DOCS), DOCS)

    def topics(q):
        return pl.ds(pl.multiple_of(q * KD, KD), KD)

    def doc_copy(dx, dc):
        to = 2 * xo(dx) + co(dc)
        return remote(
            doc_low.at[:, topics(to)],
            docs.at[doc_rows(own_docs), :],
            send_d.at[dx, dc],
            recv_d.at[own_docs],
            x_=xo(dx),
            c_=co(dc),
        )

    others = [(dx, dc) for dx in range(4) for dc in range(2) if dx + dc]
    docs[doc_rows(own_docs), :] = doc_low[:, topics(own_docs)]
    for dx, dc in others:
        doc_copy(dx, dc).start()

    wlen[...] = jnp.zeros_like(wlen)
    for q in range(4):
        ratio_t[SPAN, :, 2 * q * DOCS : (2 * q + 1) * DOCS] = jnp.zeros((WB, DOCS), BF16)
        ratio_t[0, :, (2 * q + 1) * DOCS : (2 * q + 2) * DOCS] = jnp.zeros((WB, DOCS), BF16)

    def ratio_at(q, k):
        return ratio_t.at[k + lax.rem(q, 2), :, doc_rows(q)]

    def ratio_out(k, dx):
        return remote(
            ratio_at(own_docs, k), ratio_at(own_docs, k), send_r.at[k, dx], recv_r.at[own_docs, k], x_=xo(dx)
        )

    def ratio_over(k):
        return remote(
            ratio_at(own_docs, k), ratio_at(own_docs, k), send_r.at[k, 0], recv_r.at[own_docs, k], c_=1 - c
        )

    def ratio_relay(k, dx):
        q = 2 * xo(dx) + c
        return remote(ratio_at(q, k), ratio_at(q, k), send_rf.at[k, dx - 1], recv_r.at[q, k], c_=1 - c)

    def ratio_arrived(q, k):
        return pltpu.make_async_copy(ratio_at(q, k), ratio_at(q, k), recv_r.at[q, k])

    def meet(slot):
        k = slot - i
        block = words[pl.ds(pl.multiple_of(slot * WB, WB), WB), :]
        normalizer = lax.dot_general(
            doc_low[...], block, (((1,), (1,)), ((), ())), preferred_element_type=F32
        )
        at = pl.ds(pl.multiple_of(k * WB, WB), WB)
        half = DOCS // 2
        top = live[0, k].astype(F32)
        low = live[1, k].astype(F32)
        mask = jnp.where(lax.broadcasted_iota(jnp.int32, (DOCS, WB), 0) < half, top, low)
        kept = counts[:, at].astype(F32) * mask
        wide = kept / normalizer
        ratio_t[k + c, :, doc_rows(own_docs)] = wide.T.astype(BF16)
        ratio[:, at] = wide.astype(BF16)
        wlen[...] += kept
        for dx in range(1, 4):
            ratio_out(k, dx).start()
        ratio_over(k).start()

    def relay_ratio(k):
        for dx in range(1, 4):
            ratio_arrived(2 * xo(dx) + c, k).wait()
            ratio_relay(k, dx).start()

    def near_copy(m, side):
        n = m + 2 + 2 * lax.div(m, 2)
        return remote(
            part.at[n, side], near.at[h, m], send_n.at[m, side], recv_n.at[h, m], h_=side, a_=1 - a
        )

    def far_copy(m):
        n = m + 2 * lax.div(m, 2)
        return remote(part.at[n, 1 - h], far.at[m], send_f.at[m], recv_f.at[m], h_=1 - h)

    def products(n):
        @pl.when(n == 0)
        def _():
            for dx, dc in others:
                q = 2 * xo(dx) + co(dc)
                pltpu.make_async_copy(docs.at[doc_rows(q), :], docs.at[doc_rows(q), :], recv_d.at[q]).wait()

        k = n - (1 - c)

        @pl.when(jnp.logical_and(k >= 0, k < SPAN))
        def _():
            for dx in range(4):
                ratio_arrived(2 * xo(dx) + (1 - c), k).wait()

        made = jnp.dot(ratio_t[n], docs[...], preferred_element_type=F32)
        part[n, 0] = made[:, :KH]
        part[n, 1] = made[:, KH:]
        m = n - 2 * lax.div(n, 4)

        @pl.when(lax.rem(lax.div(n, 2), 2) == 1)
        def _():
            for side in range(2):
                near_copy(m - 2, side).start()

        @pl.when(lax.rem(lax.div(n, 2), 2) == 0)
        def _():
            far_copy(m).start()

    def topic_z(dz):
        return remote(column, col_z.at[z], send_t.at[0, dz], recv_tz.at[z], z_=zo(dz))

    def own_results():
        length = jnp.sum(wlen[...], axis=1, keepdims=True)
        under = 1.0 / (length + K * alpha_prior)

        @pl.loop(0, K // 512)
        def _(n):
            at = pl.ds(pl.multiple_of(n * 512, 512), 512)
            proj = jnp.dot(
                ratio[...],
                words[pl.ds(pl.multiple_of(i * WB, WB), SPAN * WB), at],
                preferred_element_type=F32,
            )
            weight = mix[:, at].astype(F32) * scale[...] + alpha_prior
            new = weight * proj
            column[:, at] = jnp.sum(new, axis=0, keepdims=True)
            share_out[:, at] = (K * (new + alpha_prior) * under).astype(BF16)

        col_z[z] = column[...]
        for dz in range(1, 8):
            topic_z(dz).start()

    counts_load.wait()
    meet(i)

    def slot_at(e):
        return jnp.where(jnp.logical_and(e >= 4, e < 8), 4 + lax.rem(e + 2 * a, 4), e)

    @pl.loop(1, 19)
    def _(t):
        @pl.when(t <= 4)
        def _():
            r = turn(t - 1)
            arrived(4 + i, r).wait()
            column_copies(1, r, start)

        @pl.when(jnp.logical_and(t == 2, a == 0))
        def _():
            for u in range(CH):
                r = lax.rem(2 * h + CH - u, CH)
                arrived(i2, r).wait()
                relay(0, r).start()

        @pl.when(jnp.logical_and(jnp.logical_or(t == 7, t == 9), i <= 2))
        def _():
            r = 2 * h + lax.div(t - 7, 2)
            arrived(8 + i, r).wait()
            column_copies(2, r, start)

        @pl.when(jnp.logical_or(jnp.logical_and(t >= 2, t <= 4), t == 7))
        def _():
            r = lax.rem(2 * h + CH + 2 - jnp.minimum(t, 5), CH)
            arrived(4 + i2, r).wait()
            relay(1, r).start()

        @pl.when(jnp.logical_or(t <= 10, t >= 15))
        def _():
            slot = slot_at(jnp.where(t <= 10, t - 3, t - 7))

            @pl.when(jnp.logical_and(t >= 3, jnp.logical_and(slot >= i, slot < i + SPAN)))
            def _():
                relay_ratio(slot - i)

        @pl.when(jnp.logical_or(t <= 11, t >= 16))
        def _():
            ready = slot_at(jnp.where(t <= 11, t - 4, t - 8)) - 2 * a

            @pl.when(jnp.logical_and(t >= 4, jnp.logical_and(ready >= 0, ready <= SPAN)))
            def _():
                products(ready)

        @pl.when(jnp.logical_and(jnp.logical_or(t == 10, t == 12), a == 1))
        def _():
            for u in range(2):
                r = lax.div(t - 10, 2) + 2 * u
                arrived(8 + i2, r).wait()
                relay(2, r).start()

        @pl.when(jnp.logical_or(t <= 8, jnp.logical_and(t >= 12, t <= 14)))
        def _():
            slot = slot_at(jnp.where(t <= 8, t - 1, t - 4))
            column_of = lax.rem(slot, 4)

            @pl.when(jnp.logical_and(slot > i, slot < i + SPAN))
            def _():
                @pl.when(jnp.logical_and(column_of != i, column_of != i2))
                def _():
                    for r in range(CH):
                        arrived(slot, r).wait()

                meet(slot)

        @pl.when(t == 14)
        def _():
            own_results()

    def wait_far(m):
        pltpu.make_async_copy(far.at[m], far.at[m], recv_f.at[m]).wait()

    def wait_near(m):
        for side in range(2):
            pltpu.make_async_copy(near.at[side, m], near.at[side, m], recv_n.at[side, m]).wait()

    def part_rows(p):
        return slice(p * WB // PARTS, (p + 1) * WB // PARTS)

    def hop_copy(stage, q, p):
        source, target = ((4, hop1), (2, hop2))[stage]
        return remote(
            acc.at[source + q, part_rows(p), :],
            target.at[q, part_rows(p), :],
            send_z.at[stage, q, p],
            recv_z.at[stage, q, p],
            z_=zo(1),
        )

    def hop_arrived(stage, q, p):
        at = (hop1, hop2)[stage].at[q, part_rows(p), :]
        return pltpu.make_async_copy(at, at, recv_z.at[stage, q, p])

    wait_far(4)
    acc[4] = part[8, h] + far[4]

    @pl.when(a == 0)
    def _():
        for q in (4, 5):
            wait_near(q - 2)
        acc[4] += near[0, 2] + near[1, 2]
        acc[5] = near[0, 3] + near[1, 3]
        for p in range(PARTS):
            hop_copy(0, 1, p).start()

    for p in range(PARTS):
        hop_copy(0, 0, p).start()

    for q in (2, 3):
        wait_far(q)
        acc[q] = part[(4, 5)[q - 2], h] + far[q]
        m = q - 2 + 2 * a
        wait_near(m)
        acc[q] += near[0, m] + near[1, m]
    for q in (0, 1):
        wait_far(q)
        acc[q] = part[q, h] + far[q]

        @pl.when(a == 1)
        def _():
            wait_near(q)
            acc[q] += near[0, q] + near[1, q]

    for p in range(PARTS):
        rows = part_rows(p)
        hop_arrived(0, 0, p).wait()
        acc[2, rows] += hop1[0, rows]

        @pl.when(a == 0)
        def _():
            hop_arrived(0, 1, p).wait()
            acc[3, rows] += hop1[1, rows]

        for q in range(2):
            hop_copy(1, q, p).start()

    for dz in range(1, 8):
        q = zo(dz)
        pltpu.make_async_copy(col_z.at[q], col_z.at[q], recv_tz.at[q]).wait()
    column_z = col_z[0]
    for q in range(1, 8):
        column_z += col_z[q]
    col_x[x] = column_z

    def topic_x(dx):
        return remote(col_x.at[x], col_x.at[x], send_t.at[1, dx], recv_tx.at[x], x_=xo(dx))

    for dx in range(1, 4):
        topic_x(dx).start()

    def piece(q, h_):
        return pl.ds(pl.multiple_of(q * KD + h_ * KH, KH), KH)

    def gather_copy(p, dx, dh, dc):
        return remote(
            acc.at[co(dc), part_rows(p), :],
            gathered.at[part_rows(p), piece(own_docs, h)],
            send_g.at[p, dx, dh, dc],
            recv_g.at[p, own_docs, h],
            x_=xo(dx),
            h_=ho(dh),
            c_=co(dc),
        )

    def gather_arrived(p, q, h_):
        at = gathered.at[part_rows(p), piece(q, h_)]
        return pltpu.make_async_copy(at, at, recv_g.at[p, q, h_])

    def pass_y(p, dx, dc):
        q = 2 * xo(dx) + dc
        at = gathered.at[part_rows(p), piece(q, h)]
        return remote(at, at, send_p.at[p, dx - 1, dc], recv_g.at[p, q, h], h_=1 - h)

    def pass_x(p, dx, dc):
        q = 2 * x + dc
        at = gathered.at[part_rows(p), piece(q, 1 - h)]
        return remote(at, at, send_p.at[p, dx - 1, dc], recv_g.at[p, q, 1 - h], x_=xo(dx))

    fan = [(0, 1, 0), (0, 1, 1), (2, 0, 0), (2, 0, 1), (1, 0, 0), (1, 0, 1), (3, 0, 0), (3, 0, 1), (0, 0, 1)]

    def spread(p):
        rows = part_rows(p)
        for q in range(2):
            hop_arrived(1, q, p).wait()
            acc[q, rows] += hop2[q, rows]
        gathered[rows, piece(own_docs, h)] = acc[c, rows]
        for where in fan:
            gather_copy(p, *where).start()

    def pass_on(p):
        if p % 2 == 0:
            for dx in (1, 3, 2):
                for dc in range(2):
                    gather_arrived(p, 2 * xo(dx) + dc, h).wait()
                    pass_y(p, dx, dc).start()
        else:
            for dc in range(2):
                gather_arrived(p, 2 * x + dc, 1 - h).wait()
                for dx in (2, 1, 3):
                    pass_x(p, dx, dc).start()

    for p in range(PARTS):
        spread(p)
        if p:
            pass_on(p - 1)
    pass_on(PARTS - 1)

    for dx in range(1, 4):
        q = xo(dx)
        pltpu.make_async_copy(col_x.at[q], col_x.at[q], recv_tx.at[q]).wait()
    column_x = col_x[0]
    for q in range(1, 4):
        column_x += col_x[q]
    me = h * 4 + i
    col_p[me] = column_x

    def topic_p(dh, da, dc):
        return remote(
            col_p.at[me],
            col_p.at[me],
            send_t.at[2, 4 * dh + 2 * da + dc],
            recv_tp.at[me],
            h_=ho(dh),
            a_=ao(da),
            c_=co(dc),
        )

    plane = [(dh, da, dc) for dh in range(2) for da in range(2) for dc in range(2) if dh + da + dc]
    for where in plane:
        topic_p(*where).start()

    for dh, da, dc in plane:
        q = 4 * ho(dh) + 2 * ao(da) + co(dc)
        pltpu.make_async_copy(col_p.at[q], col_p.at[q], recv_tp.at[q]).wait()
    column_p = col_p[0]
    for q in range(1, 8):
        column_p += col_p[q]
    mean[...] = column_p * (1.0 / (WB * 32))

    for p in range(PARTS):
        rows = part_rows(p)
        gather_arrived(p, 2 * x + 1 - c, h).wait()
        for dc in range(2):
            if p % 2 == 0:
                gather_arrived(p, 2 * x + dc, 1 - h).wait()
            for dx in range(1, 4):
                if p % 2 == 1:
                    gather_arrived(p, 2 * xo(dx) + dc, h).wait()
                gather_arrived(p, 2 * xo(dx) + dc, 1 - h).wait()
        topic_out[rows, :] = gathered[rows, :] * topic[rows, :]

    @pl.loop(0, CH)
    def _(r):
        column_copies(0, r, drain)
        column_copies(1, r, drain)

        @pl.when(jnp.logical_and(i <= 2, mine(r)))
        def _():
            column_copies(2, r, drain)

        @pl.when(a == 0)
        def _():
            drain(relay(0, r))

        drain(relay(1, r))

        @pl.when(a == 1)
        def _():
            drain(relay(2, r))

    for dx, dc in others:
        drain(doc_copy(dx, dc))

    @pl.loop(0, SPAN)
    def _(k):
        for dx in range(1, 4):
            drain(ratio_out(k, dx))
            drain(ratio_relay(k, dx))
        drain(ratio_over(k))

    @pl.loop(0, 4)
    def _(m):
        for side in range(2):
            drain(near_copy(m, side))

    @pl.loop(0, 5)
    def _(m):
        drain(far_copy(m))

    for p in range(PARTS):
        drain(hop_copy(0, 0, p))

        @pl.when(a == 0)
        def _():
            drain(hop_copy(0, 1, p))

        for q in range(2):
            drain(hop_copy(1, q, p))
        for where in fan:
            drain(gather_copy(p, *where))
        for dx in range(1, 4):
            for dc in range(2):
                drain((pass_x if p % 2 else pass_y)(p, dx, dc))
    for dz in range(1, 8):
        drain(topic_z(dz))
    for dx in range(1, 4):
        drain(topic_x(dx))
    for where in plane:
        drain(topic_p(*where))


def exchange(counts, tile_live, lengths, doc_mix, word_topic, topic_total):
    vmem = pl.BlockSpec(memory_space=pltpu.VMEM)
    hbm = pl.BlockSpec(memory_space=pltpu.HBM)
    smem = pl.BlockSpec(memory_space=pltpu.SMEM)
    dma = pltpu.SemaphoreType.DMA
    return pl.pallas_call(
        kernel,
        name="window",
        out_shape=(
            pltpu.VMEM((DOCS, K), BF16),
            pltpu.VMEM((WB, K), F32),
            jax.ShapeDtypeStruct((1, K), F32),
        ),
        in_specs=[hbm, smem, vmem, hbm, hbm, vmem],
        out_specs=(vmem, vmem, vmem),
        scratch_shapes=[
            pltpu.VMEM((DOCS, SPAN * WB), jnp.int32),
            pltpu.VMEM((DOCS, K), BF16),
            pltpu.VMEM((WB, K), F32),
            pltpu.VMEM((1, K), F32),
            pltpu.VMEM((DOCS, 1), F32),
            pltpu.VMEM((SLOTS * WB, K), BF16),
            pltpu.VMEM((DOCS, K), BF16),
            pltpu.VMEM((DOCS, 1), F32),
            pltpu.VMEM((8 * DOCS, KD), BF16),
            pltpu.VMEM((DOCS, SPAN * WB), BF16),
            pltpu.VMEM((SPAN + 1, WB, 8 * DOCS), BF16),
            pltpu.VMEM((SPAN + 1, 2, WB, KH), F32),
            pltpu.VMEM((2, 4, WB, KH), F32),
            pltpu.VMEM((5, WB, KH), F32),
            pltpu.VMEM((6, WB, KH), F32),
            pltpu.VMEM((2, WB, KH), F32),
            pltpu.VMEM((2, WB, KH), F32),
            pltpu.VMEM((WB, K), F32),
            pltpu.VMEM((DOCS, WB), F32),
            pltpu.VMEM((1, K), F32),
            pltpu.VMEM((8, 1, K), F32),
            pltpu.VMEM((4, 1, K), F32),
            pltpu.VMEM((8, 1, K), F32),
            dma((3, CH, 5)),
            dma((SLOTS, CH)),
            dma((4, 2)),
            dma((8,)),
            dma((SPAN, 4)),
            dma((SPAN, 3)),
            dma((8, SPAN)),
            dma((4, 2)),
            dma((2, 4)),
            dma((5,)),
            dma((5,)),
            dma((2, 2, PARTS)),
            dma((2, 2, PARTS)),
            dma((PARTS, 4, 2, 2)),
            dma((PARTS, 3, 2)),
            dma((PARTS, 8, 2)),
            dma((3, 8)),
            dma((8,)),
            dma((4,)),
            dma((8,)),
            dma((CH + 2,)),
        ],
        compiler_params=pltpu.CompilerParams(
            collective_id=0, has_side_effects=True, vmem_limit_bytes=62820000
        ),
    )(counts, tile_live, lengths, doc_mix, word_topic, topic_total)


def local(counts, tile_live, doc_lengths, doc_mix, word_topic, topic_total):
    doc_share, topic_new, topic_mean = exchange(
        counts, tile_live, doc_lengths[None, :], doc_mix, word_topic, topic_total[None, :]
    )
    return (doc_share, topic_new, topic_mean[0])


def solution(mesh):
    return jax.shard_map(
        local,
        mesh=mesh,
        in_specs=(
            P(("grp", "blk"), None),
            P(("grp", "blk"), None),
            P(("grp", "blk")),
            P(("grp", "blk"), None),
            P("blk", None),
            P(),
        ),
        out_specs=(P(("grp", "blk"), None), P("blk", None), P()),
        check_vma=False,
    )
```

```python
import jax
import jax.numpy as jnp
from jax import lax
from jax.experimental import pallas as pl
from jax.experimental.pallas import tpu as pltpu
from jax.sharding import PartitionSpec as P

VOCAB = 262144

alpha_prior = 0.1
beta_prior = 0.01

MESH = pl.DeviceIdType.MESH
F32 = jnp.float32
BF16 = jnp.bfloat16

DOCS = 256
WB = 128
K = 4096
SPAN = 8
SLOTS = 11
CH = 4
ROWS = WB // CH
KD = K // 8
KH = KD // 2
PARTS = 4


RELAYS = ({8: 0, 9: 2, 10: 4, 11: 6, 15: 8, 16: 9, 17: 10}, {8: 1, 9: 3, 10: 5, 11: 7})
PRODUCTS = ({9: 0, 10: 2, 11: 4, 13: 6, 16: 8, 17: 9, 18: 10}, {9: 1, 10: 3, 11: 5, 14: 7})


def pick(t, table):
    e = jnp.int32(-1)
    for step, place_ in table.items():
        e = jnp.where(t == step, place_, e)
    return e


def place(x, h, z, a, c):
    return {"grp": x * 2 + h, "blk": (z * 2 + a) * 2 + c}


def kernel(
    counts_in,
    live,
    lengths,
    mix_in,
    topic_in,
    total,
    share_out,
    topic_out,
    mean,
    counts,
    mix,
    topic,
    inverse,
    span,
    words,
    doc_low,
    scale,
    docs,
    ratio,
    ratio_t,
    part,
    near,
    far,
    acc,
    hop1,
    hop2,
    gathered,
    wlen,
    column,
    col_z,
    col_x,
    col_p,
    send_w,
    recv_w,
    send_d,
    recv_d,
    send_r,
    send_rf,
    recv_r,
    send_n,
    recv_n,
    send_f,
    recv_f,
    send_z,
    recv_z,
    send_g,
    send_p,
    recv_g,
    send_t,
    recv_tz,
    recv_tx,
    recv_tp,
    load,
):
    grp = lax.axis_index("grp")
    blk = lax.axis_index("blk")
    x = lax.div(grp, 2)
    h = lax.rem(grp, 2)
    z = lax.div(blk, 4)
    i = lax.rem(blk, 4)
    a = lax.div(i, 2)
    c = lax.rem(i, 2)
    i2 = 2 * (1 - a) + c

    def xo(dx):
        return lax.rem(x + dx, 4)

    def zo(dz):
        return lax.rem(z + dz + 8, 8)

    def ho(dh):
        return lax.rem(h + dh, 2)

    def ao(da):
        return lax.rem(a + da, 2)

    def co(dc):
        return lax.rem(c + dc, 2)

    def remote(src, dst, send, recv, x_=x, h_=h, z_=z, a_=a, c_=c):
        return pltpu.make_async_remote_copy(
            src_ref=src,
            dst_ref=dst,
            send_sem=send,
            recv_sem=recv,
            device_id=place(x_, h_, z_, a_, c_),
            device_id_type=MESH,
        )

    def topic_load(r):
        rows = pl.ds(pl.multiple_of(r * ROWS, ROWS), ROWS)
        return pltpu.make_async_copy(topic_in.at[rows, :], topic.at[rows, :], load.at[r])

    mix_load = pltpu.make_async_copy(mix_in, mix, load.at[CH])
    counts_load = pltpu.make_async_copy(counts_in, counts, load.at[CH + 1])
    for u in range(CH):
        topic_load(lax.rem(u + 2 * h, CH)).start()
    mix_load.start()
    counts_load.start()

    barrier = pltpu.get_barrier_semaphore()
    greeted = 0

    def greet(**where):
        at = dict(x=x, h=h, z=z, a=a, c=c)
        at.update(where)
        pl.semaphore_signal(barrier, inc=1, device_id=place(**at), device_id_type=MESH)

    for dz in range(1, 8):
        greet(z=zo(dz))
        greeted += 1
    for dh in range(2):
        for da in range(2):
            for dc in range(2):
                if dh + da + dc:
                    greet(h=ho(dh), a=ao(da), c=co(dc))
                    greeted += 1
    for dx in range(1, 4):
        for dh in range(2):
            for dc in range(2):
                greet(x=xo(dx), h=ho(dh), c=co(dc))
                greeted += 1

    def chunk(slot, r):
        return words.at[pl.ds(pl.multiple_of(slot * WB + r * ROWS, ROWS), ROWS), :]

    def to_z(j, r):
        slot = 4 * j + i
        return remote(chunk(slot, r), chunk(slot + 4, r), send_w.at[j, r, 0], recv_w.at[slot + 4, r], z_=zo(-1))

    def to_partner(j, r):
        slot = 4 * j + i
        return remote(chunk(slot, r), chunk(slot, r), send_w.at[j, r, 1], recv_w.at[slot, r], c_=1 - c)

    def to_y(j, r):
        slot = 4 * j + i
        return remote(
            chunk(slot, r), chunk(slot, r), send_w.at[j, r, 2], recv_w.at[slot, r], h_=lax.rem(r + h, 2), a_=1 - a
        )

    def to_other_y(r):
        slot = 8 + i
        return remote(
            chunk(slot, r), chunk(slot, r), send_w.at[2, r, 4], recv_w.at[slot, r], h_=lax.rem(r + h + 1, 2), a_=1 - a
        )

    def to_far(r):
        slot = 8 + i
        return remote(
            chunk(slot, r), chunk(slot, r), send_w.at[2, r, 0], recv_w.at[slot, r], h_=1 - h, c_=1 - c
        )

    def relay(j, r):
        slot = 4 * j + i2
        return remote(chunk(slot, r), chunk(slot, r), send_w.at[j, r, 3], recv_w.at[slot, r], c_=1 - c)

    def arrived(slot, r):
        return pltpu.make_async_copy(chunk(slot, r), chunk(slot, r), recv_w.at[slot, r])

    def mine(r):
        return lax.div(r, CH // 2) == h

    def column_copies(j, r, act):
        if j == 0:
            act(to_z(j, r))
        elif j == 1:
            @pl.when(jnp.logical_and(i <= 2, mine(r)))
            def _():
                act(to_z(j, r))
        else:
            @pl.when(c == 0)
            def _():
                act(to_far(r))

            @pl.when(a == 0)
            def _():
                act(to_other_y(r))
        if j == 1:
            act(to_partner(j, r))
            act(to_y(j, r))
        else:
            @pl.when(c == (1 if j == 0 else 0))
            def _():
                act(to_partner(j, r))

            @pl.when(a == (1 if j == 0 else 0))
            def _():
                act(to_y(j, r))

    start = lambda copy: copy.start()
    drain = lambda copy: copy.wait_send()

    inverse[...] = 1.0 / (total[...] + beta_prior * VOCAB)
    span[...] = jnp.broadcast_to(lengths[...].astype(F32), (8, DOCS)).T[:, :1]

    def turn(u):
        return lax.rem(u + 2 * h, CH)

    @pl.loop(0, CH)
    def _(u):
        r = turn(u)
        rows = pl.ds(pl.multiple_of(r * ROWS, ROWS), ROWS)
        own = pl.ds(pl.multiple_of(i * WB + r * ROWS, ROWS), ROWS)
        topic_load(r).wait()
        weight = (topic[rows, :] + beta_prior) * inverse[...]
        topic[rows, :] = weight
        words[own, :] = weight.astype(BF16)

        @pl.when(u == 0)
        def _():
            pl.semaphore_wait(barrier, greeted)

        @pl.when(u > 0)
        def _():
            column_copies(0, turn(u - 1), start)

    own_docs = 2 * x + c
    mix_load.wait()

    @pl.loop(0, DOCS // 32)
    def _(n):
        rows = pl.ds(pl.multiple_of(n * 32, 32), 32)
        wide = mix[rows, :].astype(F32)
        factor = span[rows, :] / jnp.sum(wide, axis=1, keepdims=True)
        scale[rows, :] = factor
        doc_low[rows, :] = (wide * factor + alpha_prior).astype(BF16)

        @pl.when(n == 0)
        def _():
            column_copies(0, turn(CH - 1), start)

    def doc_rows(q):
        return pl.ds(pl.multiple_of(q * DOCS, DOCS), DOCS)

    def topics(q):
        return pl.ds(pl.multiple_of(q * KD, KD), KD)

    def doc_copy(dx, dc):
        to = 2 * xo(dx) + co(dc)
        return remote(
            doc_low.at[:, topics(to)],
            docs.at[doc_rows(own_docs), :],
            send_d.at[dx, dc],
            recv_d.at[own_docs],
            x_=xo(dx),
            c_=co(dc),
        )

    others = [(dx, dc) for dx in range(4) for dc in range(2) if dx + dc]
    wlen[...] = jnp.zeros_like(wlen)
    for q in range(4):
        ratio_t[SPAN, :, 2 * q * DOCS : (2 * q + 1) * DOCS] = jnp.zeros((WB, DOCS), BF16)
        ratio_t[0, :, (2 * q + 1) * DOCS : (2 * q + 2) * DOCS] = jnp.zeros((WB, DOCS), BF16)

    def ratio_at(q, k):
        return ratio_t.at[k + lax.rem(q, 2), :, doc_rows(q)]

    def ratio_out(k, dx):
        return remote(
            ratio_at(own_docs, k), ratio_at(own_docs, k), send_r.at[k, dx], recv_r.at[own_docs, k], x_=xo(dx)
        )

    def ratio_over(k):
        return remote(
            ratio_at(own_docs, k), ratio_at(own_docs, k), send_r.at[k, 0], recv_r.at[own_docs, k], c_=1 - c
        )

    def ratio_relay(k, dx):
        q = 2 * xo(dx) + c
        return remote(ratio_at(q, k), ratio_at(q, k), send_rf.at[k, dx - 1], recv_r.at[q, k], c_=1 - c)

    def ratio_arrived(q, k):
        return pltpu.make_async_copy(ratio_at(q, k), ratio_at(q, k), recv_r.at[q, k])

    def meet(slot):
        k = slot - i
        block = words[pl.ds(pl.multiple_of(slot * WB, WB), WB), :]
        normalizer = lax.dot_general(
            doc_low[...], block, (((1,), (1,)), ((), ())), preferred_element_type=F32
        )
        at = pl.ds(pl.multiple_of(k * WB, WB), WB)
        half = DOCS // 2
        top = live[0, k].astype(F32)
        low = live[1, k].astype(F32)
        mask = jnp.where(lax.broadcasted_iota(jnp.int32, (DOCS, WB), 0) < half, top, low)
        kept = counts[:, at].astype(F32) * mask
        wide = kept / normalizer
        ratio_t[k + c, :, doc_rows(own_docs)] = wide.T.astype(BF16)
        ratio[:, at] = wide.astype(BF16)
        wlen[...] += kept
        for dx in range(1, 4):
            ratio_out(k, dx).start()
        ratio_over(k).start()

    def relay_ratio(k):
        for dx in range(1, 4):
            ratio_arrived(2 * xo(dx) + c, k).wait()
            ratio_relay(k, dx).start()

    def near_copy(m, side):
        n = m + 2 + 2 * lax.div(m, 2)
        return remote(
            part.at[n, side], near.at[h, m], send_n.at[m, side], recv_n.at[h, m], h_=side, a_=1 - a
        )

    def far_copy(m):
        n = m + 2 * lax.div(m, 2)
        return remote(part.at[n, 1 - h], far.at[m], send_f.at[m], recv_f.at[m], h_=1 - h)

    def products(n):
        @pl.when(n == 0)
        def _():
            for dx, dc in others:
                q = 2 * xo(dx) + co(dc)
                pltpu.make_async_copy(docs.at[doc_rows(q), :], docs.at[doc_rows(q), :], recv_d.at[q]).wait()

        k = n - (1 - c)

        @pl.when(jnp.logical_and(k >= 0, k < SPAN))
        def _():
            for dx in range(4):
                ratio_arrived(2 * xo(dx) + (1 - c), k).wait()

        made = jnp.dot(ratio_t[n], docs[...], preferred_element_type=F32)
        part[n, 0] = made[:, :KH]
        part[n, 1] = made[:, KH:]
        m = n - 2 * lax.div(n, 4)

        @pl.when(lax.rem(lax.div(n, 2), 2) == 1)
        def _():
            for side in range(2):
                near_copy(m - 2, side).start()

        @pl.when(lax.rem(lax.div(n, 2), 2) == 0)
        def _():
            far_copy(m).start()

    def topic_z(dz):
        return remote(column, col_z.at[z], send_t.at[0, dz], recv_tz.at[z], z_=zo(dz))

    def own_results():
        length = jnp.sum(wlen[...], axis=1, keepdims=True)
        under = 1.0 / (length + K * alpha_prior)

        @pl.loop(0, K // 512)
        def _(n):
            at = pl.ds(pl.multiple_of(n * 512, 512), 512)
            proj = jnp.dot(
                ratio[...],
                words[pl.ds(pl.multiple_of(i * WB, WB), SPAN * WB), at],
                preferred_element_type=F32,
            )
            weight = mix[:, at].astype(F32) * scale[...] + alpha_prior
            new = weight * proj
            column[:, at] = jnp.sum(new, axis=0, keepdims=True)
            share_out[:, at] = (K * (new + alpha_prior) * under).astype(BF16)

        col_z[z] = column[...]
        for dz in range(1, 8):
            topic_z(dz).start()

    counts_load.wait()
    meet(i)
    docs[doc_rows(own_docs), :] = doc_low[:, topics(own_docs)]
    for dx, dc in others:
        doc_copy(dx, dc).start()

    def slot_at(e):
        return jnp.where(jnp.logical_and(e >= 4, e < 8), 4 + lax.rem(e + 2 * a, 4), e)

    @pl.loop(1, 19)
    def _(t):
        @pl.when(t <= 4)
        def _():
            r = turn(t - 1)
            arrived(4 + i, r).wait()
            column_copies(1, r, start)

        @pl.when(jnp.logical_and(t == 2, a == 0))
        def _():
            for u in range(CH):
                r = lax.rem(2 * h + CH - u, CH)
                arrived(i2, r).wait()
                relay(0, r).start()

        @pl.when(jnp.logical_and(jnp.logical_or(t == 7, t == 9), i <= 2))
        def _():
            r = 2 * h + lax.div(t - 7, 2)
            arrived(8 + i, r).wait()
            column_copies(2, r, start)

        @pl.when(jnp.logical_or(jnp.logical_and(t >= 2, t <= 4), t == 7))
        def _():
            r = lax.rem(2 * h + CH + 2 - jnp.minimum(t, 5), CH)
            arrived(4 + i2, r).wait()
            relay(1, r).start()

        @pl.when(jnp.logical_and(jnp.logical_or(t == 10, t == 12), a == 1))
        def _():
            for u in range(2):
                r = lax.div(t - 10, 2) + 2 * u
                arrived(8 + i2, r).wait()
                relay(2, r).start()

        @pl.when(jnp.logical_or(t <= 8, jnp.logical_and(t >= 12, t <= 14)))
        def _():
            slot = slot_at(jnp.where(t <= 8, t - 1, t - 4))
            column_of = lax.rem(slot, 4)

            @pl.when(jnp.logical_and(slot > i, slot < i + SPAN))
            def _():
                @pl.when(jnp.logical_and(column_of != i, column_of != i2))
                def _():
                    for r in range(CH):
                        arrived(slot, r).wait()

                meet(slot)

        for table in PRODUCTS:
            e = pick(t, table)
            ready = slot_at(e) - 2 * a

            @pl.when(jnp.logical_and(e >= 0, jnp.logical_and(ready >= 0, ready <= SPAN)))
            def _():
                products(ready)

        for table in RELAYS:
            e = pick(t, table)
            slot = slot_at(e)

            @pl.when(jnp.logical_and(e >= 0, jnp.logical_and(slot >= i, slot < i + SPAN)))
            def _():
                relay_ratio(slot - i)

        @pl.when(t == 14)
        def _():
            own_results()

    def wait_far(m):
        pltpu.make_async_copy(far.at[m], far.at[m], recv_f.at[m]).wait()

    def wait_near(m):
        for side in range(2):
            pltpu.make_async_copy(near.at[side, m], near.at[side, m], recv_n.at[side, m]).wait()

    def part_rows(p):
        return slice(p * WB // PARTS, (p + 1) * WB // PARTS)

    def hop_copy(stage, q, p):
        source, target = ((4, hop1), (2, hop2))[stage]
        return remote(
            acc.at[source + q, part_rows(p), :],
            target.at[q, part_rows(p), :],
            send_z.at[stage, q, p],
            recv_z.at[stage, q, p],
            z_=zo(1),
        )

    def hop_arrived(stage, q, p):
        at = (hop1, hop2)[stage].at[q, part_rows(p), :]
        return pltpu.make_async_copy(at, at, recv_z.at[stage, q, p])

    for q in (0, 1):
        wait_far(q)
        acc[q] = part[q, h] + far[q]

        @pl.when(a == 1)
        def _():
            wait_near(q)
            acc[q] += near[0, q] + near[1, q]

    wait_far(4)
    acc[4] = part[8, h] + far[4]

    @pl.when(a == 0)
    def _():
        for q in (4, 5):
            wait_near(q - 2)
        acc[4] += near[0, 2] + near[1, 2]
        acc[5] = near[0, 3] + near[1, 3]
        for p in range(PARTS):
            hop_copy(0, 1, p).start()

    for p in range(PARTS):
        hop_copy(0, 0, p).start()

    for q in (2, 3):
        wait_far(q)
        acc[q] = part[(4, 5)[q - 2], h] + far[q]
        m = q - 2 + 2 * a
        wait_near(m)
        acc[q] += near[0, m] + near[1, m]
    for p in range(PARTS):
        rows = part_rows(p)
        hop_arrived(0, 0, p).wait()
        acc[2, rows] += hop1[0, rows]

        @pl.when(a == 0)
        def _():
            hop_arrived(0, 1, p).wait()
            acc[3, rows] += hop1[1, rows]

        for q in range(2):
            hop_copy(1, q, p).start()

    for dz in range(1, 8):
        q = zo(dz)
        pltpu.make_async_copy(col_z.at[q], col_z.at[q], recv_tz.at[q]).wait()
    column_z = col_z[0]
    for q in range(1, 8):
        column_z += col_z[q]
    col_x[x] = column_z

    def topic_x(dx):
        return remote(col_x.at[x], col_x.at[x], send_t.at[1, dx], recv_tx.at[x], x_=xo(dx))

    for dx in range(1, 4):
        topic_x(dx).start()

    def piece(q, h_):
        return pl.ds(pl.multiple_of(q * KD + h_ * KH, KH), KH)

    def gather_copy(p, dx, dh, dc):
        return remote(
            acc.at[co(dc), part_rows(p), :],
            gathered.at[part_rows(p), piece(own_docs, h)],
            send_g.at[p, dx, dh, dc],
            recv_g.at[p, own_docs, h],
            x_=xo(dx),
            h_=ho(dh),
            c_=co(dc),
        )

    def gather_arrived(p, q, h_):
        at = gathered.at[part_rows(p), piece(q, h_)]
        return pltpu.make_async_copy(at, at, recv_g.at[p, q, h_])

    def pass_y(p, dx, dc):
        q = 2 * xo(dx) + dc
        at = gathered.at[part_rows(p), piece(q, h)]
        return remote(at, at, send_p.at[p, dx - 1, dc], recv_g.at[p, q, h], h_=1 - h)

    def pass_x(p, dx, dc):
        q = 2 * x + dc
        at = gathered.at[part_rows(p), piece(q, 1 - h)]
        return remote(at, at, send_p.at[p, dx - 1, dc], recv_g.at[p, q, 1 - h], x_=xo(dx))

    fan = [(0, 1, 0), (0, 1, 1), (2, 0, 0), (2, 0, 1), (1, 0, 0), (1, 0, 1), (3, 0, 0), (3, 0, 1), (0, 0, 1)]

    def spread(p):
        rows = part_rows(p)
        for q in range(2):
            hop_arrived(1, q, p).wait()
            acc[q, rows] += hop2[q, rows]
        gathered[rows, piece(own_docs, h)] = acc[c, rows]
        for where in fan:
            gather_copy(p, *where).start()

    def pass_on(p):
        if p % 2 == 0:
            for dx in (1, 3, 2):
                for dc in range(2):
                    gather_arrived(p, 2 * xo(dx) + dc, h).wait()
                    pass_y(p, dx, dc).start()
        else:
            for dc in range(2):
                gather_arrived(p, 2 * x + dc, 1 - h).wait()
                for dx in (2, 1, 3):
                    pass_x(p, dx, dc).start()

    for p in range(PARTS):
        spread(p)
        if p:
            pass_on(p - 1)
    pass_on(PARTS - 1)

    for dx in range(1, 4):
        q = xo(dx)
        pltpu.make_async_copy(col_x.at[q], col_x.at[q], recv_tx.at[q]).wait()
    column_x = col_x[0]
    for q in range(1, 4):
        column_x += col_x[q]
    me = h * 4 + i
    col_p[me] = column_x

    def topic_p(dh, da, dc):
        return remote(
            col_p.at[me],
            col_p.at[me],
            send_t.at[2, 4 * dh + 2 * da + dc],
            recv_tp.at[me],
            h_=ho(dh),
            a_=ao(da),
            c_=co(dc),
        )

    plane = [(dh, da, dc) for dh in range(2) for da in range(2) for dc in range(2) if dh + da + dc]
    for where in plane:
        topic_p(*where).start()

    for dh, da, dc in plane:
        q = 4 * ho(dh) + 2 * ao(da) + co(dc)
        pltpu.make_async_copy(col_p.at[q], col_p.at[q], recv_tp.at[q]).wait()
    column_p = col_p[0]
    for q in range(1, 8):
        column_p += col_p[q]
    mean[...] = column_p * (1.0 / (WB * 32))

    for p in range(PARTS):
        rows = part_rows(p)
        gather_arrived(p, 2 * x + 1 - c, h).wait()
        for dc in range(2):
            if p % 2 == 0:
                gather_arrived(p, 2 * x + dc, 1 - h).wait()
            for dx in range(1, 4):
                if p % 2 == 1:
                    gather_arrived(p, 2 * xo(dx) + dc, h).wait()
                gather_arrived(p, 2 * xo(dx) + dc, 1 - h).wait()
        topic_out[rows, :] = gathered[rows, :] * topic[rows, :]

    @pl.loop(0, CH)
    def _(r):
        column_copies(0, r, drain)
        column_copies(1, r, drain)

        @pl.when(jnp.logical_and(i <= 2, mine(r)))
        def _():
            column_copies(2, r, drain)

        @pl.when(a == 0)
        def _():
            drain(relay(0, r))

        drain(relay(1, r))

        @pl.when(a == 1)
        def _():
            drain(relay(2, r))

    for dx, dc in others:
        drain(doc_copy(dx, dc))

    @pl.loop(0, SPAN)
    def _(k):
        for dx in range(1, 4):
            drain(ratio_out(k, dx))
            drain(ratio_relay(k, dx))
        drain(ratio_over(k))

    @pl.loop(0, 4)
    def _(m):
        for side in range(2):
            drain(near_copy(m, side))

    @pl.loop(0, 5)
    def _(m):
        drain(far_copy(m))

    for p in range(PARTS):
        drain(hop_copy(0, 0, p))

        @pl.when(a == 0)
        def _():
            drain(hop_copy(0, 1, p))

        for q in range(2):
            drain(hop_copy(1, q, p))
        for where in fan:
            drain(gather_copy(p, *where))
        for dx in range(1, 4):
            for dc in range(2):
                drain((pass_x if p % 2 else pass_y)(p, dx, dc))
    for dz in range(1, 8):
        drain(topic_z(dz))
    for dx in range(1, 4):
        drain(topic_x(dx))
    for where in plane:
        drain(topic_p(*where))


def exchange(counts, tile_live, lengths, doc_mix, word_topic, topic_total):
    vmem = pl.BlockSpec(memory_space=pltpu.VMEM)
    hbm = pl.BlockSpec(memory_space=pltpu.HBM)
    smem = pl.BlockSpec(memory_space=pltpu.SMEM)
    dma = pltpu.SemaphoreType.DMA
    return pl.pallas_call(
        kernel,
        name="window",
        out_shape=(
            pltpu.VMEM((DOCS, K), BF16),
            pltpu.VMEM((WB, K), F32),
            jax.ShapeDtypeStruct((1, K), F32),
        ),
        in_specs=[hbm, smem, vmem, hbm, hbm, vmem],
        out_specs=(vmem, vmem, vmem),
        scratch_shapes=[
            pltpu.VMEM((DOCS, SPAN * WB), jnp.int32),
            pltpu.VMEM((DOCS, K), BF16),
            pltpu.VMEM((WB, K), F32),
            pltpu.VMEM((1, K), F32),
            pltpu.VMEM((DOCS, 1), F32),
            pltpu.VMEM((SLOTS * WB, K), BF16),
            pltpu.VMEM((DOCS, K), BF16),
            pltpu.VMEM((DOCS, 1), F32),
            pltpu.VMEM((8 * DOCS, KD), BF16),
            pltpu.VMEM((DOCS, SPAN * WB), BF16),
            pltpu.VMEM((SPAN + 1, WB, 8 * DOCS), BF16),
            pltpu.VMEM((SPAN + 1, 2, WB, KH), F32),
            pltpu.VMEM((2, 4, WB, KH), F32),
            pltpu.VMEM((5, WB, KH), F32),
            pltpu.VMEM((6, WB, KH), F32),
            pltpu.VMEM((2, WB, KH), F32),
            pltpu.VMEM((2, WB, KH), F32),
            pltpu.VMEM((WB, K), F32),
            pltpu.VMEM((DOCS, WB), F32),
            pltpu.VMEM((1, K), F32),
            pltpu.VMEM((8, 1, K), F32),
            pltpu.VMEM((4, 1, K), F32),
            pltpu.VMEM((8, 1, K), F32),
            dma((3, CH, 5)),
            dma((SLOTS, CH)),
            dma((4, 2)),
            dma((8,)),
            dma((SPAN, 4)),
            dma((SPAN, 3)),
            dma((8, SPAN)),
            dma((4, 2)),
            dma((2, 4)),
            dma((5,)),
            dma((5,)),
            dma((2, 2, PARTS)),
            dma((2, 2, PARTS)),
            dma((PARTS, 4, 2, 2)),
            dma((PARTS, 3, 2)),
            dma((PARTS, 8, 2)),
            dma((3, 8)),
            dma((8,)),
            dma((4,)),
            dma((8,)),
            dma((CH + 2,)),
        ],
        compiler_params=pltpu.CompilerParams(
            collective_id=0, has_side_effects=True, vmem_limit_bytes=62820000
        ),
    )(counts, tile_live, lengths, doc_mix, word_topic, topic_total)


def local(counts, tile_live, doc_lengths, doc_mix, word_topic, topic_total):
    doc_share, topic_new, topic_mean = exchange(
        counts, tile_live, doc_lengths[None, :], doc_mix, word_topic, topic_total[None, :]
    )
    return (doc_share, topic_new, topic_mean[0])


def solution(mesh):
    return jax.shard_map(
        local,
        mesh=mesh,
        in_specs=(
            P(("grp", "blk"), None),
            P(("grp", "blk"), None),
            P(("grp", "blk")),
            P(("grp", "blk"), None),
            P("blk", None),
            P(),
        ),
        out_specs=(P(("grp", "blk"), None), P("blk", None), P()),
        check_vma=False,
    )
```

```python
import jax
import jax.numpy as jnp
from jax import lax
from jax.experimental import pallas as pl
from jax.experimental.pallas import tpu as pltpu
from jax.sharding import PartitionSpec as P

VOCAB = 262144

alpha_prior = 0.1
beta_prior = 0.01

MESH = pl.DeviceIdType.MESH
F32 = jnp.float32
BF16 = jnp.bfloat16

DOCS = 256
WB = 128
K = 4096
SPAN = 8
SLOTS = 11
CH = 4
ROWS = WB // CH
KD = K // 8
KH = KD // 2
PARTS = 4


RELAYS = ({8: 0, 9: 2, 10: 4, 11: 6, 15: 8, 16: 9, 17: 10}, {8: 1, 9: 3, 10: 5, 11: 7})
PRODUCTS = ({9: 0, 10: 2, 11: 4, 13: 6, 16: 8, 17: 9, 18: 10}, {9: 1, 10: 3, 11: 5, 14: 7})


def pick(t, table):
    e = jnp.int32(-1)
    for step, place_ in table.items():
        e = jnp.where(t == step, place_, e)
    return e


def place(x, h, z, a, c):
    return {"grp": x * 2 + h, "blk": (z * 2 + a) * 2 + c}


def kernel(
    counts_in,
    live,
    lengths,
    mix_in,
    topic_in,
    total,
    share_out,
    topic_out,
    mean,
    counts,
    mix,
    topic,
    inverse,
    span,
    words,
    doc_low,
    scale,
    docs,
    ratio,
    ratio_t,
    part,
    near,
    far,
    acc,
    hop1,
    hop2,
    gathered,
    wlen,
    column,
    col_z,
    col_x,
    col_p,
    send_w,
    recv_w,
    send_d,
    recv_d,
    send_r,
    send_rf,
    recv_r,
    send_n,
    recv_n,
    send_f,
    recv_f,
    send_z,
    recv_z,
    send_g,
    send_p,
    recv_g,
    send_t,
    recv_tz,
    recv_tx,
    recv_tp,
    load,
):
    grp = lax.axis_index("grp")
    blk = lax.axis_index("blk")
    x = lax.div(grp, 2)
    h = lax.rem(grp, 2)
    z = lax.div(blk, 4)
    i = lax.rem(blk, 4)
    a = lax.div(i, 2)
    c = lax.rem(i, 2)
    i2 = 2 * (1 - a) + c

    def xo(dx):
        return lax.rem(x + dx, 4)

    def zo(dz):
        return lax.rem(z + dz + 8, 8)

    def ho(dh):
        return lax.rem(h + dh, 2)

    def ao(da):
        return lax.rem(a + da, 2)

    def co(dc):
        return lax.rem(c + dc, 2)

    def remote(src, dst, send, recv, x_=x, h_=h, z_=z, a_=a, c_=c):
        return pltpu.make_async_remote_copy(
            src_ref=src,
            dst_ref=dst,
            send_sem=send,
            recv_sem=recv,
            device_id=place(x_, h_, z_, a_, c_),
            device_id_type=MESH,
        )

    def topic_load(r):
        rows = pl.ds(pl.multiple_of(r * ROWS, ROWS), ROWS)
        return pltpu.make_async_copy(topic_in.at[rows, :], topic.at[rows, :], load.at[r])

    mix_load = pltpu.make_async_copy(mix_in, mix, load.at[CH])
    counts_load = pltpu.make_async_copy(counts_in, counts, load.at[CH + 1])
    for u in range(CH):
        topic_load(lax.rem(u + 2 * h, CH)).start()
    mix_load.start()
    counts_load.start()

    barrier = pltpu.get_barrier_semaphore()
    greeted = 0

    def greet(**where):
        at = dict(x=x, h=h, z=z, a=a, c=c)
        at.update(where)
        pl.semaphore_signal(barrier, inc=1, device_id=place(**at), device_id_type=MESH)

    for dz in range(1, 8):
        greet(z=zo(dz))
        greeted += 1
    for dh in range(2):
        for da in range(2):
            for dc in range(2):
                if dh + da + dc:
                    greet(h=ho(dh), a=ao(da), c=co(dc))
                    greeted += 1
    for dx in range(1, 4):
        for dh in range(2):
            for dc in range(2):
                greet(x=xo(dx), h=ho(dh), c=co(dc))
                greeted += 1

    def chunk(slot, r):
        return words.at[pl.ds(pl.multiple_of(slot * WB + r * ROWS, ROWS), ROWS), :]

    def to_z(j, r):
        slot = 4 * j + i
        return remote(chunk(slot, r), chunk(slot + 4, r), send_w.at[j, r, 0], recv_w.at[slot + 4, r], z_=zo(-1))

    def to_partner(j, r):
        slot = 4 * j + i
        return remote(chunk(slot, r), chunk(slot, r), send_w.at[j, r, 1], recv_w.at[slot, r], c_=1 - c)

    def to_y(j, r):
        slot = 4 * j + i
        return remote(
            chunk(slot, r), chunk(slot, r), send_w.at[j, r, 2], recv_w.at[slot, r], h_=lax.rem(r + h, 2), a_=1 - a
        )

    def to_other_y(r):
        slot = 8 + i
        return remote(
            chunk(slot, r), chunk(slot, r), send_w.at[2, r, 4], recv_w.at[slot, r], h_=lax.rem(r + h + 1, 2), a_=1 - a
        )

    def to_far(r):
        slot = 8 + i
        return remote(
            chunk(slot, r), chunk(slot, r), send_w.at[2, r, 0], recv_w.at[slot, r], h_=1 - h, c_=1 - c
        )

    def relay(j, r):
        slot = 4 * j + i2
        return remote(chunk(slot, r), chunk(slot, r), send_w.at[j, r, 3], recv_w.at[slot, r], c_=1 - c)

    def arrived(slot, r):
        return pltpu.make_async_copy(chunk(slot, r), chunk(slot, r), recv_w.at[slot, r])

    def mine(r):
        return lax.div(r, CH // 2) == h

    def column_copies(j, r, act):
        if j == 0:
            act(to_z(j, r))
        elif j == 1:
            @pl.when(jnp.logical_and(i <= 2, mine(r)))
            def _():
                act(to_z(j, r))
        else:
            @pl.when(c == 0)
            def _():
                act(to_far(r))

            @pl.when(a == 0)
            def _():
                act(to_other_y(r))
        if j == 1:
            act(to_partner(j, r))
            act(to_y(j, r))
        else:
            @pl.when(c == (1 if j == 0 else 0))
            def _():
                act(to_partner(j, r))

            @pl.when(a == (1 if j == 0 else 0))
            def _():
                act(to_y(j, r))

    start = lambda copy: copy.start()
    drain = lambda copy: copy.wait_send()

    inverse[...] = 1.0 / (total[...] + beta_prior * VOCAB)
    span[...] = jnp.broadcast_to(lengths[...].astype(F32), (8, DOCS)).T[:, :1]

    def turn(u):
        return lax.rem(u + 2 * h, CH)

    @pl.loop(0, CH)
    def _(u):
        r = turn(u)
        rows = pl.ds(pl.multiple_of(r * ROWS, ROWS), ROWS)
        own = pl.ds(pl.multiple_of(i * WB + r * ROWS, ROWS), ROWS)
        topic_load(r).wait()
        weight = (topic[rows, :] + beta_prior) * inverse[...]
        topic[rows, :] = weight
        words[own, :] = weight.astype(BF16)

        @pl.when(u == 0)
        def _():
            pl.semaphore_wait(barrier, greeted)

        @pl.when(u > 0)
        def _():
            column_copies(0, turn(u - 1), start)

    own_docs = 2 * x + c
    mix_load.wait()

    @pl.loop(0, DOCS // 32)
    def _(n):
        rows = pl.ds(pl.multiple_of(n * 32, 32), 32)
        wide = mix[rows, :].astype(F32)
        factor = span[rows, :] / jnp.sum(wide, axis=1, keepdims=True)
        scale[rows, :] = factor
        doc_low[rows, :] = (wide * factor + alpha_prior).astype(BF16)

        @pl.when(n == 0)
        def _():
            column_copies(0, turn(CH - 1), start)

    def doc_rows(q):
        return pl.ds(pl.multiple_of(q * DOCS, DOCS), DOCS)

    def topics(q):
        return pl.ds(pl.multiple_of(q * KD, KD), KD)

    def doc_copy(dx, dc):
        to = 2 * xo(dx) + co(dc)
        return remote(
            doc_low.at[:, topics(to)],
            docs.at[doc_rows(own_docs), :],
            send_d.at[dx, dc],
            recv_d.at[own_docs],
            x_=xo(dx),
            c_=co(dc),
        )

    others = [(dx, dc) for dx in range(4) for dc in range(2) if dx + dc]
    wlen[...] = jnp.zeros_like(wlen)
    for q in range(4):
        ratio_t[SPAN, :, 2 * q * DOCS : (2 * q + 1) * DOCS] = jnp.zeros((WB, DOCS), BF16)
        ratio_t[0, :, (2 * q + 1) * DOCS : (2 * q + 2) * DOCS] = jnp.zeros((WB, DOCS), BF16)

    def ratio_at(q, k):
        return ratio_t.at[k + lax.rem(q, 2), :, doc_rows(q)]

    def ratio_out(k, dx):
        return remote(
            ratio_at(own_docs, k), ratio_at(own_docs, k), send_r.at[k, dx], recv_r.at[own_docs, k], x_=xo(dx)
        )

    def ratio_over(k):
        return remote(
            ratio_at(own_docs, k), ratio_at(own_docs, k), send_r.at[k, 0], recv_r.at[own_docs, k], c_=1 - c
        )

    def ratio_relay(k, dx):
        q = 2 * xo(dx) + c
        return remote(ratio_at(q, k), ratio_at(q, k), send_rf.at[k, dx - 1], recv_r.at[q, k], c_=1 - c)

    def ratio_arrived(q, k):
        return pltpu.make_async_copy(ratio_at(q, k), ratio_at(q, k), recv_r.at[q, k])

    def meet(slot):
        k = slot - i
        block = words[pl.ds(pl.multiple_of(slot * WB, WB), WB), :]
        normalizer = lax.dot_general(
            doc_low[...], block, (((1,), (1,)), ((), ())), preferred_element_type=F32
        )
        at = pl.ds(pl.multiple_of(k * WB, WB), WB)
        half = DOCS // 2
        top = live[0, k].astype(F32)
        low = live[1, k].astype(F32)
        mask = jnp.where(lax.broadcasted_iota(jnp.int32, (DOCS, WB), 0) < half, top, low)
        kept = counts[:, at].astype(F32) * mask
        wide = kept / normalizer
        ratio_t[k + c, :, doc_rows(own_docs)] = wide.T.astype(BF16)
        ratio[:, at] = wide.astype(BF16)
        wlen[...] += kept
        for dx in range(1, 4):
            ratio_out(k, dx).start()
        ratio_over(k).start()

    def relay_ratio(k):
        for dx in range(1, 4):
            ratio_arrived(2 * xo(dx) + c, k).wait()
            ratio_relay(k, dx).start()

    def half_rows(w):
        return slice(w * WB // 2, (w + 1) * WB // 2)

    def near_copy(m, side, w):
        n = m + 2 + 2 * lax.div(m, 2)
        return remote(
            part.at[n, side, half_rows(w), :],
            near.at[h, m, half_rows(w), :],
            send_n.at[m, side, w],
            recv_n.at[h, m, w],
            h_=side,
            a_=1 - a,
        )

    def far_copy(m, w):
        n = m + 2 * lax.div(m, 2)
        return remote(
            part.at[n, 1 - h, half_rows(w), :], far.at[m, half_rows(w), :], send_f.at[m, w], recv_f.at[m, w], h_=1 - h
        )

    def products(n):
        @pl.when(n == 0)
        def _():
            for dx, dc in others:
                q = 2 * xo(dx) + co(dc)
                pltpu.make_async_copy(docs.at[doc_rows(q), :], docs.at[doc_rows(q), :], recv_d.at[q]).wait()

        k = n - (1 - c)

        @pl.when(jnp.logical_and(k >= 0, k < SPAN))
        def _():
            for dx in range(4):
                ratio_arrived(2 * xo(dx) + (1 - c), k).wait()

        made = jnp.dot(ratio_t[n], docs[...], preferred_element_type=F32)
        part[n, 0] = made[:, :KH]
        part[n, 1] = made[:, KH:]
        m = n - 2 * lax.div(n, 4)

        @pl.when(lax.rem(lax.div(n, 2), 2) == 1)
        def _():
            for side in range(2):
                near_copy(m - 2, side, 0).start()

        @pl.when(lax.rem(lax.div(n, 2), 2) == 0)
        def _():
            far_copy(m, 0).start()

    def topic_z(dz):
        return remote(column, col_z.at[z], send_t.at[0, dz], recv_tz.at[z], z_=zo(dz))

    def own_results():
        length = jnp.sum(wlen[...], axis=1, keepdims=True)
        under = 1.0 / (length + K * alpha_prior)

        @pl.loop(0, K // 512)
        def _(n):
            at = pl.ds(pl.multiple_of(n * 512, 512), 512)
            proj = jnp.dot(
                ratio[...],
                words[pl.ds(pl.multiple_of(i * WB, WB), SPAN * WB), at],
                preferred_element_type=F32,
            )
            weight = mix[:, at].astype(F32) * scale[...] + alpha_prior
            new = weight * proj
            column[:, at] = jnp.sum(new, axis=0, keepdims=True)
            share_out[:, at] = (K * (new + alpha_prior) * under).astype(BF16)

        col_z[z] = column[...]
        for dz in range(1, 8):
            topic_z(dz).start()

    counts_load.wait()
    meet(i)
    docs[doc_rows(own_docs), :] = doc_low[:, topics(own_docs)]
    for dx, dc in others:
        doc_copy(dx, dc).start()

    def slot_at(e):
        return jnp.where(jnp.logical_and(e >= 4, e < 8), 4 + lax.rem(e + 2 * a, 4), e)

    @pl.loop(1, 19)
    def _(t):
        @pl.when(t <= 4)
        def _():
            r = turn(t - 1)
            arrived(4 + i, r).wait()
            column_copies(1, r, start)

        @pl.when(jnp.logical_and(t == 2, a == 0))
        def _():
            for u in range(CH):
                r = lax.rem(2 * h + CH - u, CH)
                arrived(i2, r).wait()
                relay(0, r).start()

        @pl.when(jnp.logical_and(jnp.logical_or(t == 7, t == 9), i <= 2))
        def _():
            r = 2 * h + lax.div(t - 7, 2)
            arrived(8 + i, r).wait()
            column_copies(2, r, start)

        @pl.when(jnp.logical_or(jnp.logical_and(t >= 2, t <= 4), t == 7))
        def _():
            r = lax.rem(2 * h + CH + 2 - jnp.minimum(t, 5), CH)
            arrived(4 + i2, r).wait()
            relay(1, r).start()

        @pl.when(jnp.logical_and(jnp.logical_or(t == 10, t == 12), a == 1))
        def _():
            for u in range(2):
                r = lax.div(t - 10, 2) + 2 * u
                arrived(8 + i2, r).wait()
                relay(2, r).start()

        @pl.when(jnp.logical_or(t <= 8, jnp.logical_and(t >= 12, t <= 14)))
        def _():
            slot = slot_at(jnp.where(t <= 8, t - 1, t - 4))
            column_of = lax.rem(slot, 4)

            @pl.when(jnp.logical_and(slot > i, slot < i + SPAN))
            def _():
                @pl.when(jnp.logical_and(column_of != i, column_of != i2))
                def _():
                    for r in range(CH):
                        arrived(slot, r).wait()

                meet(slot)

        for table in PRODUCTS:
            e = pick(t, table)
            ready = slot_at(e) - 2 * a

            @pl.when(jnp.logical_and(e >= 0, jnp.logical_and(ready >= 0, ready <= SPAN)))
            def _():
                products(ready)

        for table in RELAYS:
            e = pick(t, table)
            slot = slot_at(e)

            @pl.when(jnp.logical_and(e >= 0, jnp.logical_and(slot >= i, slot < i + SPAN)))
            def _():
                relay_ratio(slot - i)

        @pl.when(t == 14)
        def _():
            own_results()

    @pl.loop(0, 4)
    def _(m):
        for side in range(2):
            near_copy(3 - m, side, 1).start()

    @pl.loop(0, 5)
    def _(m):
        far_copy(4 - m, 1).start()

    def wait_far(m, w):
        at = far.at[m, half_rows(w), :]
        pltpu.make_async_copy(at, at, recv_f.at[m, w]).wait()

    def wait_near(m, w):
        for side in range(2):
            at = near.at[side, m, half_rows(w), :]
            pltpu.make_async_copy(at, at, recv_n.at[side, m, w]).wait()

    def part_rows(p):
        return slice(p * WB // PARTS, (p + 1) * WB // PARTS)

    def hop_copy(stage, q, p):
        source, target = ((4, hop1), (2, hop2))[stage]
        return remote(
            acc.at[source + q, part_rows(p), :],
            target.at[q, part_rows(p), :],
            send_z.at[stage, q, p],
            recv_z.at[stage, q, p],
            z_=zo(1),
        )

    def hop_arrived(stage, q, p):
        at = (hop1, hop2)[stage].at[q, part_rows(p), :]
        return pltpu.make_async_copy(at, at, recv_z.at[stage, q, p])

    def sums_over_y(w):
        rows = half_rows(w)
        parts = range(w * PARTS // 2, (w + 1) * PARTS // 2)
        for q in (0, 1):
            wait_far(q, w)
            acc[q, rows] = part[q, h, rows] + far[q, rows]

            @pl.when(a == 1)
            def _():
                wait_near(q, w)
                acc[q, rows] += near[0, q, rows] + near[1, q, rows]

        wait_far(4, w)
        acc[4, rows] = part[8, h, rows] + far[4, rows]

        @pl.when(a == 0)
        def _():
            for m in (2, 3):
                wait_near(m, w)
            acc[4, rows] += near[0, 2, rows] + near[1, 2, rows]
            acc[5, rows] = near[0, 3, rows] + near[1, 3, rows]
            for p in parts:
                hop_copy(0, 1, p).start()

        for p in parts:
            hop_copy(0, 0, p).start()
        for q in (2, 3):
            wait_far(q, w)
            m = q - 2 + 2 * a
            wait_near(m, w)
            acc[q, rows] = part[(4, 5)[q - 2], h, rows] + far[q, rows] + near[0, m, rows] + near[1, m, rows]

    def hop_on(p):
        rows = part_rows(p)
        hop_arrived(0, 0, p).wait()
        acc[2, rows] += hop1[0, rows]

        @pl.when(a == 0)
        def _():
            hop_arrived(0, 1, p).wait()
            acc[3, rows] += hop1[1, rows]

        for q in range(2):
            hop_copy(1, q, p).start()

    first, second = range(PARTS // 2), range(PARTS // 2, PARTS)
    sums_over_y(0)
    for p in first:
        hop_on(p)

    for dz in range(1, 8):
        q = zo(dz)
        pltpu.make_async_copy(col_z.at[q], col_z.at[q], recv_tz.at[q]).wait()
    column_z = col_z[0]
    for q in range(1, 8):
        column_z += col_z[q]
    col_x[x] = column_z

    def topic_x(dx):
        return remote(col_x.at[x], col_x.at[x], send_t.at[1, dx], recv_tx.at[x], x_=xo(dx))

    for dx in range(1, 4):
        topic_x(dx).start()

    def piece(q, h_):
        return pl.ds(pl.multiple_of(q * KD + h_ * KH, KH), KH)

    def gather_copy(p, dx, dh, dc):
        return remote(
            acc.at[co(dc), part_rows(p), :],
            gathered.at[part_rows(p), piece(own_docs, h)],
            send_g.at[p, dx, dh, dc],
            recv_g.at[p, own_docs, h],
            x_=xo(dx),
            h_=ho(dh),
            c_=co(dc),
        )

    def gather_arrived(p, q, h_):
        at = gathered.at[part_rows(p), piece(q, h_)]
        return pltpu.make_async_copy(at, at, recv_g.at[p, q, h_])

    def pass_y(p, dx, dc):
        q = 2 * xo(dx) + dc
        at = gathered.at[part_rows(p), piece(q, h)]
        return remote(at, at, send_p.at[p, dx - 1, dc], recv_g.at[p, q, h], h_=1 - h)

    def pass_x(p, dx, dc):
        q = 2 * x + dc
        at = gathered.at[part_rows(p), piece(q, 1 - h)]
        return remote(at, at, send_p.at[p, dx - 1, dc], recv_g.at[p, q, 1 - h], x_=xo(dx))

    fan = [(0, 1, 0), (0, 1, 1), (2, 0, 0), (2, 0, 1), (1, 0, 0), (1, 0, 1), (3, 0, 0), (3, 0, 1), (0, 0, 1)]

    def spread(p):
        rows = part_rows(p)
        for q in range(2):
            hop_arrived(1, q, p).wait()
            acc[q, rows] += hop2[q, rows]
        gathered[rows, piece(own_docs, h)] = acc[c, rows]
        for where in fan:
            gather_copy(p, *where).start()

    def pass_on(p):
        if p % 2 == 0:
            for dx in (1, 3, 2):
                for dc in range(2):
                    gather_arrived(p, 2 * xo(dx) + dc, h).wait()
                    pass_y(p, dx, dc).start()
        else:
            for dc in range(2):
                gather_arrived(p, 2 * x + dc, 1 - h).wait()
                for dx in (2, 1, 3):
                    pass_x(p, dx, dc).start()

    for p in first:
        spread(p)
    sums_over_y(1)
    pass_on(0)
    for p in second:
        hop_on(p)
    for p in first[1:]:
        pass_on(p)
    for p in second:
        spread(p)
    for p in second:
        pass_on(p)

    for dx in range(1, 4):
        q = xo(dx)
        pltpu.make_async_copy(col_x.at[q], col_x.at[q], recv_tx.at[q]).wait()
    column_x = col_x[0]
    for q in range(1, 4):
        column_x += col_x[q]
    me = h * 4 + i
    col_p[me] = column_x

    def topic_p(dh, da, dc):
        return remote(
            col_p.at[me],
            col_p.at[me],
            send_t.at[2, 4 * dh + 2 * da + dc],
            recv_tp.at[me],
            h_=ho(dh),
            a_=ao(da),
            c_=co(dc),
        )

    plane = [(dh, da, dc) for dh in range(2) for da in range(2) for dc in range(2) if dh + da + dc]
    for where in plane:
        topic_p(*where).start()

    for dh, da, dc in plane:
        q = 4 * ho(dh) + 2 * ao(da) + co(dc)
        pltpu.make_async_copy(col_p.at[q], col_p.at[q], recv_tp.at[q]).wait()
    column_p = col_p[0]
    for q in range(1, 8):
        column_p += col_p[q]
    mean[...] = column_p * (1.0 / (WB * 32))

    for p in range(PARTS):
        rows = part_rows(p)
        gather_arrived(p, 2 * x + 1 - c, h).wait()
        for dc in range(2):
            if p % 2 == 0:
                gather_arrived(p, 2 * x + dc, 1 - h).wait()
            for dx in range(1, 4):
                if p % 2 == 1:
                    gather_arrived(p, 2 * xo(dx) + dc, h).wait()
                gather_arrived(p, 2 * xo(dx) + dc, 1 - h).wait()
        topic_out[rows, :] = gathered[rows, :] * topic[rows, :]

    @pl.loop(0, CH)
    def _(r):
        column_copies(0, r, drain)
        column_copies(1, r, drain)

        @pl.when(jnp.logical_and(i <= 2, mine(r)))
        def _():
            column_copies(2, r, drain)

        @pl.when(a == 0)
        def _():
            drain(relay(0, r))

        drain(relay(1, r))

        @pl.when(a == 1)
        def _():
            drain(relay(2, r))

    for dx, dc in others:
        drain(doc_copy(dx, dc))

    @pl.loop(0, SPAN)
    def _(k):
        for dx in range(1, 4):
            drain(ratio_out(k, dx))
            drain(ratio_relay(k, dx))
        drain(ratio_over(k))

    @pl.loop(0, 4)
    def _(m):
        for side in range(2):
            for w in range(2):
                drain(near_copy(m, side, w))

    @pl.loop(0, 5)
    def _(m):
        for w in range(2):
            drain(far_copy(m, w))

    for p in range(PARTS):
        drain(hop_copy(0, 0, p))

        @pl.when(a == 0)
        def _():
            drain(hop_copy(0, 1, p))

        for q in range(2):
            drain(hop_copy(1, q, p))
        for where in fan:
            drain(gather_copy(p, *where))
        for dx in range(1, 4):
            for dc in range(2):
                drain((pass_x if p % 2 else pass_y)(p, dx, dc))
    for dz in range(1, 8):
        drain(topic_z(dz))
    for dx in range(1, 4):
        drain(topic_x(dx))
    for where in plane:
        drain(topic_p(*where))


def exchange(counts, tile_live, lengths, doc_mix, word_topic, topic_total):
    vmem = pl.BlockSpec(memory_space=pltpu.VMEM)
    hbm = pl.BlockSpec(memory_space=pltpu.HBM)
    smem = pl.BlockSpec(memory_space=pltpu.SMEM)
    dma = pltpu.SemaphoreType.DMA
    return pl.pallas_call(
        kernel,
        name="window",
        out_shape=(
            pltpu.VMEM((DOCS, K), BF16),
            pltpu.VMEM((WB, K), F32),
            jax.ShapeDtypeStruct((1, K), F32),
        ),
        in_specs=[hbm, smem, vmem, hbm, hbm, vmem],
        out_specs=(vmem, vmem, vmem),
        scratch_shapes=[
            pltpu.VMEM((DOCS, SPAN * WB), jnp.int32),
            pltpu.VMEM((DOCS, K), BF16),
            pltpu.VMEM((WB, K), F32),
            pltpu.VMEM((1, K), F32),
            pltpu.VMEM((DOCS, 1), F32),
            pltpu.VMEM((SLOTS * WB, K), BF16),
            pltpu.VMEM((DOCS, K), BF16),
            pltpu.VMEM((DOCS, 1), F32),
            pltpu.VMEM((8 * DOCS, KD), BF16),
            pltpu.VMEM((DOCS, SPAN * WB), BF16),
            pltpu.VMEM((SPAN + 1, WB, 8 * DOCS), BF16),
            pltpu.VMEM((SPAN + 1, 2, WB, KH), F32),
            pltpu.VMEM((2, 4, WB, KH), F32),
            pltpu.VMEM((5, WB, KH), F32),
            pltpu.VMEM((6, WB, KH), F32),
            pltpu.VMEM((2, WB, KH), F32),
            pltpu.VMEM((2, WB, KH), F32),
            pltpu.VMEM((WB, K), F32),
            pltpu.VMEM((DOCS, WB), F32),
            pltpu.VMEM((1, K), F32),
            pltpu.VMEM((8, 1, K), F32),
            pltpu.VMEM((4, 1, K), F32),
            pltpu.VMEM((8, 1, K), F32),
            dma((3, CH, 5)),
            dma((SLOTS, CH)),
            dma((4, 2)),
            dma((8,)),
            dma((SPAN, 4)),
            dma((SPAN, 3)),
            dma((8, SPAN)),
            dma((4, 2, 2)),
            dma((2, 4, 2)),
            dma((5, 2)),
            dma((5, 2)),
            dma((2, 2, PARTS)),
            dma((2, 2, PARTS)),
            dma((PARTS, 4, 2, 2)),
            dma((PARTS, 3, 2)),
            dma((PARTS, 8, 2)),
            dma((3, 8)),
            dma((8,)),
            dma((4,)),
            dma((8,)),
            dma((CH + 2,)),
        ],
        compiler_params=pltpu.CompilerParams(
            collective_id=0, has_side_effects=True, vmem_limit_bytes=62820000
        ),
    )(counts, tile_live, lengths, doc_mix, word_topic, topic_total)


def local(counts, tile_live, doc_lengths, doc_mix, word_topic, topic_total):
    doc_share, topic_new, topic_mean = exchange(
        counts, tile_live, doc_lengths[None, :], doc_mix, word_topic, topic_total[None, :]
    )
    return (doc_share, topic_new, topic_mean[0])


def solution(mesh):
    return jax.shard_map(
        local,
        mesh=mesh,
        in_specs=(
            P(("grp", "blk"), None),
            P(("grp", "blk"), None),
            P(("grp", "blk")),
            P(("grp", "blk"), None),
            P("blk", None),
            P(),
        ),
        out_specs=(P(("grp", "blk"), None), P("blk", None), P()),
        check_vma=False,
    )
```

```python
import jax
import jax.numpy as jnp
from jax import lax
from jax.experimental import pallas as pl
from jax.experimental.pallas import tpu as pltpu
from jax.sharding import PartitionSpec as P

VOCAB = 262144

alpha_prior = 0.1
beta_prior = 0.01

MESH = pl.DeviceIdType.MESH
F32 = jnp.float32
BF16 = jnp.bfloat16

DOCS = 256
WB = 128
K = 4096
SPAN = 8
SLOTS = 11
CH = 4
ROWS = WB // CH
KD = K // 8
KH = KD // 2
PARTS = 4


RELAYS = ({8: 0, 9: 2, 10: 4, 11: 6, 15: 8, 16: 9, 17: 10}, {8: 1, 9: 3, 10: 5, 11: 7})
PRODUCTS = ({9: 0, 10: 2, 11: 4, 13: 6, 16: 8, 17: 9, 18: 10}, {9: 1, 10: 3, 11: 5, 14: 7})


def pick(t, table):
    e = jnp.int32(-1)
    for step, place_ in table.items():
        e = jnp.where(t == step, place_, e)
    return e


def place(x, h, z, a, c):
    return {"grp": x * 2 + h, "blk": (z * 2 + a) * 2 + c}


def kernel(
    counts_in,
    live,
    lengths,
    mix_in,
    topic_in,
    total,
    share_out,
    topic_out,
    mean,
    counts,
    mix,
    topic,
    inverse,
    span,
    words,
    doc_low,
    scale,
    docs,
    ratio,
    ratio_t,
    part,
    near,
    far,
    acc,
    hop1,
    hop2,
    gathered,
    wlen,
    column,
    col_z,
    col_x,
    col_p,
    send_w,
    recv_w,
    send_d,
    recv_d,
    send_r,
    send_rf,
    recv_r,
    send_n,
    recv_n,
    send_f,
    recv_f,
    send_z,
    recv_z,
    send_g,
    send_p,
    recv_g,
    send_t,
    recv_tz,
    recv_tx,
    recv_tp,
    load,
):
    grp = lax.axis_index("grp")
    blk = lax.axis_index("blk")
    x = lax.div(grp, 2)
    h = lax.rem(grp, 2)
    z = lax.div(blk, 4)
    i = lax.rem(blk, 4)
    a = lax.div(i, 2)
    c = lax.rem(i, 2)
    i2 = 2 * (1 - a) + c

    def xo(dx):
        return lax.rem(x + dx, 4)

    def zo(dz):
        return lax.rem(z + dz + 8, 8)

    def ho(dh):
        return lax.rem(h + dh, 2)

    def ao(da):
        return lax.rem(a + da, 2)

    def co(dc):
        return lax.rem(c + dc, 2)

    def remote(src, dst, send, recv, x_=x, h_=h, z_=z, a_=a, c_=c):
        return pltpu.make_async_remote_copy(
            src_ref=src,
            dst_ref=dst,
            send_sem=send,
            recv_sem=recv,
            device_id=place(x_, h_, z_, a_, c_),
            device_id_type=MESH,
        )

    def topic_load(r):
        rows = pl.ds(pl.multiple_of(r * ROWS, ROWS), ROWS)
        return pltpu.make_async_copy(topic_in.at[rows, :], topic.at[rows, :], load.at[r])

    mix_load = pltpu.make_async_copy(mix_in, mix, load.at[CH])
    counts_load = pltpu.make_async_copy(counts_in, counts, load.at[CH + 1])
    for u in range(CH):
        topic_load(lax.rem(u + 2 * h, CH)).start()
    mix_load.start()
    counts_load.start()

    barrier = pltpu.get_barrier_semaphore()
    greeted = 0

    def greet(**where):
        at = dict(x=x, h=h, z=z, a=a, c=c)
        at.update(where)
        pl.semaphore_signal(barrier, inc=1, device_id=place(**at), device_id_type=MESH)

    for dz in range(1, 8):
        greet(z=zo(dz))
        greeted += 1
    for dh in range(2):
        for da in range(2):
            for dc in range(2):
                if dh + da + dc:
                    greet(h=ho(dh), a=ao(da), c=co(dc))
                    greeted += 1
    for dx in range(1, 4):
        for dh in range(2):
            for dc in range(2):
                greet(x=xo(dx), h=ho(dh), c=co(dc))
                greeted += 1

    def chunk(slot, r):
        return words.at[pl.ds(pl.multiple_of(slot * WB + r * ROWS, ROWS), ROWS), :]

    def turn(u):
        return lax.rem(u + 2 * h, CH)

    def to_z(j, r):
        slot = 4 * j + i
        return remote(chunk(slot, r), chunk(slot + 4, r), send_w.at[j, r, 0], recv_w.at[slot + 4, r], z_=zo(-1))

    def to_partner(j, r):
        slot = 4 * j + i
        return remote(chunk(slot, r), chunk(slot, r), send_w.at[j, r, 1], recv_w.at[slot, r], c_=1 - c)

    def to_y(j, r):
        slot = 4 * j + i
        return remote(
            chunk(slot, r), chunk(slot, r), send_w.at[j, r, 2], recv_w.at[slot, r], h_=lax.rem(r + h, 2), a_=1 - a
        )

    def to_other_y(r):
        slot = 8 + i
        return remote(
            chunk(slot, r), chunk(slot, r), send_w.at[2, r, 4], recv_w.at[slot, r], h_=lax.rem(r + h + 1, 2), a_=1 - a
        )

    def to_far(r):
        slot = 8 + i
        return remote(
            chunk(slot, r), chunk(slot, r), send_w.at[2, r, 0], recv_w.at[slot, r], h_=1 - h, c_=1 - c
        )

    def relay(j, r):
        slot = 4 * j + i2
        return remote(chunk(slot, r), chunk(slot, r), send_w.at[j, r, 3], recv_w.at[slot, r], c_=1 - c)

    def arrived(slot, r):
        return pltpu.make_async_copy(chunk(slot, r), chunk(slot, r), recv_w.at[slot, r])

    def swap(r):
        slot = 4 + i
        return remote(chunk(slot, r), chunk(slot, r), send_w.at[1, r, 4], recv_w.at[slot, r], h_=1 - h)

    def mine(r):
        return lax.div(r, CH // 2) == h

    def column_copies(j, r, act):
        if j == 0:
            @pl.when(r != turn(CH - 1))
            def _():
                act(to_z(j, r))
        elif j == 1:
            @pl.when(r == turn(1))
            def _():
                act(swap(r))

            @pl.when(jnp.logical_and(i <= 2, mine(r)))
            def _():
                act(to_z(j, r))
        else:
            @pl.when(c == 0)
            def _():
                act(to_far(r))

            @pl.when(a == 0)
            def _():
                act(to_other_y(r))
        if j == 1:
            act(to_partner(j, r))
            act(to_y(j, r))
        else:
            @pl.when(c == (1 if j == 0 else 0))
            def _():
                act(to_partner(j, r))

            @pl.when(a == (1 if j == 0 else 0))
            def _():
                act(to_y(j, r))

    start = lambda copy: copy.start()
    drain = lambda copy: copy.wait_send()

    inverse[...] = 1.0 / (total[...] + beta_prior * VOCAB)
    span[...] = jnp.broadcast_to(lengths[...].astype(F32), (8, DOCS)).T[:, :1]

    @pl.loop(0, CH)
    def _(u):
        r = turn(u)
        rows = pl.ds(pl.multiple_of(r * ROWS, ROWS), ROWS)
        own = pl.ds(pl.multiple_of(i * WB + r * ROWS, ROWS), ROWS)
        topic_load(r).wait()
        weight = (topic[rows, :] + beta_prior) * inverse[...]
        topic[rows, :] = weight
        words[own, :] = weight.astype(BF16)

        @pl.when(u == 0)
        def _():
            pl.semaphore_wait(barrier, greeted)

        @pl.when(u > 0)
        def _():
            column_copies(0, turn(u - 1), start)

    own_docs = 2 * x + c
    mix_load.wait()

    @pl.loop(0, DOCS // 32)
    def _(n):
        rows = pl.ds(pl.multiple_of(n * 32, 32), 32)
        wide = mix[rows, :].astype(F32)
        factor = span[rows, :] / jnp.sum(wide, axis=1, keepdims=True)
        scale[rows, :] = factor
        doc_low[rows, :] = (wide * factor + alpha_prior).astype(BF16)

        @pl.when(n == 0)
        def _():
            column_copies(0, turn(CH - 1), start)

    def doc_rows(q):
        return pl.ds(pl.multiple_of(q * DOCS, DOCS), DOCS)

    def topics(q):
        return pl.ds(pl.multiple_of(q * KD, KD), KD)

    def doc_copy(dx, dc):
        to = 2 * xo(dx) + co(dc)
        return remote(
            doc_low.at[:, topics(to)],
            docs.at[doc_rows(own_docs), :],
            send_d.at[dx, dc],
            recv_d.at[own_docs],
            x_=xo(dx),
            c_=co(dc),
        )

    others = [(dx, dc) for dx in range(4) for dc in range(2) if dx + dc]
    wlen[...] = jnp.zeros_like(wlen)
    for q in range(4):
        ratio_t[SPAN, :, 2 * q * DOCS : (2 * q + 1) * DOCS] = jnp.zeros((WB, DOCS), BF16)
        ratio_t[0, :, (2 * q + 1) * DOCS : (2 * q + 2) * DOCS] = jnp.zeros((WB, DOCS), BF16)

    def ratio_at(q, k):
        return ratio_t.at[k + lax.rem(q, 2), :, doc_rows(q)]

    def ratio_out(k, dx):
        return remote(
            ratio_at(own_docs, k), ratio_at(own_docs, k), send_r.at[k, dx], recv_r.at[own_docs, k], x_=xo(dx)
        )

    def ratio_over(k):
        return remote(
            ratio_at(own_docs, k), ratio_at(own_docs, k), send_r.at[k, 0], recv_r.at[own_docs, k], c_=1 - c
        )

    def ratio_relay(k, dx):
        q = 2 * xo(dx) + c
        return remote(ratio_at(q, k), ratio_at(q, k), send_rf.at[k, dx - 1], recv_r.at[q, k], c_=1 - c)

    def ratio_arrived(q, k):
        return pltpu.make_async_copy(ratio_at(q, k), ratio_at(q, k), recv_r.at[q, k])

    def meet(slot):
        k = slot - i
        block = words[pl.ds(pl.multiple_of(slot * WB, WB), WB), :]
        normalizer = lax.dot_general(
            doc_low[...], block, (((1,), (1,)), ((), ())), preferred_element_type=F32
        )
        at = pl.ds(pl.multiple_of(k * WB, WB), WB)
        half = DOCS // 2
        top = live[0, k].astype(F32)
        low = live[1, k].astype(F32)
        mask = jnp.where(lax.broadcasted_iota(jnp.int32, (DOCS, WB), 0) < half, top, low)
        kept = counts[:, at].astype(F32) * mask
        wide = kept / normalizer
        ratio_t[k + c, :, doc_rows(own_docs)] = wide.T.astype(BF16)
        ratio[:, at] = wide.astype(BF16)
        wlen[...] += kept
        for dx in range(1, 4):
            ratio_out(k, dx).start()
        ratio_over(k).start()

    def relay_ratio(k):
        for dx in range(1, 4):
            ratio_arrived(2 * xo(dx) + c, k).wait()
            ratio_relay(k, dx).start()

    def half_rows(w):
        return slice(w * WB // 2, (w + 1) * WB // 2)

    def near_copy(m, side, w):
        n = m + 2 + 2 * lax.div(m, 2)
        return remote(
            part.at[n, side, half_rows(w), :],
            near.at[h, m, half_rows(w), :],
            send_n.at[m, side, w],
            recv_n.at[h, m, w],
            h_=side,
            a_=1 - a,
        )

    def far_copy(m, w):
        n = m + 2 * lax.div(m, 2)
        return remote(
            part.at[n, 1 - h, half_rows(w), :], far.at[m, half_rows(w), :], send_f.at[m, w], recv_f.at[m, w], h_=1 - h
        )

    def products(n):
        @pl.when(n == 0)
        def _():
            for dx, dc in others:
                q = 2 * xo(dx) + co(dc)
                pltpu.make_async_copy(docs.at[doc_rows(q), :], docs.at[doc_rows(q), :], recv_d.at[q]).wait()

        k = n - (1 - c)

        @pl.when(jnp.logical_and(k >= 0, k < SPAN))
        def _():
            for dx in range(4):
                ratio_arrived(2 * xo(dx) + (1 - c), k).wait()

        made = jnp.dot(ratio_t[n], docs[...], preferred_element_type=F32)
        part[n, 0] = made[:, :KH]
        part[n, 1] = made[:, KH:]
        m = n - 2 * lax.div(n, 4)

        @pl.when(lax.rem(lax.div(n, 2), 2) == 1)
        def _():
            for side in range(2):
                near_copy(m - 2, side, 0).start()

        @pl.when(lax.rem(lax.div(n, 2), 2) == 0)
        def _():
            far_copy(m, 0).start()

    def topic_z(dz):
        return remote(column, col_z.at[z], send_t.at[0, dz], recv_tz.at[z], z_=zo(dz))

    def own_results():
        length = jnp.sum(wlen[...], axis=1, keepdims=True)
        under = 1.0 / (length + K * alpha_prior)

        @pl.loop(0, K // 512)
        def _(n):
            at = pl.ds(pl.multiple_of(n * 512, 512), 512)
            proj = jnp.dot(
                ratio[...],
                words[pl.ds(pl.multiple_of(i * WB, WB), SPAN * WB), at],
                preferred_element_type=F32,
            )
            weight = mix[:, at].astype(F32) * scale[...] + alpha_prior
            new = weight * proj
            column[:, at] = jnp.sum(new, axis=0, keepdims=True)
            share_out[:, at] = (K * (new + alpha_prior) * under).astype(BF16)

        col_z[z] = column[...]
        for dz in range(1, 8):
            topic_z(dz).start()

    counts_load.wait()
    meet(i)
    docs[doc_rows(own_docs), :] = doc_low[:, topics(own_docs)]
    for dx, dc in others:
        doc_copy(dx, dc).start()

    def slot_at(e):
        return jnp.where(jnp.logical_and(e >= 4, e < 8), 4 + lax.rem(e + 2 * a, 4), e)

    @pl.loop(1, 19)
    def _(t):
        @pl.when(t <= 4)
        def _():
            r = turn(t - 1)
            arrived(4 + i, r).wait()
            column_copies(1, r, start)

        @pl.when(jnp.logical_and(t == 2, a == 0))
        def _():
            for u in range(CH):
                r = lax.rem(2 * h + CH - u, CH)
                arrived(i2, r).wait()
                relay(0, r).start()

        @pl.when(jnp.logical_and(jnp.logical_or(t == 7, t == 9), i <= 2))
        def _():
            r = 2 * h + lax.div(t - 7, 2)
            arrived(8 + i, r).wait()
            column_copies(2, r, start)

        @pl.when(jnp.logical_or(jnp.logical_and(t >= 2, t <= 4), t == 7))
        def _():
            r = lax.rem(2 * h + CH + 2 - jnp.minimum(t, 5), CH)
            arrived(4 + i2, r).wait()
            relay(1, r).start()

        @pl.when(jnp.logical_and(jnp.logical_or(t == 10, t == 12), a == 1))
        def _():
            for u in range(2):
                r = lax.div(t - 10, 2) + 2 * u
                arrived(8 + i2, r).wait()
                relay(2, r).start()

        @pl.when(jnp.logical_or(t <= 8, jnp.logical_and(t >= 12, t <= 14)))
        def _():
            slot = slot_at(jnp.where(t <= 8, t - 1, t - 4))
            column_of = lax.rem(slot, 4)

            @pl.when(jnp.logical_and(slot > i, slot < i + SPAN))
            def _():
                @pl.when(jnp.logical_and(column_of != i, column_of != i2))
                def _():
                    for r in range(CH):
                        arrived(slot, r).wait()

                meet(slot)

        for table in PRODUCTS:
            e = pick(t, table)
            ready = slot_at(e) - 2 * a

            @pl.when(jnp.logical_and(e >= 0, jnp.logical_and(ready >= 0, ready <= SPAN)))
            def _():
                products(ready)

        for table in RELAYS:
            e = pick(t, table)
            slot = slot_at(e)

            @pl.when(jnp.logical_and(e >= 0, jnp.logical_and(slot >= i, slot < i + SPAN)))
            def _():
                relay_ratio(slot - i)

        @pl.when(t == 14)
        def _():
            own_results()

    @pl.loop(0, 4)
    def _(m):
        for side in range(2):
            near_copy(3 - m, side, 1).start()

    @pl.loop(0, 5)
    def _(m):
        far_copy(4 - m, 1).start()

    def wait_far(m, w):
        at = far.at[m, half_rows(w), :]
        pltpu.make_async_copy(at, at, recv_f.at[m, w]).wait()

    def wait_near(m, w):
        for side in range(2):
            at = near.at[side, m, half_rows(w), :]
            pltpu.make_async_copy(at, at, recv_n.at[side, m, w]).wait()

    def part_rows(p):
        return slice(p * WB // PARTS, (p + 1) * WB // PARTS)

    def hop_copy(stage, q, p):
        source, target = ((4, hop1), (2, hop2))[stage]
        return remote(
            acc.at[source + q, part_rows(p), :],
            target.at[q, part_rows(p), :],
            send_z.at[stage, q, p],
            recv_z.at[stage, q, p],
            z_=zo(1),
        )

    def hop_arrived(stage, q, p):
        at = (hop1, hop2)[stage].at[q, part_rows(p), :]
        return pltpu.make_async_copy(at, at, recv_z.at[stage, q, p])

    def sums_over_y(w):
        rows = half_rows(w)
        parts = range(w * PARTS // 2, (w + 1) * PARTS // 2)
        for q in (0, 1):
            wait_far(q, w)
            acc[q, rows] = part[q, h, rows] + far[q, rows]

            @pl.when(a == 1)
            def _():
                wait_near(q, w)
                acc[q, rows] += near[0, q, rows] + near[1, q, rows]

        wait_far(4, w)
        acc[4, rows] = part[8, h, rows] + far[4, rows]

        @pl.when(a == 0)
        def _():
            for m in (2, 3):
                wait_near(m, w)
            acc[4, rows] += near[0, 2, rows] + near[1, 2, rows]
            acc[5, rows] = near[0, 3, rows] + near[1, 3, rows]
            for p in parts:
                hop_copy(0, 1, p).start()

        for p in parts:
            hop_copy(0, 0, p).start()
        for q in (2, 3):
            wait_far(q, w)
            m = q - 2 + 2 * a
            wait_near(m, w)
            acc[q, rows] = part[(4, 5)[q - 2], h, rows] + far[q, rows] + near[0, m, rows] + near[1, m, rows]

    def hop_on(p):
        rows = part_rows(p)
        hop_arrived(0, 0, p).wait()
        acc[2, rows] += hop1[0, rows]

        @pl.when(a == 0)
        def _():
            hop_arrived(0, 1, p).wait()
            acc[3, rows] += hop1[1, rows]

        for q in range(2):
            hop_copy(1, q, p).start()

    first, second = range(PARTS // 2), range(PARTS // 2, PARTS)
    sums_over_y(0)
    for p in first:
        hop_on(p)

    for dz in range(1, 8):
        q = zo(dz)
        pltpu.make_async_copy(col_z.at[q], col_z.at[q], recv_tz.at[q]).wait()
    column_z = col_z[0]
    for q in range(1, 8):
        column_z += col_z[q]
    col_x[x] = column_z

    def topic_x(dx):
        return remote(col_x.at[x], col_x.at[x], send_t.at[1, dx], recv_tx.at[x], x_=xo(dx))

    for dx in range(1, 4):
        topic_x(dx).start()

    def piece(q, h_):
        return pl.ds(pl.multiple_of(q * KD + h_ * KH, KH), KH)

    def gather_copy(p, dx, dh, dc):
        return remote(
            acc.at[co(dc), part_rows(p), :],
            gathered.at[part_rows(p), piece(own_docs, h)],
            send_g.at[p, dx, dh, dc],
            recv_g.at[p, own_docs, h],
            x_=xo(dx),
            h_=ho(dh),
            c_=co(dc),
        )

    def gather_arrived(p, q, h_):
        at = gathered.at[part_rows(p), piece(q, h_)]
        return pltpu.make_async_copy(at, at, recv_g.at[p, q, h_])

    def pass_y(p, dx, dc):
        q = 2 * xo(dx) + dc
        at = gathered.at[part_rows(p), piece(q, h)]
        return remote(at, at, send_p.at[p, dx - 1, dc], recv_g.at[p, q, h], h_=1 - h)

    def pass_x(p, dx, dc):
        q = 2 * x + dc
        at = gathered.at[part_rows(p), piece(q, 1 - h)]
        return remote(at, at, send_p.at[p, dx - 1, dc], recv_g.at[p, q, 1 - h], x_=xo(dx))

    fan = [(0, 1, 0), (0, 1, 1), (2, 0, 0), (2, 0, 1), (1, 0, 0), (1, 0, 1), (3, 0, 0), (3, 0, 1), (0, 0, 1)]

    def spread(p):
        rows = part_rows(p)
        for q in range(2):
            hop_arrived(1, q, p).wait()
            acc[q, rows] += hop2[q, rows]
        gathered[rows, piece(own_docs, h)] = acc[c, rows]
        for where in fan:
            gather_copy(p, *where).start()

    def pass_on(p):
        if p % 2 == 0:
            for dx in (1, 3, 2):
                for dc in range(2):
                    gather_arrived(p, 2 * xo(dx) + dc, h).wait()
                    pass_y(p, dx, dc).start()
        else:
            for dc in range(2):
                gather_arrived(p, 2 * x + dc, 1 - h).wait()
                for dx in (2, 1, 3):
                    pass_x(p, dx, dc).start()

    for p in first:
        spread(p)
    sums_over_y(1)
    pass_on(0)
    for p in second:
        hop_on(p)
    for p in first[1:]:
        pass_on(p)
    for p in second:
        spread(p)
    for p in second:
        pass_on(p)

    for dx in range(1, 4):
        q = xo(dx)
        pltpu.make_async_copy(col_x.at[q], col_x.at[q], recv_tx.at[q]).wait()
    column_x = col_x[0]
    for q in range(1, 4):
        column_x += col_x[q]
    me = h * 4 + i
    col_p[me] = column_x

    def topic_p(dh, da, dc):
        return remote(
            col_p.at[me],
            col_p.at[me],
            send_t.at[2, 4 * dh + 2 * da + dc],
            recv_tp.at[me],
            h_=ho(dh),
            a_=ao(da),
            c_=co(dc),
        )

    plane = [(dh, da, dc) for dh in range(2) for da in range(2) for dc in range(2) if dh + da + dc]
    for where in plane:
        topic_p(*where).start()

    for dh, da, dc in plane:
        q = 4 * ho(dh) + 2 * ao(da) + co(dc)
        pltpu.make_async_copy(col_p.at[q], col_p.at[q], recv_tp.at[q]).wait()
    column_p = col_p[0]
    for q in range(1, 8):
        column_p += col_p[q]
    mean[...] = column_p * (1.0 / (WB * 32))

    for p in range(PARTS):
        rows = part_rows(p)
        gather_arrived(p, 2 * x + 1 - c, h).wait()
        for dc in range(2):
            if p % 2 == 0:
                gather_arrived(p, 2 * x + dc, 1 - h).wait()
            for dx in range(1, 4):
                if p % 2 == 1:
                    gather_arrived(p, 2 * xo(dx) + dc, h).wait()
                gather_arrived(p, 2 * xo(dx) + dc, 1 - h).wait()
        topic_out[rows, :] = gathered[rows, :] * topic[rows, :]

    @pl.loop(0, CH)
    def _(r):
        column_copies(0, r, drain)
        column_copies(1, r, drain)

        @pl.when(jnp.logical_and(i <= 2, mine(r)))
        def _():
            column_copies(2, r, drain)

        @pl.when(a == 0)
        def _():
            drain(relay(0, r))

        drain(relay(1, r))

        @pl.when(a == 1)
        def _():
            drain(relay(2, r))

    for dx, dc in others:
        drain(doc_copy(dx, dc))

    @pl.loop(0, SPAN)
    def _(k):
        for dx in range(1, 4):
            drain(ratio_out(k, dx))
            drain(ratio_relay(k, dx))
        drain(ratio_over(k))

    @pl.loop(0, 4)
    def _(m):
        for side in range(2):
            for w in range(2):
                drain(near_copy(m, side, w))

    @pl.loop(0, 5)
    def _(m):
        for w in range(2):
            drain(far_copy(m, w))

    for p in range(PARTS):
        drain(hop_copy(0, 0, p))

        @pl.when(a == 0)
        def _():
            drain(hop_copy(0, 1, p))

        for q in range(2):
            drain(hop_copy(1, q, p))
        for where in fan:
            drain(gather_copy(p, *where))
        for dx in range(1, 4):
            for dc in range(2):
                drain((pass_x if p % 2 else pass_y)(p, dx, dc))
    for dz in range(1, 8):
        drain(topic_z(dz))
    for dx in range(1, 4):
        drain(topic_x(dx))
    for where in plane:
        drain(topic_p(*where))


def exchange(counts, tile_live, lengths, doc_mix, word_topic, topic_total):
    vmem = pl.BlockSpec(memory_space=pltpu.VMEM)
    hbm = pl.BlockSpec(memory_space=pltpu.HBM)
    smem = pl.BlockSpec(memory_space=pltpu.SMEM)
    dma = pltpu.SemaphoreType.DMA
    return pl.pallas_call(
        kernel,
        name="window",
        out_shape=(
            pltpu.VMEM((DOCS, K), BF16),
            pltpu.VMEM((WB, K), F32),
            jax.ShapeDtypeStruct((1, K), F32),
        ),
        in_specs=[hbm, smem, vmem, hbm, hbm, vmem],
        out_specs=(vmem, vmem, vmem),
        scratch_shapes=[
            pltpu.VMEM((DOCS, SPAN * WB), jnp.int32),
            pltpu.VMEM((DOCS, K), BF16),
            pltpu.VMEM((WB, K), F32),
            pltpu.VMEM((1, K), F32),
            pltpu.VMEM((DOCS, 1), F32),
            pltpu.VMEM((SLOTS * WB, K), BF16),
            pltpu.VMEM((DOCS, K), BF16),
            pltpu.VMEM((DOCS, 1), F32),
            pltpu.VMEM((8 * DOCS, KD), BF16),
            pltpu.VMEM((DOCS, SPAN * WB), BF16),
            pltpu.VMEM((SPAN + 1, WB, 8 * DOCS), BF16),
            pltpu.VMEM((SPAN + 1, 2, WB, KH), F32),
            pltpu.VMEM((2, 4, WB, KH), F32),
            pltpu.VMEM((5, WB, KH), F32),
            pltpu.VMEM((6, WB, KH), F32),
            pltpu.VMEM((2, WB, KH), F32),
            pltpu.VMEM((2, WB, KH), F32),
            pltpu.VMEM((WB, K), F32),
            pltpu.VMEM((DOCS, WB), F32),
            pltpu.VMEM((1, K), F32),
            pltpu.VMEM((8, 1, K), F32),
            pltpu.VMEM((4, 1, K), F32),
            pltpu.VMEM((8, 1, K), F32),
            dma((3, CH, 5)),
            dma((SLOTS, CH)),
            dma((4, 2)),
            dma((8,)),
            dma((SPAN, 4)),
            dma((SPAN, 3)),
            dma((8, SPAN)),
            dma((4, 2, 2)),
            dma((2, 4, 2)),
            dma((5, 2)),
            dma((5, 2)),
            dma((2, 2, PARTS)),
            dma((2, 2, PARTS)),
            dma((PARTS, 4, 2, 2)),
            dma((PARTS, 3, 2)),
            dma((PARTS, 8, 2)),
            dma((3, 8)),
            dma((8,)),
            dma((4,)),
            dma((8,)),
            dma((CH + 2,)),
        ],
        compiler_params=pltpu.CompilerParams(
            collective_id=0, has_side_effects=True, vmem_limit_bytes=62820000
        ),
    )(counts, tile_live, lengths, doc_mix, word_topic, topic_total)


def local(counts, tile_live, doc_lengths, doc_mix, word_topic, topic_total):
    doc_share, topic_new, topic_mean = exchange(
        counts, tile_live, doc_lengths[None, :], doc_mix, word_topic, topic_total[None, :]
    )
    return (doc_share, topic_new, topic_mean[0])


def solution(mesh):
    return jax.shard_map(
        local,
        mesh=mesh,
        in_specs=(
            P(("grp", "blk"), None),
            P(("grp", "blk"), None),
            P(("grp", "blk")),
            P(("grp", "blk"), None),
            P("blk", None),
            P(),
        ),
        out_specs=(P(("grp", "blk"), None), P("blk", None), P()),
        check_vma=False,
    )
```

```python
import jax
import jax.numpy as jnp
from jax import lax
from jax.experimental import pallas as pl
from jax.experimental.pallas import tpu as pltpu
from jax.sharding import PartitionSpec as P

VOCAB = 262144

alpha_prior = 0.1
beta_prior = 0.01

MESH = pl.DeviceIdType.MESH
F32 = jnp.float32
BF16 = jnp.bfloat16

DOCS = 256
WB = 128
K = 4096
SPAN = 8
SLOTS = 11
CH = 4
ROWS = WB // CH
KD = K // 8
KH = KD // 2
PARTS = 4


RELAYS = ({8: 0, 9: 2, 10: 4, 11: 6, 15: 8, 16: 9, 17: 10}, {8: 1, 9: 3, 10: 5, 11: 7})
PRODUCTS = ({9: 0, 10: 2, 11: 4, 13: 6, 16: 8, 17: 9, 18: 10}, {9: 1, 10: 3, 11: 5, 14: 7})


def pick(t, table):
    e = jnp.int32(-1)
    for step, place_ in table.items():
        e = jnp.where(t == step, place_, e)
    return e


def place(x, h, z, a, c):
    return {"grp": x * 2 + h, "blk": (z * 2 + a) * 2 + c}


def kernel(
    counts_in,
    live,
    lengths,
    mix_in,
    topic_in,
    total,
    share_out,
    topic_out,
    mean,
    counts,
    mix,
    topic,
    inverse,
    span,
    words,
    doc_low,
    scale,
    docs,
    ratio,
    ratio_t,
    part,
    near,
    far,
    acc,
    hop1,
    hop2,
    gathered,
    wlen,
    column,
    col_z,
    col_x,
    col_p,
    send_w,
    recv_w,
    send_d,
    recv_d,
    send_r,
    send_rf,
    recv_r,
    send_n,
    recv_n,
    send_f,
    recv_f,
    send_z,
    recv_z,
    send_g,
    send_p,
    recv_g,
    send_t,
    recv_tz,
    recv_tx,
    recv_tp,
    load,
):
    grp = lax.axis_index("grp")
    blk = lax.axis_index("blk")
    x = lax.div(grp, 2)
    h = lax.rem(grp, 2)
    z = lax.div(blk, 4)
    i = lax.rem(blk, 4)
    a = lax.div(i, 2)
    c = lax.rem(i, 2)
    i2 = 2 * (1 - a) + c

    def xo(dx):
        return lax.rem(x + dx, 4)

    def zo(dz):
        return lax.rem(z + dz + 8, 8)

    def ho(dh):
        return lax.rem(h + dh, 2)

    def ao(da):
        return lax.rem(a + da, 2)

    def co(dc):
        return lax.rem(c + dc, 2)

    def remote(src, dst, send, recv, x_=x, h_=h, z_=z, a_=a, c_=c):
        return pltpu.make_async_remote_copy(
            src_ref=src,
            dst_ref=dst,
            send_sem=send,
            recv_sem=recv,
            device_id=place(x_, h_, z_, a_, c_),
            device_id_type=MESH,
        )

    def topic_load(r):
        rows = pl.ds(pl.multiple_of(r * ROWS, ROWS), ROWS)
        return pltpu.make_async_copy(topic_in.at[rows, :], topic.at[rows, :], load.at[r])

    mix_load = pltpu.make_async_copy(mix_in, mix, load.at[CH])
    counts_load = pltpu.make_async_copy(counts_in, counts, load.at[CH + 1])
    for u in range(CH):
        topic_load(lax.rem(u + 2 * h, CH)).start()
    mix_load.start()
    counts_load.start()

    barrier = pltpu.get_barrier_semaphore()
    greeted = 0

    def greet(**where):
        at = dict(x=x, h=h, z=z, a=a, c=c)
        at.update(where)
        pl.semaphore_signal(barrier, inc=1, device_id=place(**at), device_id_type=MESH)

    for dz in range(1, 8):
        greet(z=zo(dz))
        greeted += 1
    for dh in range(2):
        for da in range(2):
            for dc in range(2):
                if dh + da + dc:
                    greet(h=ho(dh), a=ao(da), c=co(dc))
                    greeted += 1
    for dx in range(1, 4):
        for dh in range(2):
            for dc in range(2):
                greet(x=xo(dx), h=ho(dh), c=co(dc))
                greeted += 1

    def chunk(slot, r):
        return words.at[pl.ds(pl.multiple_of(slot * WB + r * ROWS, ROWS), ROWS), :]

    def to_z(j, r):
        slot = 4 * j + i
        return remote(chunk(slot, r), chunk(slot + 4, r), send_w.at[j, r, 0], recv_w.at[slot + 4, r], z_=zo(-1))

    def to_partner(j, r):
        slot = 4 * j + i
        return remote(chunk(slot, r), chunk(slot, r), send_w.at[j, r, 1], recv_w.at[slot, r], c_=1 - c)

    def to_y(j, r):
        slot = 4 * j + i
        return remote(
            chunk(slot, r), chunk(slot, r), send_w.at[j, r, 2], recv_w.at[slot, r], h_=lax.rem(r + h, 2), a_=1 - a
        )

    def to_other_y(r):
        slot = 8 + i
        return remote(
            chunk(slot, r), chunk(slot, r), send_w.at[2, r, 4], recv_w.at[slot, r], h_=lax.rem(r + h + 1, 2), a_=1 - a
        )

    def to_far(r):
        slot = 8 + i
        return remote(
            chunk(slot, r), chunk(slot, r), send_w.at[2, r, 0], recv_w.at[slot, r], h_=1 - h, c_=1 - c
        )

    def relay(j, r):
        slot = 4 * j + i2
        return remote(chunk(slot, r), chunk(slot, r), send_w.at[j, r, 3], recv_w.at[slot, r], c_=1 - c)

    def arrived(slot, r):
        return pltpu.make_async_copy(chunk(slot, r), chunk(slot, r), recv_w.at[slot, r])

    def mine(r):
        return lax.div(r, CH // 2) == h

    def column_copies(j, r, act):
        if j == 0:
            act(to_z(j, r))
        elif j == 1:
            @pl.when(jnp.logical_and(i <= 2, mine(r)))
            def _():
                act(to_z(j, r))
        else:
            @pl.when(c == 0)
            def _():
                act(to_far(r))

            @pl.when(a == 0)
            def _():
                act(to_other_y(r))
        if j == 1:
            act(to_partner(j, r))
            act(to_y(j, r))
        else:
            @pl.when(c == (1 if j == 0 else 0))
            def _():
                act(to_partner(j, r))

            @pl.when(a == (1 if j == 0 else 0))
            def _():
                act(to_y(j, r))

    start = lambda copy: copy.start()
    drain = lambda copy: copy.wait_send()

    inverse[...] = 1.0 / (total[...] + beta_prior * VOCAB)
    span[...] = jnp.broadcast_to(lengths[...].astype(F32), (8, DOCS)).T[:, :1]

    def turn(u):
        return lax.rem(u + 2 * h, CH)

    @pl.loop(0, CH)
    def _(u):
        r = turn(u)
        rows = pl.ds(pl.multiple_of(r * ROWS, ROWS), ROWS)
        own = pl.ds(pl.multiple_of(i * WB + r * ROWS, ROWS), ROWS)
        topic_load(r).wait()
        weight = (topic[rows, :] + beta_prior) * inverse[...]
        topic[rows, :] = weight
        words[own, :] = weight.astype(BF16)

        @pl.when(u == 0)
        def _():
            pl.semaphore_wait(barrier, greeted)

        @pl.when(u > 0)
        def _():
            column_copies(0, turn(u - 1), start)

    own_docs = 2 * x + c

    def doc_rows(q):
        return pl.ds(pl.multiple_of(q * DOCS, DOCS), DOCS)

    def topics(q):
        return pl.ds(pl.multiple_of(q * KD, KD), KD)

    def doc_copy(dx, dc, w):
        to = 2 * xo(dx) + co(dc)
        half = DOCS // 2
        return remote(
            doc_low.at[w * half : (w + 1) * half, topics(to)],
            docs.at[pl.ds(pl.multiple_of(own_docs * DOCS + w * half, half), half), :],
            send_d.at[dx, dc, w],
            recv_d.at[own_docs, w],
            x_=xo(dx),
            c_=co(dc),
        )

    others = [(dx, dc) for dx in (2, 1, 3, 0) for dc in range(2) if dx + dc]

    mix_load.wait()

    @pl.loop(0, DOCS // 32)
    def _(n):
        rows = pl.ds(pl.multiple_of(n * 32, 32), 32)
        wide = mix[rows, :].astype(F32)
        factor = span[rows, :] / jnp.sum(wide, axis=1, keepdims=True)
        scale[rows, :] = factor
        doc_low[rows, :] = (wide * factor + alpha_prior).astype(BF16)

        @pl.when(n == 0)
        def _():
            column_copies(0, turn(CH - 1), start)

        @pl.when(n == DOCS // 64)
        def _():
            for dx, dc in others:
                doc_copy(dx, dc, 0).start()

    wlen[...] = jnp.zeros_like(wlen)
    for q in range(4):
        ratio_t[SPAN, :, 2 * q * DOCS : (2 * q + 1) * DOCS] = jnp.zeros((WB, DOCS), BF16)
        ratio_t[0, :, (2 * q + 1) * DOCS : (2 * q + 2) * DOCS] = jnp.zeros((WB, DOCS), BF16)

    def ratio_at(q, k):
        return ratio_t.at[k + lax.rem(q, 2), :, doc_rows(q)]

    def ratio_out(k, dx):
        return remote(
            ratio_at(own_docs, k), ratio_at(own_docs, k), send_r.at[k, dx], recv_r.at[own_docs, k], x_=xo(dx)
        )

    def ratio_over(k):
        return remote(
            ratio_at(own_docs, k), ratio_at(own_docs, k), send_r.at[k, 0], recv_r.at[own_docs, k], c_=1 - c
        )

    def ratio_relay(k, dx):
        q = 2 * xo(dx) + c
        return remote(ratio_at(q, k), ratio_at(q, k), send_rf.at[k, dx - 1], recv_r.at[q, k], c_=1 - c)

    def ratio_arrived(q, k):
        return pltpu.make_async_copy(ratio_at(q, k), ratio_at(q, k), recv_r.at[q, k])

    def meet(slot):
        k = slot - i
        block = words[pl.ds(pl.multiple_of(slot * WB, WB), WB), :]
        normalizer = lax.dot_general(
            doc_low[...], block, (((1,), (1,)), ((), ())), preferred_element_type=F32
        )
        at = pl.ds(pl.multiple_of(k * WB, WB), WB)
        half = DOCS // 2
        top = live[0, k].astype(F32)
        low = live[1, k].astype(F32)
        mask = jnp.where(lax.broadcasted_iota(jnp.int32, (DOCS, WB), 0) < half, top, low)
        kept = counts[:, at].astype(F32) * mask
        wide = kept / normalizer
        ratio_t[k + c, :, doc_rows(own_docs)] = wide.T.astype(BF16)
        ratio[:, at] = wide.astype(BF16)
        wlen[...] += kept
        for dx in (2, 1, 3):
            ratio_out(k, dx).start()
        ratio_over(k).start()

    def relay_ratio(k):
        for dx in (1, 3, 2):
            ratio_arrived(2 * xo(dx) + c, k).wait()
            ratio_relay(k, dx).start()

    def half_rows(w):
        return slice(w * WB // 2, (w + 1) * WB // 2)

    def near_copy(m, side, w):
        n = m + 2 + 2 * lax.div(m, 2)
        return remote(
            part.at[n, side, half_rows(w), :],
            near.at[h, m, half_rows(w), :],
            send_n.at[m, side, w],
            recv_n.at[h, m, w],
            h_=side,
            a_=1 - a,
        )

    def far_copy(m, w):
        n = m + 2 * lax.div(m, 2)
        return remote(
            part.at[n, 1 - h, half_rows(w), :], far.at[m, half_rows(w), :], send_f.at[m, w], recv_f.at[m, w], h_=1 - h
        )

    def products(n):
        @pl.when(n == 0)
        def _():
            for dx, dc in others:
                q = 2 * xo(dx) + co(dc)
                for w in range(2):
                    at = docs.at[pl.ds(pl.multiple_of(q * DOCS + w * DOCS // 2, DOCS // 2), DOCS // 2), :]
                    pltpu.make_async_copy(at, at, recv_d.at[q, w]).wait()

        k = n - (1 - c)

        @pl.when(jnp.logical_and(k >= 0, k < SPAN))
        def _():
            for dx in range(4):
                ratio_arrived(2 * xo(dx) + (1 - c), k).wait()

        made = jnp.dot(ratio_t[n], docs[...], preferred_element_type=F32)
        part[n, 0] = made[:, :KH]
        part[n, 1] = made[:, KH:]
        m = n - 2 * lax.div(n, 4)

        @pl.when(lax.rem(lax.div(n, 2), 2) == 1)
        def _():
            for side in range(2):
                near_copy(m - 2, side, 0).start()

        @pl.when(lax.rem(lax.div(n, 2), 2) == 0)
        def _():
            far_copy(m, 0).start()

    def topic_z(dz):
        return remote(column, col_z.at[z], send_t.at[0, dz], recv_tz.at[z], z_=zo(dz))

    def own_results():
        length = jnp.sum(wlen[...], axis=1, keepdims=True)
        under = 1.0 / (length + K * alpha_prior)

        @pl.loop(0, K // 512)
        def _(n):
            at = pl.ds(pl.multiple_of(n * 512, 512), 512)
            proj = jnp.dot(
                ratio[...],
                words[pl.ds(pl.multiple_of(i * WB, WB), SPAN * WB), at],
                preferred_element_type=F32,
            )
            weight = mix[:, at].astype(F32) * scale[...] + alpha_prior
            new = weight * proj
            column[:, at] = jnp.sum(new, axis=0, keepdims=True)
            share_out[:, at] = (K * (new + alpha_prior) * under).astype(BF16)

        col_z[z] = column[...]
        for dz in range(1, 8):
            topic_z(dz).start()

    for dx, dc in others:
        doc_copy(dx, dc, 1).start()
    counts_load.wait()
    meet(i)
    docs[doc_rows(own_docs), :] = doc_low[:, topics(own_docs)]

    def slot_at(e):
        return jnp.where(jnp.logical_and(e >= 4, e < 8), 4 + lax.rem(e + 2 * a, 4), e)

    @pl.loop(1, 19)
    def _(t):
        @pl.when(t <= 4)
        def _():
            r = turn(t - 1)
            arrived(4 + i, r).wait()
            column_copies(1, r, start)

        @pl.when(jnp.logical_and(t == 2, a == 0))
        def _():
            for u in range(CH):
                r = lax.rem(2 * h + CH - u, CH)
                arrived(i2, r).wait()
                relay(0, r).start()

        @pl.when(jnp.logical_and(jnp.logical_or(t == 7, t == 9), i <= 2))
        def _():
            r = 2 * h + lax.div(t - 7, 2)
            arrived(8 + i, r).wait()
            column_copies(2, r, start)

        @pl.when(jnp.logical_or(jnp.logical_and(t >= 2, t <= 4), t == 7))
        def _():
            r = lax.rem(2 * h + CH + 2 - jnp.minimum(t, 5), CH)
            arrived(4 + i2, r).wait()
            relay(1, r).start()

        @pl.when(jnp.logical_and(jnp.logical_or(t == 10, t == 12), a == 1))
        def _():
            for u in range(2):
                r = lax.div(t - 10, 2) + 2 * u
                arrived(8 + i2, r).wait()
                relay(2, r).start()

        @pl.when(jnp.logical_or(t <= 8, jnp.logical_and(t >= 12, t <= 14)))
        def _():
            slot = slot_at(jnp.where(t <= 8, t - 1, t - 4))
            column_of = lax.rem(slot, 4)

            @pl.when(jnp.logical_and(slot > i, slot < i + SPAN))
            def _():
                @pl.when(jnp.logical_and(column_of != i, column_of != i2))
                def _():
                    for r in range(CH):
                        arrived(slot, r).wait()

                meet(slot)

        for table in PRODUCTS:
            e = pick(t, table)
            ready = slot_at(e) - 2 * a

            @pl.when(jnp.logical_and(e >= 0, jnp.logical_and(ready >= 0, ready <= SPAN)))
            def _():
                products(ready)

        for table in RELAYS:
            e = pick(t, table)
            slot = slot_at(e)

            @pl.when(jnp.logical_and(e >= 0, jnp.logical_and(slot >= i, slot < i + SPAN)))
            def _():
                relay_ratio(slot - i)

        @pl.when(t == 14)
        def _():
            own_results()

    @pl.loop(0, 4)
    def _(m):
        for side in range(2):
            near_copy(3 - m, side, 1).start()

    @pl.loop(0, 5)
    def _(m):
        far_copy(4 - m, 1).start()

    def wait_far(m, w):
        at = far.at[m, half_rows(w), :]
        pltpu.make_async_copy(at, at, recv_f.at[m, w]).wait()

    def wait_near(m, w):
        for side in range(2):
            at = near.at[side, m, half_rows(w), :]
            pltpu.make_async_copy(at, at, recv_n.at[side, m, w]).wait()

    def part_rows(p):
        return slice(p * WB // PARTS, (p + 1) * WB // PARTS)

    def hop_copy(stage, q, p):
        source, target = ((4, hop1), (2, hop2))[stage]
        return remote(
            acc.at[source + q, part_rows(p), :],
            target.at[q, part_rows(p), :],
            send_z.at[stage, q, p],
            recv_z.at[stage, q, p],
            z_=zo(1),
        )

    def hop_arrived(stage, q, p):
        at = (hop1, hop2)[stage].at[q, part_rows(p), :]
        return pltpu.make_async_copy(at, at, recv_z.at[stage, q, p])

    def sums_over_y(w):
        rows = half_rows(w)
        parts = range(w * PARTS // 2, (w + 1) * PARTS // 2)
        for q in (0, 1):
            wait_far(q, w)
            acc[q, rows] = part[q, h, rows] + far[q, rows]

            @pl.when(a == 1)
            def _():
                wait_near(q, w)
                acc[q, rows] += near[0, q, rows] + near[1, q, rows]

        wait_far(4, w)
        acc[4, rows] = part[8, h, rows] + far[4, rows]

        @pl.when(a == 0)
        def _():
            for m in (2, 3):
                wait_near(m, w)
            acc[4, rows] += near[0, 2, rows] + near[1, 2, rows]
            acc[5, rows] = near[0, 3, rows] + near[1, 3, rows]
            for p in parts:
                hop_copy(0, 1, p).start()

        for p in parts:
            hop_copy(0, 0, p).start()
        for q in (2, 3):
            wait_far(q, w)
            m = q - 2 + 2 * a
            wait_near(m, w)
            acc[q, rows] = part[(4, 5)[q - 2], h, rows] + far[q, rows] + near[0, m, rows] + near[1, m, rows]

    def hop_on(p):
        rows = part_rows(p)
        hop_arrived(0, 0, p).wait()
        acc[2, rows] += hop1[0, rows]

        @pl.when(a == 0)
        def _():
            hop_arrived(0, 1, p).wait()
            acc[3, rows] += hop1[1, rows]

        for q in range(2):
            hop_copy(1, q, p).start()

    first, second = range(PARTS // 2), range(PARTS // 2, PARTS)
    sums_over_y(0)
    for p in first:
        hop_on(p)

    for dz in range(1, 8):
        q = zo(dz)
        pltpu.make_async_copy(col_z.at[q], col_z.at[q], recv_tz.at[q]).wait()
    column_z = col_z[0]
    for q in range(1, 8):
        column_z += col_z[q]
    col_x[x] = column_z

    def topic_x(dx):
        return remote(col_x.at[x], col_x.at[x], send_t.at[1, dx], recv_tx.at[x], x_=xo(dx))

    for dx in range(1, 4):
        topic_x(dx).start()

    def piece(q, h_):
        return pl.ds(pl.multiple_of(q * KD + h_ * KH, KH), KH)

    def gather_copy(p, dx, dh, dc):
        return remote(
            acc.at[co(dc), part_rows(p), :],
            gathered.at[part_rows(p), piece(own_docs, h)],
            send_g.at[p, dx, dh, dc],
            recv_g.at[p, own_docs, h],
            x_=xo(dx),
            h_=ho(dh),
            c_=co(dc),
        )

    def gather_arrived(p, q, h_):
        at = gathered.at[part_rows(p), piece(q, h_)]
        return pltpu.make_async_copy(at, at, recv_g.at[p, q, h_])

    def pass_y(p, dx, dc):
        q = 2 * xo(dx) + dc
        at = gathered.at[part_rows(p), piece(q, h)]
        return remote(at, at, send_p.at[p, dx - 1, dc], recv_g.at[p, q, h], h_=1 - h)

    def pass_x(p, dx, dc):
        q = 2 * x + dc
        at = gathered.at[part_rows(p), piece(q, 1 - h)]
        return remote(at, at, send_p.at[p, dx - 1, dc], recv_g.at[p, q, 1 - h], x_=xo(dx))

    fan = [(0, 1, 0), (0, 1, 1), (2, 0, 0), (2, 0, 1), (1, 0, 0), (1, 0, 1), (3, 0, 0), (3, 0, 1), (0, 0, 1)]

    def spread(p):
        rows = part_rows(p)
        for q in range(2):
            hop_arrived(1, q, p).wait()
            acc[q, rows] += hop2[q, rows]
        gathered[rows, piece(own_docs, h)] = acc[c, rows]
        for where in fan:
            gather_copy(p, *where).start()

    def pass_on(p):
        if p % 2 == 0:
            for dx in (1, 3, 2):
                for dc in range(2):
                    gather_arrived(p, 2 * xo(dx) + dc, h).wait()
                    pass_y(p, dx, dc).start()
        else:
            for dc in range(2):
                gather_arrived(p, 2 * x + dc, 1 - h).wait()
                for dx in (2, 1, 3):
                    pass_x(p, dx, dc).start()

    for p in first:
        spread(p)
    sums_over_y(1)
    pass_on(0)
    for p in second:
        hop_on(p)
    for p in first[1:]:
        pass_on(p)
    for p in second:
        spread(p)
    for p in second:
        pass_on(p)

    for dx in range(1, 4):
        q = xo(dx)
        pltpu.make_async_copy(col_x.at[q], col_x.at[q], recv_tx.at[q]).wait()
    column_x = col_x[0]
    for q in range(1, 4):
        column_x += col_x[q]
    me = h * 4 + i
    col_p[me] = column_x

    def topic_p(dh, da, dc):
        return remote(
            col_p.at[me],
            col_p.at[me],
            send_t.at[2, 4 * dh + 2 * da + dc],
            recv_tp.at[me],
            h_=ho(dh),
            a_=ao(da),
            c_=co(dc),
        )

    plane = [(dh, da, dc) for dh in range(2) for da in range(2) for dc in range(2) if dh + da + dc]
    for where in plane:
        topic_p(*where).start()

    for dh, da, dc in plane:
        q = 4 * ho(dh) + 2 * ao(da) + co(dc)
        pltpu.make_async_copy(col_p.at[q], col_p.at[q], recv_tp.at[q]).wait()
    column_p = col_p[0]
    for q in range(1, 8):
        column_p += col_p[q]
    mean[...] = column_p * (1.0 / (WB * 32))

    for p in range(PARTS):
        rows = part_rows(p)
        gather_arrived(p, 2 * x + 1 - c, h).wait()
        for dc in range(2):
            if p % 2 == 0:
                gather_arrived(p, 2 * x + dc, 1 - h).wait()
            for dx in range(1, 4):
                if p % 2 == 1:
                    gather_arrived(p, 2 * xo(dx) + dc, h).wait()
                gather_arrived(p, 2 * xo(dx) + dc, 1 - h).wait()
        topic_out[rows, :] = gathered[rows, :] * topic[rows, :]

    @pl.loop(0, CH)
    def _(r):
        column_copies(0, r, drain)
        column_copies(1, r, drain)

        @pl.when(jnp.logical_and(i <= 2, mine(r)))
        def _():
            column_copies(2, r, drain)

        @pl.when(a == 0)
        def _():
            drain(relay(0, r))

        drain(relay(1, r))

        @pl.when(a == 1)
        def _():
            drain(relay(2, r))

    for dx, dc in others:
        for w in range(2):
            drain(doc_copy(dx, dc, w))

    @pl.loop(0, SPAN)
    def _(k):
        for dx in range(1, 4):
            drain(ratio_out(k, dx))
            drain(ratio_relay(k, dx))
        drain(ratio_over(k))

    @pl.loop(0, 4)
    def _(m):
        for side in range(2):
            for w in range(2):
                drain(near_copy(m, side, w))

    @pl.loop(0, 5)
    def _(m):
        for w in range(2):
            drain(far_copy(m, w))

    for p in range(PARTS):
        drain(hop_copy(0, 0, p))

        @pl.when(a == 0)
        def _():
            drain(hop_copy(0, 1, p))

        for q in range(2):
            drain(hop_copy(1, q, p))
        for where in fan:
            drain(gather_copy(p, *where))
        for dx in range(1, 4):
            for dc in range(2):
                drain((pass_x if p % 2 else pass_y)(p, dx, dc))
    for dz in range(1, 8):
        drain(topic_z(dz))
    for dx in range(1, 4):
        drain(topic_x(dx))
    for where in plane:
        drain(topic_p(*where))


def exchange(counts, tile_live, lengths, doc_mix, word_topic, topic_total):
    vmem = pl.BlockSpec(memory_space=pltpu.VMEM)
    hbm = pl.BlockSpec(memory_space=pltpu.HBM)
    smem = pl.BlockSpec(memory_space=pltpu.SMEM)
    dma = pltpu.SemaphoreType.DMA
    return pl.pallas_call(
        kernel,
        name="window",
        out_shape=(
            pltpu.VMEM((DOCS, K), BF16),
            pltpu.VMEM((WB, K), F32),
            jax.ShapeDtypeStruct((1, K), F32),
        ),
        in_specs=[hbm, smem, vmem, hbm, hbm, vmem],
        out_specs=(vmem, vmem, vmem),
        scratch_shapes=[
            pltpu.VMEM((DOCS, SPAN * WB), jnp.int32),
            pltpu.VMEM((DOCS, K), BF16),
            pltpu.VMEM((WB, K), F32),
            pltpu.VMEM((1, K), F32),
            pltpu.VMEM((DOCS, 1), F32),
            pltpu.VMEM((SLOTS * WB, K), BF16),
            pltpu.VMEM((DOCS, K), BF16),
            pltpu.VMEM((DOCS, 1), F32),
            pltpu.VMEM((8 * DOCS, KD), BF16),
            pltpu.VMEM((DOCS, SPAN * WB), BF16),
            pltpu.VMEM((SPAN + 1, WB, 8 * DOCS), BF16),
            pltpu.VMEM((SPAN + 1, 2, WB, KH), F32),
            pltpu.VMEM((2, 4, WB, KH), F32),
            pltpu.VMEM((5, WB, KH), F32),
            pltpu.VMEM((6, WB, KH), F32),
            pltpu.VMEM((2, WB, KH), F32),
            pltpu.VMEM((2, WB, KH), F32),
            pltpu.VMEM((WB, K), F32),
            pltpu.VMEM((DOCS, WB), F32),
            pltpu.VMEM((1, K), F32),
            pltpu.VMEM((8, 1, K), F32),
            pltpu.VMEM((4, 1, K), F32),
            pltpu.VMEM((8, 1, K), F32),
            dma((3, CH, 5)),
            dma((SLOTS, CH)),
            dma((4, 2, 2)),
            dma((8, 2)),
            dma((SPAN, 4)),
            dma((SPAN, 3)),
            dma((8, SPAN)),
            dma((4, 2, 2)),
            dma((2, 4, 2)),
            dma((5, 2)),
            dma((5, 2)),
            dma((2, 2, PARTS)),
            dma((2, 2, PARTS)),
            dma((PARTS, 4, 2, 2)),
            dma((PARTS, 3, 2)),
            dma((PARTS, 8, 2)),
            dma((3, 8)),
            dma((8,)),
            dma((4,)),
            dma((8,)),
            dma((CH + 2,)),
        ],
        compiler_params=pltpu.CompilerParams(
            collective_id=0, has_side_effects=True, vmem_limit_bytes=62820000
        ),
    )(counts, tile_live, lengths, doc_mix, word_topic, topic_total)


def local(counts, tile_live, doc_lengths, doc_mix, word_topic, topic_total):
    doc_share, topic_new, topic_mean = exchange(
        counts, tile_live, doc_lengths[None, :], doc_mix, word_topic, topic_total[None, :]
    )
    return (doc_share, topic_new, topic_mean[0])


def solution(mesh):
    return jax.shard_map(
        local,
        mesh=mesh,
        in_specs=(
            P(("grp", "blk"), None),
            P(("grp", "blk"), None),
            P(("grp", "blk")),
            P(("grp", "blk"), None),
            P("blk", None),
            P(),
        ),
        out_specs=(P(("grp", "blk"), None), P("blk", None), P()),
        check_vma=False,
    )
```
